256 devices in a mesh: px: 32 (over y, x, z_hi), py: 8 (over z_lo, core).
Axes of the slice: x: 4, y: 4, z: 8 (z_hi: 2, z_lo: 4; z = z_hi * 4 + z_lo), core: 2. Of those that a mesh axis runs over, the one named last changes fastest.
Arguments:
- levels: int32 [512, 8192], P('px', 'py'), may hold values from 0 to 15
- conv_table: bfloat16 [64, 144], replicated, may hold values from -2 to 2
- conv_bias: float32 [64], replicated, may hold values from -3 to 3
- mix_weight: bfloat16 [64, 64], replicated, may hold values from -0.75 to 0.75
- mix_bias: float32 [64], replicated, may hold values from -3 to 3
- decoder: bfloat16 [5, 40, 64], replicated, may hold values from -0.15625 to 0.15625
- green_rows: float32 [8, 2, 64, 512], P(None, None, None, 'px'), may hold values from -0.25 to 0.25
- green_cols: float32 [8, 2, 64, 8192], P(None, None, None, 'py'), may hold values from -0.0625 to 0.0625
- focal_order: int32 [64], replicated, may hold values from 0 to 63, each once
Outputs:
- focal: float32 [8, 64, 512], P('py', 'px')
The draws below stay inside these ranges and needn't reach their ends.
Inputs may be any that keep to these rules, and one draw needn't show every extreme that they name: `focal_order`: each of the 64 focal rows appears exactly once.
All inputs are finite; a program needn't handle non-finite values.
Results may differ from the reference program's by a relative error of at most 0.0045.
Values sent between devices are 32-bit elements; how exact they have to be, the bound alone decides.
No kernel may reach another device: no remote copies, remote signals or barrier semaphores. Data moves between devices by JAX's collectives and lax.ppermute only.
A program may use at most 128 MiB of HBM per device.

```python
import jax
import jax.numpy as jnp
from jax import lax

R_DEV = 16
HID = 64
LEVELS = 16
CH = 8
M = 2
KS = 5
Z = 8
U = 64
V = 64
NXA = 512
NYA = 8192
N_PX = 32


def set_ends(array, rng, least, top_value):
    index_at = [jax.random.randint(jax.random.fold_in(rng, axis), (), 0, length) for axis, length in enumerate(array.shape)]
    widest = array.shape.index(max(array.shape))
    neighbour = index_at[:widest] + [(index_at[widest] + 1) % array.shape[widest]] + index_at[widest + 1:]
    return array.at[tuple(index_at)].set(least).at[tuple(neighbour)].set(top_value)


def shard_levels(stream_key, dims, cuts, least, largest):
    def one(dim, blocks):
        steps = jax.random.uniform(jax.random.fold_in(jax.random.fold_in(stream_key, 6), dim), (blocks,), jnp.float32, least / len(cuts), largest / len(cuts))
        return jnp.repeat(jnp.exp(steps), dims[dim] // blocks).reshape((-1,) + (1,) * (len(dims) - dim - 1))

    factor_of = one(*cuts[0])
    for cut in cuts[1:]:
        factor_of = factor_of * one(*cut)
    return factor_of


def noise(rng, shape, deviation, bound, split=(), kind=jnp.bfloat16):
    factor_of = shard_levels(rng, shape, split, -0.22, 0.18) if split else 1.0
    entries = jax.random.normal(rng, shape, jnp.float32) * deviation * factor_of
    return jnp.minimum(jnp.maximum(entries, -bound), bound).astype(kind)


def setup_inputs(seed: int = 0) -> dict:
    arg_keys = jax.random.split(jax.random.key(seed), 10)
    levels = set_ends(jax.random.randint(arg_keys[0], (NXA, NYA), 0, LEVELS), jax.random.fold_in(arg_keys[0], 1), 0, LEVELS - 1).astype(jnp.int32)
    conv_table = noise(arg_keys[1], (HID, 9 * LEVELS), 9 ** -0.5, 2.0)
    conv_bias = noise(arg_keys[2], (HID,), 0.5, 3.0, (), jnp.float32)
    mix_weight = noise(arg_keys[3], (HID, HID), HID ** -0.5, 0.75)
    mix_bias = noise(arg_keys[4], (HID,), 0.5, 3.0, (), jnp.float32)
    decoder = noise(arg_keys[5], (KS, KS * CH, HID), (KS * KS * HID) ** -0.5, 0.15625)
    green_rows = noise(arg_keys[6], (Z, 2, U, NXA), NXA ** -0.5, 0.25, ((3, 32),), jnp.float32)
    green_cols = noise(arg_keys[7], (Z, 2, V, NYA), NYA ** -0.5, 0.0625, ((3, 8),), jnp.float32)
    focal_order = jax.random.permutation(arg_keys[8], U).astype(jnp.int32)
    return dict(levels=levels, conv_table=conv_table, conv_bias=conv_bias, mix_weight=mix_weight, mix_bias=mix_bias, decoder=decoder, green_rows=green_rows, green_cols=green_cols, focal_order=focal_order)


exact_prec = lax.Precision.HIGHEST


def level_features(levels_ext, valid_ext, rows_out, cols_out, conv_table, conv_bias, mix_weight, mix_bias):
    count_levels = conv_table.shape[1] // 9
    level_ids = jnp.arange(count_levels, dtype=jnp.int32)[:, None, None]
    stacks = []
    for row_tap in range(3):
        for col_tap in range(3):
            window = levels_ext[row_tap:row_tap + rows_out, col_tap:col_tap + cols_out]
            inside = valid_ext[row_tap:row_tap + rows_out, col_tap:col_tap + cols_out]
            match_map = (window[None] == level_ids).astype(jnp.float32) * inside[None]
            stacks.append(match_map.astype(jnp.bfloat16))
    onehot = jnp.concatenate(stacks, axis=0).reshape(9 * count_levels, rows_out * cols_out)
    pre_act = jnp.dot(conv_table, onehot, preferred_element_type=jnp.float32) + conv_bias[:, None]
    hidden = jax.nn.gelu(pre_act).astype(jnp.bfloat16)
    mix_act = jnp.dot(mix_weight, hidden, preferred_element_type=jnp.float32) + mix_bias[:, None]
    center = valid_ext[1:1 + rows_out, 1:1 + cols_out].reshape(1, rows_out * cols_out)
    return (jax.nn.gelu(mix_act) * center).astype(jnp.bfloat16)


def focal_plane(product):
    real_part = product[0, 0] - product[1, 1]
    imag_part = product[0, 1] + product[1, 0]
    joined = jnp.stack([real_part, imag_part], axis=1)
    return joined.reshape(joined.shape[0], -1)


def reference(levels, conv_table, conv_bias, mix_weight, mix_bias, decoder, green_rows, green_cols, focal_order):
    total_cols = levels.shape[1]
    border = M + 1
    half = CH // 2
    levels_pad = jnp.pad(levels, border)
    valid_pad = jnp.pad(jnp.ones(levels.shape, jnp.float32), border)
    ordered = jnp.take(green_rows, focal_order, axis=2)
    blocks = ordered.reshape(Z, 2, U, N_PX, R_DEV).transpose(3, 0, 1, 2, 4)
    rows_out = R_DEV + 2 * M
    cols_out = total_cols + 2 * M

    def scan_step(running, inputs):
        block_id, gblock = inputs
        first_row = (block_id * R_DEV).astype(jnp.int32)
        levels_blk = lax.dynamic_slice_in_dim(levels_pad, first_row, R_DEV + 2 * border, 0)
        valid_blk = lax.dynamic_slice_in_dim(valid_pad, first_row, R_DEV + 2 * border, 0)
        features = level_features(levels_blk, valid_blk, rows_out, cols_out, conv_table, conv_bias, mix_weight, mix_bias)
        near_field = jnp.zeros((CH, R_DEV, total_cols), jnp.float32)
        for row_tap in range(KS):
            tap_block = jnp.dot(decoder[row_tap], features, preferred_element_type=jnp.float32).reshape(KS, CH, rows_out, cols_out)
            for col_tap in range(KS):
                near_field = near_field + tap_block[col_tap, :, 2 * M - row_tap:2 * M - row_tap + R_DEV, 2 * M - col_tap:2 * M - col_tap + total_cols]
        partial_value = jnp.einsum('zkur,hrc->zkuhc', gblock, near_field, precision=exact_prec)
        real_part = partial_value[:, 0, :, :half] - partial_value[:, 1, :, half:]
        imag_part = partial_value[:, 0, :, half:] + partial_value[:, 1, :, :half]
        return running + jnp.stack([real_part, imag_part], axis=1), None

    initial = jnp.zeros((Z, 2, U, half, total_cols), jnp.float32)
    aperture_sum, _ = lax.scan(scan_step, initial, (jnp.arange(N_PX, dtype=jnp.int32), blocks))
    planes = []
    for plane_id in range(Z):
        product = jnp.einsum('jvc,iupc->jiupv', green_cols[plane_id], aperture_sum[plane_id], precision=exact_prec)
        planes.append(focal_plane(product))
    return jnp.stack(planes, axis=0)
```

```python
import jax
import jax.numpy as jnp
from jax import lax
from jax.experimental import pallas as pl
from jax.experimental.pallas import tpu as pltpu
from jax.sharding import PartitionSpec as P

HIGH = lax.Precision.HIGHEST
F32 = jnp.float32
BF16 = jnp.bfloat16
NT = (((1,), (1,)), ((), ()))
TN = (((0,), (0,)), ((), ()))

ROWS = 16
COLS = 1024
HID = 64
LEVELS = 16
CH = 8
KS = 5
Z = 8
U = 64
V = 64
HALO = 4
ROWS_EXT = ROWS + HALO
SLOT = 64
BLOCK = 4
REL_ORDER = (0, 2, 4, 6, 1, 3, 5, 7)

GELU_A = 0.7978845608028654
GELU_B = GELU_A * 0.044715


def iota(shape, dim):
    return lax.broadcasted_iota(jnp.int32, shape, dim)


def twice_gelu(x):
    return x + x * jnp.tanh(x * (GELU_A + GELU_B * (x * x)))


def split3(x):
    a = lax.reduce_precision(x, 8, 7)
    b = lax.reduce_precision(x - a, 8, 7)
    return a.astype(BF16), b.astype(BF16), (x - a - b).astype(BF16)


def pack_kernel(idx_ref, lev_ref, rows_ref, cols_ref, to_x_ref, to_y_ref, to_d_ref):
    lev = lev_ref[...].astype(F32)
    to_x_ref[:, :COLS] = lev[8:, :]
    pick = (iota((8, ROWS), 1) == iota((8, ROWS), 0) + (ROWS - 8)).astype(F32)
    rows = rows_ref[...].reshape(2 * U, ROWS)
    to_x_ref[:, COLS:] = lax.dot_general(
        pick, rows, NT, precision=HIGH, preferred_element_type=F32
    )
    to_d_ref[...] = lev[8:, COLS - 128 :]
    to_y_ref[:ROWS, :] = lev[:, COLS - 128 :]
    pick = (iota((8, 128), 1) == iota((8, 128), 0) + (128 - HALO)).astype(F32)
    cols = cols_ref[...].reshape(Z * 2 * V, 128)
    edge = lax.dot_general(pick, cols, NT, precision=HIGH, preferred_element_type=F32)
    for z in range(Z):
        to_y_ref[ROWS + HALO * z : ROWS + HALO * (z + 1), :] = edge[
            :HALO, 128 * z : 128 * (z + 1)
        ]


def pack(idx, levels, green_rows, green_cols):
    return pl.pallas_call(
        pack_kernel,
        grid_spec=pltpu.PrefetchScalarGridSpec(
            num_scalar_prefetch=1,
            grid=(1,),
            in_specs=[
                pl.BlockSpec((ROWS, COLS), lambda i, s: (0, 0)),
                pl.BlockSpec((1, 2, U, ROWS), lambda i, s: (s[1], 0, 0, 0)),
                pl.BlockSpec((Z, 2, V, 128), lambda i, s: (0, 0, 0, COLS // 128 - 1)),
            ],
            out_specs=[
                pl.BlockSpec((8, COLS + 128), lambda i, s: (0, 0)),
                pl.BlockSpec((ROWS + Z * HALO, 128), lambda i, s: (0, 0)),
                pl.BlockSpec((8, 128), lambda i, s: (0, 0)),
            ],
        ),
        out_shape=[
            jax.ShapeDtypeStruct((8, COLS + 128), F32),
            jax.ShapeDtypeStruct((ROWS + Z * HALO, 128), F32),
            jax.ShapeDtypeStruct((8, 128), F32),
        ],
        name="pack",
    )(idx, levels, green_rows, green_cols)


def split_kernel(idx_ref, cols_ref, hi_ref, lo_ref):
    x = cols_ref[...].reshape(2 * V, COLS)
    hi = x.astype(BF16)
    hi_ref[0] = hi
    lo_ref[0] = (x - hi.astype(F32)).astype(BF16)


def split_cols(idx, green_cols):
    def plane(g, s):
        rel = jnp.where(g < 4, 2 * g, 2 * g - 7)
        return (s[1] ^ rel, 0, 0, 0)

    return pl.pallas_call(
        split_kernel,
        grid_spec=pltpu.PrefetchScalarGridSpec(
            num_scalar_prefetch=1,
            grid=(Z,),
            in_specs=[pl.BlockSpec((1, 2, V, COLS), plane)],
            out_specs=[pl.BlockSpec((1, 2 * V, COLS), lambda g, s: (g, 0, 0))] * 2,
        ),
        out_shape=[jax.ShapeDtypeStruct((Z, 2 * V, COLS), BF16)] * 2,
        name="split_cols",
    )(idx, green_cols)


def field_kernel(
    idx_ref, lev_ref, from_x_ref, from_y_ref, from_d_ref, conv_ref, mix_ref, dec_ref,
    hi_ref, lo_ref, keep_ref, send_ref,
    ext_ref, hot_ref, hid_ref, feat_ref, nf_ref, edge_ref,
):
    first_y = idx_ref[1] == 0
    main = jnp.concatenate([from_x_ref[:, :COLS], lev_ref[...].astype(F32)], axis=0)
    left = jnp.concatenate([from_d_ref[...], from_y_ref[:ROWS, :]], axis=0)
    ext = jnp.concatenate([left, main], axis=1)
    lane = iota((24, COLS), 1)
    for b in range(3):
        window = pltpu.roll(ext, 3 - b, 1)[:, 128:]
        if b != 1:
            cut = first_y & (lane == (2 if b == 0 else 1))
            window = jnp.where(cut, -1.0, window)
        ext_ref[b] = window
    level_ids = iota((LEVELS, COLS), 0).astype(F32)
    ones = jnp.ones((LEVELS, COLS), BF16)

    def make_hot(q, _):
        for b in range(3):
            row = jnp.broadcast_to(ext_ref[b, pl.ds(q + 5, 1), :], (LEVELS, COLS))
            hot_ref[pl.ds(q * SLOT + b * LEVELS, LEVELS), :] = jnp.where(
                row == level_ids, 1.0, 0.0
            ).astype(BF16)
        hot_ref[pl.ds(q * SLOT + 3 * LEVELS, LEVELS), :] = ones
        return 0

    lax.fori_loop(0, ROWS + 2, make_hot, 0)
    hid_ref[2 * HID :, :] = ones
    feat_ref[: BLOCK * HID, :] = jnp.zeros((BLOCK * HID, COLS), BF16)
    feat_ref[(BLOCK + ROWS) * HID :, :] = jnp.zeros((BLOCK * HID, COLS), BF16)

    def features(i, _):
        pre = jnp.dot(
            conv_ref[jnp.minimum(i, 2)],
            hot_ref[pl.ds(i * 2 * SLOT, 4 * SLOT), :],
            preferred_element_type=F32,
        )
        hid_ref[: 2 * HID, :] = twice_gelu(pre).astype(BF16)
        mixed = jnp.dot(mix_ref[...], hid_ref[...], preferred_element_type=F32)
        feat_ref[pl.ds((BLOCK + 2 * i) * HID, 2 * HID), :] = twice_gelu(mixed).astype(BF16)
        return 0

    lax.fori_loop(0, ROWS // 2, features, 0)

    lane = iota((1, COLS), 1)
    near = iota((1, 128), 1)
    keep_main, keep_edge = [], []
    for s in range(KS):
        k = KS - 1 - s
        ok = lane < COLS - k
        ok = ok & ((lane + k >= 2) | jnp.logical_not(first_y))
        keep_main.append(ok.astype(F32))
        ok = (near >= s) & (near < HALO)
        ok = ok & ((near - s < 2) | jnp.logical_not(first_y))
        keep_edge.append(ok.astype(F32))
    half = BLOCK * CH // 2

    def near_field(i, _):
        taps = jnp.dot(
            dec_ref[jnp.minimum(i, 2)],
            feat_ref[pl.ds(i * BLOCK * HID, 2 * BLOCK * HID), :],
            preferred_element_type=F32,
        )
        acc = jnp.zeros((2 * half, COLS), F32)
        edge = jnp.zeros((2 * half, 128), F32)
        for s in range(KS):
            part = taps[2 * half * s : 2 * half * (s + 1), :]
            k = KS - 1 - s
            moved = part if k == 0 else pltpu.roll(part, COLS - k, 1)
            acc = acc + moved * keep_main[s]
            part = part[:, :128]
            moved = part if s == 0 else pltpu.roll(part, s, 1)
            edge = edge + moved * keep_edge[s]
        hi = acc.astype(BF16)
        lo = (acc - hi.astype(F32)).astype(BF16)
        for k in range(2):
            at = k * ROWS_EXT * 4 + i * half
            nf_ref[pl.ds(at, half), :] = hi[k * half : (k + 1) * half]
            nf_ref[pl.ds(at + ROWS_EXT * CH, half), :] = lo[k * half : (k + 1) * half]
            edge_ref[pl.ds(at, half), :] = edge[k * half : (k + 1) * half]
        return 0

    lax.fori_loop(0, ROWS_EXT // BLOCK, near_field, 0)

    n = ROWS_EXT * CH
    m = n // 2
    lane = iota((1, 128), 1)
    sign = jnp.where(lane < V, -1.0, 1.0)

    for g in range(Z):
        hi = hi_ref[g]
        out = lax.dot_general(nf_ref[...], hi, NT, preferred_element_type=F32)
        out = out[:n] + out[n:]
        out = out + lax.dot_general(nf_ref[:n, :], lo_ref[g], NT, preferred_element_type=F32)
        rel = REL_ORDER[g]
        z = idx_ref[1] ^ rel
        green = from_y_ref[pl.ds(ROWS + HALO * z, HALO), :]
        green = jnp.concatenate([green, jnp.zeros((4, 128), F32)], axis=0)
        out = out + jnp.dot(
            edge_ref[:, :8], green, precision=HIGH, preferred_element_type=F32
        )
        total = out[:m] + sign * pltpu.roll(out[m:], V, 1)
        if g < 4:
            keep_ref[g] = total
        else:
            send_ref[g - 4] = total


def field(idx, levels, from_x, from_y, from_d, conv_w, mix_w, dec_w, hi, lo):
    m = ROWS_EXT * CH // 2
    return pl.pallas_call(
        field_kernel,
        in_specs=[pl.BlockSpec(memory_space=pltpu.SMEM)]
        + [pl.BlockSpec(memory_space=pltpu.VMEM)] * 9,
        out_specs=[pl.BlockSpec(memory_space=pltpu.VMEM)] * 2,
        out_shape=[jax.ShapeDtypeStruct((4, m, 128), F32)] * 2,
        scratch_shapes=[
            pltpu.VMEM((3, 24, COLS), F32),
            pltpu.VMEM(((ROWS + 2) * SLOT, COLS), BF16),
            pltpu.VMEM((2 * HID + LEVELS, COLS), BF16),
            pltpu.VMEM(((ROWS + 2 * BLOCK) * HID, COLS), BF16),
            pltpu.VMEM((2 * ROWS_EXT * CH, COLS), BF16),
            pltpu.VMEM((ROWS_EXT * CH, 128), F32),
        ],
        compiler_params=pltpu.CompilerParams(vmem_limit_bytes=40 << 20),
        name="field",
    )(idx, levels, from_x, from_y, from_d, conv_w, mix_w, dec_w, hi, lo)


def rows_kernel(idx_ref, order_ref, rows_ref, from_x_ref, out_ref):
    n = ROWS_EXT * 4
    own = rows_ref[...].reshape(2 * U, ROWS)
    spread = (iota((ROWS, n), 1) // 4 == iota((ROWS, n), 0) + HALO).astype(F32)
    wide = jnp.dot(own, spread, precision=HIGH, preferred_element_type=F32)
    spread = (iota((8, n), 1) // 4 == iota((8, n), 0) - (8 - HALO)).astype(F32)
    wide = wide + lax.dot_general(
        from_x_ref[:, COLS:], spread, TN, precision=HIGH, preferred_element_type=F32
    )
    pick = (order_ref[...] == iota((U, U * 4), 0)).astype(F32)
    mask = (iota((U * 4, n), 0) % 4 == iota((U * 4, n), 1) % 4).astype(F32)
    for j in range(2):
        out_ref[j] = mask * lax.dot_general(
            pick, wide[j * U : (j + 1) * U], TN, precision=HIGH, preferred_element_type=F32
        )


def row_factors(idx, order, green_rows, from_x):
    n = ROWS_EXT * 4
    return pl.pallas_call(
        rows_kernel,
        grid_spec=pltpu.PrefetchScalarGridSpec(
            num_scalar_prefetch=1,
            grid=(1,),
            in_specs=[
                pl.BlockSpec((1, U * 4), lambda i, s: (0, 0)),
                pl.BlockSpec((1, 2, U, ROWS), lambda i, s: (s[1], 0, 0, 0)),
                pl.BlockSpec((8, COLS + 128), lambda i, s: (0, 0)),
            ],
            out_specs=pl.BlockSpec((2, U * 4, n), lambda i, s: (0, 0, 0)),
        ),
        out_shape=jax.ShapeDtypeStruct((2, U * 4, n), F32),
        name="row_factors",
    )(idx, order, green_rows, from_x)


def focal_kernel(rows_ref, a_ref, b_ref, c_ref, d_ref, out_ref):
    t = (a_ref[...] + b_ref[...]) + (c_ref[...] + d_ref[...])
    re = jnp.dot(rows_ref[0], t, precision=HIGH, preferred_element_type=F32)
    im = jnp.dot(rows_ref[1], t, precision=HIGH, preferred_element_type=F32)
    sign = jnp.where(iota((1, 128), 1) < V, -1.0, 1.0)
    out_ref[...] = (re + sign * pltpu.roll(im, V, 1)).reshape(out_ref.shape)


def focal_share(rows, a, b, c, d):
    return pl.pallas_call(
        focal_kernel,
        in_specs=[pl.BlockSpec(memory_space=pltpu.VMEM)] * 5,
        out_specs=pl.BlockSpec(memory_space=pltpu.VMEM),
        out_shape=jax.ShapeDtypeStruct((U // 2, 8, 128), F32),
        name="focal_share",
    )(rows, a, b, c, d)


def total_kernel(x_ref, out_ref):
    s = jnp.sum(x_ref[...], axis=0)
    for u in range(2):
        for k in range(2):
            for p in range(4):
                at = (k * 4 + p) * V
                out_ref[0, u : u + 1, at : at + V] = s[u * 4 + p : u * 4 + p + 1, k * V : (k + 1) * V]


def total(parts):
    return pl.pallas_call(
        total_kernel,
        in_specs=[pl.BlockSpec(memory_space=pltpu.VMEM)],
        out_specs=pl.BlockSpec(memory_space=pltpu.VMEM),
        out_shape=jax.ShapeDtypeStruct((1, 2, 8 * V), F32),
        name="total",
    )(parts)


def conv_weights(conv_table, conv_bias, first_x):
    table = conv_table.reshape(HID, 3, 3 * LEVELS)
    bias = jnp.stack(split3(conv_bias), axis=1)
    bias = jnp.pad(bias, ((0, 0), (0, LEVELS - 3)))[:, None, :]
    bias = jnp.pad(bias, ((0, 0), (1, 1), (0, 0)))
    slots = jnp.concatenate([table, bias], axis=2).reshape(HID, 3 * SLOT)
    both = jnp.concatenate(
        [jnp.pad(slots, ((0, 0), (0, SLOT))), jnp.pad(slots, ((0, 0), (SLOT, 0)))], axis=0
    )
    col = jnp.arange(4 * SLOT)
    hot = col % SLOT < 3 * LEVELS
    last = first_x & hot & (col // SLOT == 3)
    head = first_x & hot & (col // SLOT == 0)
    zero = jnp.zeros((), BF16)
    return jnp.stack([jnp.where(last, zero, both), jnp.where(head, zero, both), both])


def mix_weights(mix_weight, mix_bias):
    w = mix_weight * jnp.asarray(0.5, BF16)
    bias = jnp.stack(split3(mix_bias), axis=1)
    top = jnp.concatenate([w, jnp.zeros_like(w)], axis=1)
    low = jnp.concatenate([jnp.zeros_like(w), w], axis=1)
    tail = jnp.pad(bias, ((0, 0), (0, LEVELS - 3)))
    return jnp.concatenate(
        [jnp.concatenate([top, low], axis=0), jnp.concatenate([tail, tail], axis=0)], axis=1
    )


def decoder_weights(decoder, first_x):
    d = decoder * jnp.asarray(0.5, BF16)
    d = d[::-1].reshape(KS, KS, 2, 4, HID).transpose(1, 2, 3, 0, 4)
    rows = [
        jnp.pad(d, ((0, 0), (0, 0), (0, 0), (r, BLOCK - 1 - r), (0, 0))) for r in range(BLOCK)
    ]
    w = jnp.stack(rows, axis=2).reshape(KS * CH * BLOCK, 2 * BLOCK * HID)
    at = jnp.arange(2 * BLOCK * HID) // HID
    zero = jnp.zeros((), BF16)
    return jnp.stack(
        [jnp.where(first_x & (at >= 6), zero, w), jnp.where(first_x & (at < 2), zero, w), w]
    )


def on_device(
    levels, conv_table, conv_bias, mix_weight, mix_bias, decoder, green_rows, green_cols, focal_order
):
    count_px = lax.axis_size("px")
    count_py = lax.axis_size("py")
    ix = lax.axis_index("px")
    iy = lax.axis_index("py")
    idx = jnp.stack([ix, iy]).astype(jnp.int32)
    to_x, to_y, to_d = pack(idx, levels, green_rows, green_cols)
    next_x = [(i, (i + 1) % count_px) for i in range(count_px)]
    next_y = [(i, (i + 1) % count_py) for i in range(count_py)]
    next_d = [
        (i * count_py + j, ((i + 1) % count_px) * count_py + (j + 1) % count_py)
        for i in range(count_px)
        for j in range(count_py)
    ]
    from_x = lax.ppermute(to_x, "px", next_x)
    from_d = lax.ppermute(to_d, ("px", "py"), next_d)
    from_y = lax.ppermute(to_y, "py", next_y)
    hi, lo = split_cols(idx, green_cols)
    first_x = ix == 0
    conv_w = conv_weights(conv_table, conv_bias, first_x)
    mix_w = mix_weights(mix_weight, mix_bias)
    dec_w = decoder_weights(decoder, first_x)
    order = jnp.broadcast_to(focal_order[:, None], (U, 4)).reshape(1, U * 4)
    keep, send = field(idx, levels, from_x, from_y, from_d, conv_w, mix_w, dec_w, hi, lo)
    rows = row_factors(idx, order, green_rows, from_x)

    def swap(x, mask):
        return lax.ppermute(x, "py", [(i, i ^ mask) for i in range(count_py)])

    part = keep + swap(send, 1)
    b, c, d = (swap(part[i], 2 * i) for i in (1, 2, 3))
    share = focal_share(rows, part[0], b, c, d)
    return total(lax.all_to_all(share, "px", 0, 0))


def solution(mesh):
    return jax.shard_map(
        on_device,
        mesh=mesh,
        in_specs=(
            P("px", "py"),
            P(),
            P(),
            P(),
            P(),
            P(),
            P(None, None, None, "px"),
            P(None, None, None, "py"),
            P(),
        ),
        out_specs=P("py", "px", None),
        check_vma=False,
    )
```

```python
import jax
import jax.numpy as jnp
from jax import lax
from jax.experimental import pallas as pl
from jax.experimental.pallas import tpu as pltpu
from jax.sharding import PartitionSpec as P

HIGH = lax.Precision.HIGHEST
F32 = jnp.float32
BF16 = jnp.bfloat16
NT = (((1,), (1,)), ((), ()))
TN = (((0,), (0,)), ((), ()))

ROWS = 16
COLS = 1024
HID = 64
LEVELS = 16
CH = 8
KS = 5
Z = 8
U = 64
V = 64
HALO = 4
ROWS_EXT = ROWS + HALO
SLOT = 64
BLOCK = 4
REL_ORDER = (0, 2, 4, 6, 1, 3, 5, 7)
PART = ROWS_EXT * CH // 2
VMEM = pl.BlockSpec(memory_space=pltpu.VMEM)
HBM = pl.BlockSpec(memory_space=pltpu.HBM)


def params(mib):
    return pltpu.CompilerParams(vmem_limit_bytes=mib << 20)

GELU_A = 0.7978845608028654
GELU_B = GELU_A * 0.044715


def iota(shape, dim):
    return lax.broadcasted_iota(jnp.int32, shape, dim)


def twice_gelu(x):
    return x + x * jnp.tanh(x * (GELU_A + GELU_B * (x * x)))


def split3(x):
    a = lax.reduce_precision(x, 8, 7)
    b = lax.reduce_precision(x - a, 8, 7)
    return a.astype(BF16), b.astype(BF16), (x - a - b).astype(BF16)


def pack_kernel(lev_hbm, rows_hbm, cols_hbm, to_x_ref, to_y_ref, to_d_ref, lev_ref, tile_ref, rows_ref, cols_ref, sems):
    z = lax.axis_index("py")
    last = pl.ds(COLS - 128, 128)
    copies = [
        pltpu.make_async_copy(cols_hbm.at[:, :, :, last], cols_ref, sems.at[0]),
        pltpu.make_async_copy(lev_hbm.at[pl.ds(8, 8), :], lev_ref, sems.at[1]),
        pltpu.make_async_copy(lev_hbm.at[:, last], tile_ref, sems.at[2]),
        pltpu.make_async_copy(rows_hbm.at[z], rows_ref, sems.at[3]),
    ]
    for copy in copies:
        copy.start()
    for copy in copies[1:]:
        copy.wait()
    to_x_ref[:, :COLS] = lev_ref[...].astype(F32)
    to_x_ref[:, COLS:] = jnp.concatenate([rows_ref[0, 8:, :], rows_ref[1, 8:, :]], axis=1)
    tile = tile_ref[...].astype(F32)
    to_d_ref[...] = tile[8:, :]
    to_y_ref[:ROWS, :] = tile
    copies[0].wait()
    for i in range(Z):
        edge = cols_ref[i].reshape(2 * V, 128).T
        to_y_ref[ROWS + HALO * i : ROWS + HALO * (i + 1), :] = edge[128 - HALO :, :]


def pack(levels, rows_t, green_cols):
    return pl.pallas_call(
        pack_kernel,
        in_specs=[HBM] * 3,
        out_specs=[VMEM] * 3,
        out_shape=[
            jax.ShapeDtypeStruct((8, COLS + 128), F32),
            jax.ShapeDtypeStruct((ROWS + Z * HALO, 128), F32),
            jax.ShapeDtypeStruct((8, 128), F32),
        ],
        scratch_shapes=[
            pltpu.VMEM((8, COLS), jnp.int32),
            pltpu.VMEM((ROWS, 128), jnp.int32),
            pltpu.VMEM((2, ROWS, U), F32),
            pltpu.VMEM((Z, 2, V, 128), F32),
            pltpu.SemaphoreType.DMA((4,)),
        ],
        compiler_params=params(4),
        name="pack",
    )(*(pltpu.with_memory_space_constraint(x, pltpu.HBM) for x in (levels, rows_t, green_cols)))


def one_hot(row, level_ids):
    row = jnp.broadcast_to(row, level_ids.shape)
    return jnp.where(row == level_ids, 1.0, 0.0).astype(BF16)


def inner_kernel(lev_ref, conv_ref, mix_ref, cols_hbm, feat_ref, hi_ref, lo_ref, ext_ref, hot_ref, hid_ref, cols_ref, sems):
    z = lax.axis_index("py")
    copies = [
        pltpu.make_async_copy(cols_hbm.at[z ^ REL_ORDER[g]], cols_ref.at[g], sems.at[g])
        for g in range(Z)
    ]
    for copy in copies:
        copy.start()
    wide = COLS - 128
    lev = lev_ref[...].astype(F32)
    for b in range(3):
        ext_ref[b] = pltpu.roll(lev, 3 - b, 1)[:, 128:]
    level_ids = iota((LEVELS, wide), 0).astype(F32)
    ones = jnp.ones((LEVELS, wide), BF16)

    def make_hot(q, _):
        for b in range(3):
            hot_ref[pl.ds(q * SLOT + b * LEVELS, LEVELS), :] = one_hot(
                ext_ref[b, pl.ds(q + 1, 1), :], level_ids
            )
        hot_ref[pl.ds(q * SLOT + 3 * LEVELS, LEVELS), :] = ones
        return 0

    lax.fori_loop(0, ROWS - 2, make_hot, 0)
    hid_ref[2 * HID :, :] = ones
    feat_ref[: BLOCK * HID, :] = jnp.zeros((BLOCK * HID, COLS), BF16)
    feat_ref[(BLOCK + ROWS) * HID :, :] = jnp.zeros((BLOCK * HID, COLS), BF16)

    def features(i, _):
        pre = jnp.dot(
            conv_ref[2], hot_ref[pl.ds(i * 2 * SLOT, 4 * SLOT), :], preferred_element_type=F32
        )
        hid_ref[: 2 * HID, :] = twice_gelu(pre).astype(BF16)
        mixed = jnp.dot(mix_ref[...], hid_ref[...], preferred_element_type=F32)
        feat_ref[pl.ds((2 * BLOCK + 2 * i) * HID, 2 * HID), 128:] = twice_gelu(mixed).astype(BF16)
        return 0

    lax.fori_loop(0, ROWS // 2 - 2, features, 0)
    for copy in copies:
        copy.wait()

    def split(g, _):
        x = cols_ref[g].reshape(2 * V, COLS)
        hi = x.astype(BF16)
        hi_ref[g] = hi
        lo_ref[g] = (x - hi.astype(F32)).astype(BF16)
        return 0

    lax.fori_loop(0, Z, split, 0)


def inner(levels, conv_w, mix_w, green_cols):
    wide = COLS - 128
    return pl.pallas_call(
        inner_kernel,
        in_specs=[VMEM] * 3 + [HBM],
        out_specs=[VMEM] * 3,
        out_shape=[
            jax.ShapeDtypeStruct(((ROWS + 2 * BLOCK) * HID, COLS), BF16),
            jax.ShapeDtypeStruct((Z, 2 * V, COLS), BF16),
            jax.ShapeDtypeStruct((Z, 2 * V, COLS), BF16),
        ],
        scratch_shapes=[
            pltpu.VMEM((3, ROWS, wide), F32),
            pltpu.VMEM(((ROWS - 2) * SLOT, wide), BF16),
            pltpu.VMEM((2 * HID + LEVELS, wide), BF16),
            pltpu.VMEM((Z, 2, V, COLS), F32),
            pltpu.SemaphoreType.DMA((Z,)),
        ],
        compiler_params=params(24),
        name="inner",
    )(levels, conv_w, mix_w, pltpu.with_memory_space_constraint(green_cols, pltpu.HBM))


def split2(x):
    hi = x.astype(BF16)
    return hi, (x - hi.astype(F32)).astype(BF16)


def make_row_factors(from_x_ref, rows_ref, order_ref, out_ref):
    green = jnp.concatenate([rows_ref[0], rows_ref[1]], axis=1)
    green = jnp.concatenate([from_x_ref[:, COLS:], green], axis=0)
    n = ROWS + 8
    pick = (order_ref[...] == iota((U, U * 4), 0)).astype(BF16)
    spread = (iota((PART, n), 0) // 4 == iota((PART, n), 1) - (8 - HALO)).astype(BF16)
    mask = iota((PART, U * 4), 0) % 4 == iota((PART, U * 4), 1) % 4
    for i, part in enumerate(split2(green)):
        for j in range(2):
            ordered = jnp.dot(part[:, j * U : (j + 1) * U], pick, preferred_element_type=F32)
            wide = jnp.dot(spread, ordered.astype(BF16), preferred_element_type=F32)
            wide = jnp.where(mask, wide, 0.0)
            out_ref[i, j * U * 4 : (j + 1) * U * 4, :] = wide.T.astype(BF16)


def field_kernel(
    lev_ref, from_x_ref, from_y_ref, from_d_ref, conv_ref, mix_ref, dec_ref, rows_hbm, order_ref,
    hi_ref, lo_ref, _, keep_ref, send_ref, factor_ref, feat_ref,
    ext_ref, hot_ref, hid_ref, nf_ref, edge_ref, rows_ref, sem,
):
    iy = lax.axis_index("py")
    copy = pltpu.make_async_copy(rows_hbm.at[iy], rows_ref, sem)
    copy.start()
    first_y = iy == 0
    main = jnp.concatenate([from_x_ref[:, :COLS], lev_ref[...].astype(F32)], axis=0)
    left = jnp.concatenate([from_d_ref[...], from_y_ref[:ROWS, :]], axis=0)
    ext = jnp.concatenate([left, main], axis=1)
    lane = iota((24, COLS), 1)
    for b in range(3):
        window = pltpu.roll(ext, 3 - b, 1)[:, 128:]
        if b != 1:
            cut = first_y & (lane == (2 if b == 0 else 1))
            window = jnp.where(cut, -1.0, window)
        ext_ref[b] = window
    level_ids = iota((LEVELS, COLS), 0).astype(F32)
    ones = jnp.ones((LEVELS, COLS), BF16)
    for o in range(4):
        for b in range(3):
            at = pl.ds(o * SLOT + b * LEVELS, LEVELS)
            for w in range(2):
                q = 2 * w + o
                hot_ref[w, at, :] = one_hot(ext_ref[b, q + 5 : q + 6, :], level_ids)
            for t in range(6):
                q = 2 * t + 4 + o
                hot_ref[2, at, t * 128 : (t + 1) * 128] = one_hot(
                    ext_ref[b, q + 5 : q + 6, :128], level_ids[:, :128]
                )
            hot_ref[2, at, 768:] = jnp.zeros((LEVELS, COLS - 768), BF16)
        for w in range(3):
            hot_ref[w, pl.ds(o * SLOT + 3 * LEVELS, LEVELS), :] = ones
    hid_ref[2 * HID :, :] = ones

    def features(w):
        pre = jnp.dot(conv_ref[w], hot_ref[w], preferred_element_type=F32)
        hid_ref[: 2 * HID, :] = twice_gelu(pre).astype(BF16)
        mixed = jnp.dot(mix_ref[...], hid_ref[...], preferred_element_type=F32)
        return twice_gelu(mixed).astype(BF16)

    def whole_rows(w, _):
        feat_ref[pl.ds((BLOCK + 2 * w) * HID, 2 * HID), :] = features(w)
        return 0

    lax.fori_loop(0, 2, whole_rows, 0)
    tiles = features(2)
    for t in range(6):
        at = (2 * BLOCK + 2 * t) * HID
        feat_ref[at : at + 2 * HID, :128] = tiles[:, t * 128 : (t + 1) * 128]

    lane = iota((1, COLS), 1)
    near = iota((1, 128), 1)
    keep_main, keep_edge = [], []
    for s in range(KS):
        k = KS - 1 - s
        ok = lane < COLS - k
        ok = ok & ((lane + k >= 2) | jnp.logical_not(first_y))
        keep_main.append(ok.astype(F32))
        ok = (near >= s) & (near < HALO)
        ok = ok & ((near - s < 2) | jnp.logical_not(first_y))
        keep_edge.append(ok.astype(F32))
    half = BLOCK * CH // 2

    def near_field(i, _):
        taps = jnp.dot(
            dec_ref[jnp.minimum(i, 2)],
            feat_ref[pl.ds(i * BLOCK * HID, 2 * BLOCK * HID), :],
            preferred_element_type=F32,
        )
        acc = jnp.zeros((2 * half, COLS), F32)
        edge = jnp.zeros((2 * half, 128), F32)
        for s in range(KS):
            part = taps[2 * half * s : 2 * half * (s + 1), :]
            k = KS - 1 - s
            moved = part if k == 0 else pltpu.roll(part, COLS - k, 1)
            acc = acc + moved * keep_main[s]
            part = part[:, :128]
            moved = part if s == 0 else pltpu.roll(part, s, 1)
            edge = edge + moved * keep_edge[s]
        hi, lo = split2(acc)
        for k in range(2):
            at = k * PART + i * half
            nf_ref[pl.ds(at, half), :] = hi[k * half : (k + 1) * half]
            nf_ref[pl.ds(at + 2 * PART, half), :] = lo[k * half : (k + 1) * half]
            edge_ref[pl.ds(at, half), :] = edge[k * half : (k + 1) * half]
        return 0

    lax.fori_loop(0, ROWS_EXT // BLOCK, near_field, 0)

    n = 2 * PART
    sign = jnp.where(iota((1, 128), 1) < V, -1.0, 1.0)
    for g in range(Z):
        out = lax.dot_general(nf_ref[...], hi_ref[g], NT, preferred_element_type=F32)
        out = out[:n] + out[n:]
        out = out + lax.dot_general(nf_ref[:n, :], lo_ref[g], NT, preferred_element_type=F32)
        green = from_y_ref[pl.ds(ROWS + HALO * (iy ^ REL_ORDER[g]), HALO), :]
        green = jnp.concatenate([green, jnp.zeros((4, 128), F32)], axis=0)
        out = out + jnp.dot(
            edge_ref[:, :8], green, precision=HIGH, preferred_element_type=F32
        )
        total = out[:PART] + sign * pltpu.roll(out[PART:], V, 1)
        if g < 4:
            keep_ref[g] = total
        else:
            send_ref[g - 4] = total
    copy.wait()
    make_row_factors(from_x_ref, rows_ref, order_ref, factor_ref)


def field(levels, from_x, from_y, from_d, conv_w, mix_w, dec_w, rows, order, hi, lo, feat):
    return pl.pallas_call(
        field_kernel,
        in_specs=[VMEM] * 7 + [HBM] + [VMEM] * 4,
        out_specs=[VMEM] * 4,
        out_shape=[
            jax.ShapeDtypeStruct((4, PART, 128), F32),
            jax.ShapeDtypeStruct((4, PART, 128), F32),
            jax.ShapeDtypeStruct((2, 2 * U * 4, PART), BF16),
            jax.ShapeDtypeStruct(feat.shape, BF16),
        ],
        input_output_aliases={11: 3},
        scratch_shapes=[
            pltpu.VMEM((3, 24, COLS), F32),
            pltpu.VMEM((3, 4 * SLOT, COLS), BF16),
            pltpu.VMEM((2 * HID + LEVELS, COLS), BF16),
            pltpu.VMEM((4 * PART, COLS), BF16),
            pltpu.VMEM((2 * PART, 128), F32),
            pltpu.VMEM((2, ROWS, U), F32),
            pltpu.SemaphoreType.DMA,
        ],
        compiler_params=params(24),
        name="field",
    )(
        levels, from_x, from_y, from_d, conv_w, mix_w, dec_w,
        pltpu.with_memory_space_constraint(rows, pltpu.HBM), order, hi, lo, feat,
    )


def focal_kernel(factor_ref, keep_ref, got_ref, b_ref, c_ref, d_ref, out_ref):
    t = ((keep_ref[0] + got_ref[0]) + b_ref[...]) + (c_ref[...] + d_ref[...])
    hi, lo = split2(t)
    out = jnp.dot(factor_ref[0], hi, preferred_element_type=F32)
    out = out + jnp.dot(factor_ref[1], hi, preferred_element_type=F32)
    out = out + jnp.dot(factor_ref[0], lo, preferred_element_type=F32)
    n = U * 4
    sign = jnp.where(iota((1, 128), 1) < V, -1.0, 1.0)
    out_ref[...] = (out[:n] + sign * pltpu.roll(out[n:], V, 1)).reshape(out_ref.shape)


def focal_share(factors, keep, got, b, c, d):
    return pl.pallas_call(
        focal_kernel,
        in_specs=[VMEM] * 6,
        out_specs=VMEM,
        out_shape=jax.ShapeDtypeStruct((U // 2, 8, 128), F32),
        compiler_params=params(4),
        name="focal_share",
    )(factors, keep, got, b, c, d)


def total_kernel(x_ref, out_ref):
    s = jnp.sum(x_ref[...], axis=0)
    for u in range(2):
        for k in range(2):
            for p in range(4):
                at = (k * 4 + p) * V
                row = u * 4 + p
                out_ref[0, u : u + 1, at : at + V] = s[row : row + 1, k * V : (k + 1) * V]


def total(parts):
    return pl.pallas_call(
        total_kernel,
        in_specs=[VMEM],
        out_specs=VMEM,
        out_shape=jax.ShapeDtypeStruct((1, 2, 8 * V), F32),
        compiler_params=params(4),
        name="total",
    )(parts)


def conv_weights(conv_table, conv_bias, first_x):
    table = conv_table.reshape(HID, 3, 3 * LEVELS)
    bias = jnp.stack(split3(conv_bias), axis=1)
    bias = jnp.pad(bias, ((0, 0), (0, LEVELS - 3)))[:, None, :]
    bias = jnp.pad(bias, ((0, 0), (1, 1), (0, 0)))
    slots = jnp.concatenate([table, bias], axis=2).reshape(HID, 3 * SLOT)
    both = jnp.concatenate(
        [jnp.pad(slots, ((0, 0), (0, SLOT))), jnp.pad(slots, ((0, 0), (SLOT, 0)))], axis=0
    )
    col = jnp.arange(4 * SLOT)
    hot = col % SLOT < 3 * LEVELS
    last = first_x & hot & (col // SLOT == 3)
    head = first_x & hot & (col // SLOT == 0)
    zero = jnp.zeros((), BF16)
    return jnp.stack([jnp.where(last, zero, both), jnp.where(head, zero, both), both])


def mix_weights(mix_weight, mix_bias):
    w = mix_weight * jnp.asarray(0.5, BF16)
    bias = jnp.stack(split3(mix_bias), axis=1)
    top = jnp.concatenate([w, jnp.zeros_like(w)], axis=1)
    low = jnp.concatenate([jnp.zeros_like(w), w], axis=1)
    tail = jnp.pad(bias, ((0, 0), (0, LEVELS - 3)))
    return jnp.concatenate(
        [jnp.concatenate([top, low], axis=0), jnp.concatenate([tail, tail], axis=0)], axis=1
    )


def decoder_weights(decoder, first_x):
    d = decoder * jnp.asarray(0.5, BF16)
    d = d[::-1].reshape(KS, KS, 2, 4, HID).transpose(1, 2, 3, 0, 4)
    rows = [
        jnp.pad(d, ((0, 0), (0, 0), (0, 0), (r, BLOCK - 1 - r), (0, 0))) for r in range(BLOCK)
    ]
    w = jnp.stack(rows, axis=2).reshape(KS * CH * BLOCK, 2 * BLOCK * HID)
    at = jnp.arange(2 * BLOCK * HID) // HID
    zero = jnp.zeros((), BF16)
    return jnp.stack(
        [jnp.where(first_x & (at >= 6), zero, w), jnp.where(first_x & (at < 2), zero, w), w]
    )


def on_device(
    levels, conv_table, conv_bias, mix_weight, mix_bias, decoder, green_rows, green_cols, focal_order
):
    count_px = lax.axis_size("px")
    count_py = lax.axis_size("py")
    rows_t = jnp.swapaxes(green_rows, 2, 3)
    to_x, to_y, to_d = pack(levels, rows_t, green_cols)
    next_x = [(i, (i + 1) % count_px) for i in range(count_px)]
    next_y = [(i, (i + 1) % count_py) for i in range(count_py)]
    next_d = [
        (i * count_py + j, ((i + 1) % count_px) * count_py + (j + 1) % count_py)
        for i in range(count_px)
        for j in range(count_py)
    ]
    from_x = lax.ppermute(to_x, "px", next_x)
    from_d = lax.ppermute(to_d, ("px", "py"), next_d)
    from_y = lax.ppermute(to_y, "py", next_y)
    first_x = lax.axis_index("px") == 0
    conv_w = conv_weights(conv_table, conv_bias, first_x)
    mix_w = mix_weights(mix_weight, mix_bias)
    dec_w = decoder_weights(decoder, first_x)
    order = jnp.broadcast_to(focal_order[:, None], (U, 4)).reshape(1, U * 4)
    feat, hi, lo = inner(levels, conv_w, mix_w, green_cols)
    keep, send, factors, _ = field(
        levels, from_x, from_y, from_d, conv_w, mix_w, dec_w, rows_t, order, hi, lo, feat
    )

    def swap(x, mask):
        return lax.ppermute(x, "py", [(i, i ^ mask) for i in range(count_py)])

    got = swap(send, 1)
    b, c, d = (swap(keep[i] + got[i], 2 * i) for i in (1, 2, 3))
    share = focal_share(factors, keep, got, b, c, d)
    return total(lax.all_to_all(share, "px", 0, 0))


def solution(mesh):
    return jax.shard_map(
        on_device,
        mesh=mesh,
        in_specs=(
            P("px", "py"),
            P(),
            P(),
            P(),
            P(),
            P(),
            P(None, None, None, "px"),
            P(None, None, None, "py"),
            P(),
        ),
        out_specs=P("py", "px", None),
        check_vma=False,
    )
```

```python
import jax
import jax.numpy as jnp
from jax import lax
from jax.experimental import pallas as pl
from jax.experimental.pallas import tpu as pltpu
from jax.sharding import PartitionSpec as P

HIGH = lax.Precision.HIGHEST
F32 = jnp.float32
BF16 = jnp.bfloat16
NT = (((1,), (1,)), ((), ()))
TN = (((0,), (0,)), ((), ()))

ROWS = 16
COLS = 1024
HID = 64
LEVELS = 16
CH = 8
KS = 5
Z = 8
U = 64
V = 64
HALO = 4
ROWS_EXT = ROWS + HALO
SLOT = 3 * LEVELS
WINDOW = 4 * SLOT
BLOCK = 4
REL_ORDER = (0, 2, 4, 6, 1, 3, 5, 7)
PART = ROWS_EXT * CH // 2
HALF = BLOCK * CH // 2
VMEM = pl.BlockSpec(memory_space=pltpu.VMEM)
HBM = pl.BlockSpec(memory_space=pltpu.HBM)


def params(mib):
    return pltpu.CompilerParams(vmem_limit_bytes=mib << 20)

GELU_A = 0.7978845608028654
GELU_B = GELU_A * 0.044715


def iota(shape, dim):
    return lax.broadcasted_iota(jnp.int32, shape, dim)


def twice_gelu(x):
    return x + x * jnp.tanh(x * (GELU_A + GELU_B * (x * x)))


def split2(x):
    hi = x.astype(BF16)
    return hi, (x - hi.astype(F32)).astype(BF16)


def hbm(x):
    return pltpu.with_memory_space_constraint(x, pltpu.HBM)


def pack_y_kernel(lev_hbm, cols_hbm, out_ref, tile_ref, cols_ref, sems):
    last = pl.ds(COLS - 128, 128)
    copies = [
        pltpu.make_async_copy(cols_hbm.at[:, :, :, last], cols_ref, sems.at[0]),
        pltpu.make_async_copy(lev_hbm.at[:, last], tile_ref, sems.at[1]),
    ]
    for copy in copies:
        copy.start()
    copies[1].wait()
    out_ref[:ROWS, :] = tile_ref[...].astype(F32)
    copies[0].wait()
    for i in range(Z):
        edge = cols_ref[i].reshape(2 * V, 128).T
        out_ref[ROWS + HALO * i : ROWS + HALO * (i + 1), :] = edge[128 - HALO :, :]


def pack_y(levels, green_cols):
    return pl.pallas_call(
        pack_y_kernel,
        in_specs=[HBM] * 2,
        out_specs=VMEM,
        out_shape=jax.ShapeDtypeStruct((ROWS + Z * HALO, 128), F32),
        scratch_shapes=[
            pltpu.VMEM((ROWS, 128), jnp.int32),
            pltpu.VMEM((Z, 2, V, 128), F32),
            pltpu.SemaphoreType.DMA((2,)),
        ],
        compiler_params=params(4),
        name="pack_y",
    )(hbm(levels), hbm(green_cols))


def pack_x_kernel(lev_ref, rows_ref, from_y_ref, out_ref):
    z = lax.axis_index("py")
    out_ref[:, :128] = from_y_ref[8:ROWS, :]
    out_ref[:, 128 : 128 + COLS] = lev_ref[8:, :].astype(F32)
    out_ref[:, 128 + COLS :] = jnp.concatenate(
        [rows_ref[z, 0, 8:, :], rows_ref[z, 1, 8:, :]], axis=1
    )


def pack_x(levels, rows_t, from_y):
    return pl.pallas_call(
        pack_x_kernel,
        in_specs=[VMEM] * 3,
        out_specs=VMEM,
        out_shape=jax.ShapeDtypeStruct((8, COLS + 256), F32),
        compiler_params=params(4),
        name="pack_x",
    )(levels, rows_t, from_y)


def one_hot(row, level_ids):
    row = jnp.broadcast_to(row, level_ids.shape)
    return jnp.where(row == level_ids, 1.0, 0.0).astype(BF16)


def features(window, conv, conv_bias, mix, mix_bias):
    pre = jnp.dot(conv, window, preferred_element_type=F32) + conv_bias
    hidden = twice_gelu(pre).astype(BF16)
    mixed = jnp.dot(mix, hidden, preferred_element_type=F32) + mix_bias
    return twice_gelu(mixed).astype(BF16)


def inner_kernel(
    lev_ref, conv_ref, cb_ref, mix_ref, mb_ref, cols_hbm, feat_ref, cols_ref, ext_ref, hot_ref, sems
):
    z = lax.axis_index("py")
    copies = [
        pltpu.make_async_copy(cols_hbm.at[z ^ REL_ORDER[g]], cols_ref.at[g], sems.at[g])
        for g in range(Z)
    ]
    for copy in copies:
        copy.start()
    wide = COLS - 128
    lev = lev_ref[...].astype(F32)
    for b in range(3):
        ext_ref[b] = pltpu.roll(lev, 3 - b, 1)[:, 128:]
    level_ids = iota((LEVELS, wide), 0).astype(F32)

    def make_hot(q, _):
        for b in range(3):
            hot_ref[pl.ds(q * SLOT + b * LEVELS, LEVELS), :] = one_hot(
                ext_ref[b, pl.ds(q + 1, 1), :], level_ids
            )
        return 0

    lax.fori_loop(0, ROWS - 2, make_hot, 0, unroll=2)
    feat_ref[: BLOCK * HID, :] = jnp.zeros((BLOCK * HID, COLS), BF16)
    feat_ref[(BLOCK + ROWS) * HID :, :] = jnp.zeros((BLOCK * HID, COLS), BF16)
    conv_bias = jnp.broadcast_to(cb_ref[...], (2 * HID, wide))
    mix_bias = jnp.broadcast_to(mb_ref[...], (2 * HID, wide))
    for i in range(ROWS // 2 - 2):
        at = (2 * BLOCK + 2 * i) * HID
        feat_ref[at : at + 2 * HID, 128:] = features(
            hot_ref[i * 2 * SLOT : i * 2 * SLOT + WINDOW, :],
            conv_ref[...], conv_bias, mix_ref[...], mix_bias,
        )
    for copy in copies:
        copy.wait()


def inner(levels, conv_w, conv_b, mix_w, mix_b, green_cols):
    wide = COLS - 128
    return pl.pallas_call(
        inner_kernel,
        in_specs=[VMEM] * 5 + [HBM],
        out_specs=[VMEM] * 2,
        out_shape=[
            jax.ShapeDtypeStruct(((ROWS + 2 * BLOCK) * HID, COLS), BF16),
            jax.ShapeDtypeStruct((Z, 2, V, COLS), F32),
        ],
        scratch_shapes=[
            pltpu.VMEM((3, ROWS, wide), F32),
            pltpu.VMEM(((ROWS - 2) * SLOT, wide), BF16),
            pltpu.SemaphoreType.DMA((Z,)),
        ],
        compiler_params=params(16),
        name="inner",
    )(levels, conv_w, conv_b, mix_w, mix_b, hbm(green_cols))


def split_kernel(cols_ref, hi_ref, lo_ref):
    def split(g, _):
        hi_ref[g], lo_ref[g] = split2(cols_ref[g].reshape(2 * V, COLS))
        return 0

    lax.fori_loop(0, Z, split, 0)


def split_cols(cols):
    return pl.pallas_call(
        split_kernel,
        in_specs=[VMEM],
        out_specs=[VMEM] * 2,
        out_shape=[jax.ShapeDtypeStruct((Z, 2 * V, COLS), BF16)] * 2,
        compiler_params=params(4),
        name="split_cols",
    )(cols)


def column_sum(hi_ref, lo_ref, nf_ref, edge_ref, from_y_ref, out_ref, first):
    iy = lax.axis_index("py")
    n = 2 * PART
    sign = jnp.where(iota((1, 128), 1) < V, -1.0, 1.0)
    hi = hi_ref[first : first + 4].reshape(8 * V, COLS)
    lo = lo_ref[first : first + 4].reshape(8 * V, COLS)
    both = lax.dot_general(hi, nf_ref[:n, :], NT, preferred_element_type=F32)
    both = both + lax.dot_general(lo, nf_ref[:n, :], NT, preferred_element_type=F32)
    both = both + lax.dot_general(hi, nf_ref[n:, :], NT, preferred_element_type=F32)
    for g in range(4):
        out = both[2 * V * g : 2 * V * (g + 1)].T
        z = iy ^ REL_ORDER[first + g]
        green = from_y_ref[pl.ds(ROWS + HALO * z, HALO), :]
        green = jnp.concatenate([green, jnp.zeros((4, 128), F32)], axis=0)
        out = out + jnp.dot(edge_ref[:, :8], green, precision=HIGH, preferred_element_type=F32)
        out_ref[g] = out[:PART] + sign * pltpu.roll(out[PART:], V, 1)


def field_kernel(
    lev_ref, from_x_ref, from_y_ref, conv_ref, cb_ref, mix_ref, mb_ref, dec_ref,
    hi_ref, lo_ref, _, send_ref, nf_ref, edge_ref, feat_ref, ext_ref, hot_ref,
):
    first_x = lax.axis_index("px") == 0
    first_y = lax.axis_index("py") == 0
    own = jnp.concatenate([from_y_ref[:ROWS, :], lev_ref[...].astype(F32)], axis=1)
    ext = jnp.concatenate([from_x_ref[:, : 128 + COLS], own], axis=0)
    lane = iota((24, COLS), 1)
    for b in range(3):
        window = pltpu.roll(ext, 3 - b, 1)[:, 128:]
        if b != 1:
            cut = first_y & (lane == (2 if b == 0 else 1))
            window = jnp.where(cut, -1.0, window)
        ext_ref[b] = window
    level_ids = iota((LEVELS, COLS), 0).astype(F32)
    for o in range(4):
        for b in range(3):
            at = pl.ds(o * SLOT + b * LEVELS, LEVELS)
            for w in range(2):
                q = 2 * w + o
                hot_ref[w, at, :] = one_hot(ext_ref[b, q + 5 : q + 6, :], level_ids)
            for t in range(6):
                q = 2 * t + 4 + o
                hot_ref[2, at, t * 128 : (t + 1) * 128] = one_hot(
                    ext_ref[b, q + 5 : q + 6, :128], level_ids[:, :128]
                )
    conv_bias = jnp.broadcast_to(cb_ref[...], (2 * HID, COLS))
    mix_bias = jnp.broadcast_to(mb_ref[...], (2 * HID, COLS))
    slot = iota((1, WINDOW), 1) // SLOT
    for w in range(2):
        keep = jnp.where(first_x & (slot == (3 if w == 0 else 0)), 0.0, 1.0).astype(BF16)
        at = (BLOCK + 2 * w) * HID
        feat_ref[at : at + 2 * HID, :] = features(
            hot_ref[w], conv_ref[...] * keep, conv_bias, mix_ref[...], mix_bias
        )
    tiles = features(
        hot_ref[2, :, :768], conv_ref[...], conv_bias[:, :768], mix_ref[...], mix_bias[:, :768]
    )
    for t in range(6):
        at = (2 * BLOCK + 2 * t) * HID
        feat_ref[at : at + 2 * HID, :128] = tiles[:, t * 128 : (t + 1) * 128]

    lane = iota((1, COLS), 1)
    near = iota((1, 128), 1)
    pillar = iota((1, 2 * BLOCK * HID), 1) // HID
    for i in range(ROWS_EXT // BLOCK):
        dec = dec_ref[...]
        if i < 2:
            keep = jnp.where(first_x & ((pillar >= 6) if i == 0 else (pillar < 2)), 0.0, 1.0)
            dec = dec * keep.astype(BF16)
        at = i * BLOCK * HID
        taps = jnp.dot(
            dec, feat_ref[at : at + 2 * BLOCK * HID, :], preferred_element_type=F32
        )
        acc = jnp.zeros((2 * HALF, COLS), F32)
        edge = jnp.zeros((2 * HALF, 128), F32)
        for s in range(KS):
            part = taps[2 * HALF * s : 2 * HALF * (s + 1), :]
            k = KS - 1 - s
            ok = (lane < COLS - k) & ((lane + k >= 2) | jnp.logical_not(first_y))
            moved = part if k == 0 else pltpu.roll(part, COLS - k, 1)
            acc = acc + jnp.where(ok, moved, 0.0)
            ok = (near >= s) & (near < HALO) & ((near - s < 2) | jnp.logical_not(first_y))
            part = part[:, :128]
            moved = part if s == 0 else pltpu.roll(part, s, 1)
            edge = edge + jnp.where(ok, moved, 0.0)
        for part, values in enumerate(split2(acc)):
            for k in range(2):
                at = (2 * part + k) * PART + i * HALF
                nf_ref[at : at + HALF, :] = values[k * HALF : (k + 1) * HALF]
        for k in range(2):
            at = k * PART + i * HALF
            edge_ref[at : at + HALF, :] = edge[k * HALF : (k + 1) * HALF]

    column_sum(hi_ref, lo_ref, nf_ref, edge_ref, from_y_ref, send_ref, 4)


def field(levels, from_x, from_y, conv_w, conv_b, mix_w, mix_b, dec_w, hi, lo, feat):
    return pl.pallas_call(
        field_kernel,
        in_specs=[VMEM] * 11,
        out_specs=[VMEM] * 4,
        out_shape=[
            jax.ShapeDtypeStruct((4, PART, 128), F32),
            jax.ShapeDtypeStruct((4 * PART, COLS), BF16),
            jax.ShapeDtypeStruct((2 * PART, 128), F32),
            jax.ShapeDtypeStruct(feat.shape, BF16),
        ],
        input_output_aliases={10: 3},
        scratch_shapes=[
            pltpu.VMEM((3, 24, COLS), F32),
            pltpu.VMEM((3, WINDOW, COLS), BF16),
        ],
        compiler_params=params(16),
        name="field",
    )(levels, from_x, from_y, conv_w, conv_b, mix_w, mix_b, dec_w, hi, lo, feat)


def keep_kernel(hi_ref, lo_ref, nf_ref, edge_ref, from_y_ref, out_ref):
    column_sum(hi_ref, lo_ref, nf_ref, edge_ref, from_y_ref, out_ref, 0)


def keep_half(hi, lo, nf, edge, from_y):
    return pl.pallas_call(
        keep_kernel,
        in_specs=[VMEM] * 5,
        out_specs=VMEM,
        out_shape=jax.ShapeDtypeStruct((4, PART, 128), F32),
        compiler_params=params(8),
        name="keep_half",
    )(hi, lo, nf, edge, from_y)


def rows_kernel(from_x_ref, rows_ref, order_ref, out_ref):
    z = lax.axis_index("py")
    green = jnp.concatenate([rows_ref[z, 0], rows_ref[z, 1]], axis=1)
    green = jnp.concatenate([from_x_ref[:, 128 + COLS :], green], axis=0)
    n = ROWS + 8
    green = jnp.concatenate(split2(green), axis=0)
    pick = (order_ref[...] == iota((U, U * 4), 0)).astype(BF16)
    row = iota((3 * PART, 2 * n), 0)
    source = (row % PART) // 4 + (8 - HALO) + jnp.where(row // PART == 1, n, 0)
    spread = (iota((3 * PART, 2 * n), 1) == source).astype(BF16)
    mask = iota((3 * PART, U * 4), 0) % 4 == iota((3 * PART, U * 4), 1) % 4
    for j in range(2):
        ordered = jnp.dot(green[:, j * U : (j + 1) * U], pick, preferred_element_type=F32)
        wide = jnp.dot(spread, ordered.astype(BF16), preferred_element_type=F32)
        out_ref[j * U * 4 : (j + 1) * U * 4, :] = jnp.where(mask, wide, 0.0).T.astype(BF16)


def row_factors(from_x, rows_t, order):
    return pl.pallas_call(
        rows_kernel,
        in_specs=[VMEM] * 3,
        out_specs=VMEM,
        out_shape=jax.ShapeDtypeStruct((2 * U * 4, 3 * PART), BF16),
        compiler_params=params(4),
        name="row_factors",
    )(from_x, rows_t, order)


def focal_kernel(factor_ref, keep_ref, got_ref, b_ref, c_ref, d_ref, out_ref):
    t = ((keep_ref[0] + got_ref[0]) + b_ref[...]) + (c_ref[...] + d_ref[...])
    hi, lo = split2(t)
    out = jnp.dot(
        factor_ref[...], jnp.concatenate([hi, hi, lo], axis=0), preferred_element_type=F32
    )
    n = U * 4
    sign = jnp.where(iota((1, 128), 1) < V, -1.0, 1.0)
    out_ref[...] = (out[:n] + sign * pltpu.roll(out[n:], V, 1)).reshape(out_ref.shape)


def focal_share(factors, keep, got, b, c, d):
    return pl.pallas_call(
        focal_kernel,
        in_specs=[VMEM] * 6,
        out_specs=VMEM,
        out_shape=jax.ShapeDtypeStruct((U // 2, 8, 128), F32),
        compiler_params=params(4),
        name="focal_share",
    )(factors, keep, got, b, c, d)


def total_kernel(x_ref, out_ref):
    s = jnp.sum(x_ref[...], axis=0)
    for u in range(2):
        for k in range(2):
            for p in range(4):
                at = (k * 4 + p) * V
                row = u * 4 + p
                out_ref[0, u : u + 1, at : at + V] = s[row : row + 1, k * V : (k + 1) * V]


def total(parts):
    return pl.pallas_call(
        total_kernel,
        in_specs=[VMEM],
        out_specs=VMEM,
        out_shape=jax.ShapeDtypeStruct((1, 2, 8 * V), F32),
        compiler_params=params(4),
        name="total",
    )(parts)


def conv_weights(conv_table):
    return jnp.concatenate(
        [jnp.pad(conv_table, ((0, 0), (0, SLOT))), jnp.pad(conv_table, ((0, 0), (SLOT, 0)))], axis=0
    )


def mix_weights(mix_weight):
    w = mix_weight * jnp.asarray(0.5, BF16)
    return jnp.concatenate(
        [jnp.pad(w, ((0, 0), (0, HID))), jnp.pad(w, ((0, 0), (HID, 0)))], axis=0
    )


def decoder_weights(decoder):
    d = decoder * jnp.asarray(0.5, BF16)
    d = d[::-1].reshape(KS, KS, 2, 4, HID).transpose(1, 2, 3, 0, 4)
    rows = [
        jnp.pad(d, ((0, 0), (0, 0), (0, 0), (r, BLOCK - 1 - r), (0, 0))) for r in range(BLOCK)
    ]
    return jnp.stack(rows, axis=2).reshape(KS * CH * BLOCK, 2 * BLOCK * HID)


def bias_column(bias):
    return jnp.concatenate([bias, bias])[:, None]


def on_device(
    levels, conv_table, conv_bias, mix_weight, mix_bias, decoder, green_rows, green_cols, focal_order
):
    count_px = lax.axis_size("px")
    count_py = lax.axis_size("py")
    rows_t = jnp.swapaxes(green_rows, 2, 3)
    next_x = [(i, (i + 1) % count_px) for i in range(count_px)]
    next_y = [(i, (i + 1) % count_py) for i in range(count_py)]
    conv_w = conv_weights(conv_table)
    mix_w = mix_weights(mix_weight)
    dec_w = decoder_weights(decoder)
    conv_b = bias_column(conv_bias)
    mix_b = bias_column(mix_bias)
    order = jnp.broadcast_to(focal_order[:, None], (U, 4)).reshape(1, U * 4)
    conv_w, conv_b, mix_w, mix_b, dec_w, order = lax.optimization_barrier(
        (conv_w, conv_b, mix_w, mix_b, dec_w, order)
    )

    from_y = lax.ppermute(pack_y(levels, green_cols), "py", next_y)
    feat, cols = inner(levels, conv_w, conv_b, mix_w, mix_b, green_cols)
    from_y, feat, cols = lax.optimization_barrier((from_y, feat, cols))
    from_x = lax.ppermute(pack_x(levels, rows_t, from_y), "px", next_x)
    hi, lo = split_cols(cols)
    send, nf, edge, _ = field(
        levels, from_x, from_y, conv_w, conv_b, mix_w, mix_b, dec_w, hi, lo, feat
    )

    def swap(x, mask):
        return lax.ppermute(x, "py", [(i, i ^ mask) for i in range(count_py)])

    got = swap(send, 1)
    keep = keep_half(hi, lo, nf, edge, from_y)
    b, c, d = (swap(keep[i] + got[i], 2 * i) for i in (1, 2, 3))
    factors = row_factors(from_x, rows_t, order)
    share = focal_share(factors, keep, got, b, c, d)
    return total(lax.all_to_all(share, "px", 0, 0))


def solution(mesh):
    return jax.shard_map(
        on_device,
        mesh=mesh,
        in_specs=(
            P("px", "py"),
            P(),
            P(),
            P(),
            P(),
            P(),
            P(None, None, None, "px"),
            P(None, None, None, "py"),
            P(),
        ),
        out_specs=P("py", "px", None),
        check_vma=False,
    )
```

```python
import jax
import jax.numpy as jnp
from jax import lax
from jax.experimental import pallas as pl
from jax.experimental.pallas import tpu as pltpu
from jax.sharding import PartitionSpec as P

HIGH = lax.Precision.HIGHEST
F32 = jnp.float32
BF16 = jnp.bfloat16
NT = (((1,), (1,)), ((), ()))
TN = (((0,), (0,)), ((), ()))

ROWS = 16
COLS = 1024
HID = 64
LEVELS = 16
CH = 8
KS = 5
Z = 8
U = 64
V = 64
HALO = 4
ROWS_EXT = ROWS + HALO
SLOT = 3 * LEVELS
WINDOW = 4 * SLOT
BLOCK = 4
REL_ORDER = (0, 2, 4, 6, 1, 3, 5, 7)
PART = ROWS_EXT * CH // 2
HALF = BLOCK * CH // 2
VMEM = pl.BlockSpec(memory_space=pltpu.VMEM)
HBM = pl.BlockSpec(memory_space=pltpu.HBM)


def params(mib):
    return pltpu.CompilerParams(vmem_limit_bytes=mib << 20)

GELU_A = 0.7978845608028654
GELU_B = GELU_A * 0.044715


def iota(shape, dim):
    return lax.broadcasted_iota(jnp.int32, shape, dim)


def twice_gelu(x):
    return x + x * jnp.tanh(x * (GELU_A + GELU_B * (x * x)))


def split2(x):
    hi = x.astype(BF16)
    return hi, (x - hi.astype(F32)).astype(BF16)


def hbm(x):
    return pltpu.with_memory_space_constraint(x, pltpu.HBM)


def pack_kernel(lev_hbm, rows_hbm, cols_hbm, to_x_ref, to_y_ref, lev_ref, tile_ref, rows_ref, cols_ref, sems):
    z = lax.axis_index("py")
    last = pl.ds(COLS - 128, 128)
    copies = [
        pltpu.make_async_copy(cols_hbm.at[:, :, :, last], cols_ref, sems.at[0]),
        pltpu.make_async_copy(lev_hbm.at[pl.ds(8, 8), :], lev_ref, sems.at[1]),
        pltpu.make_async_copy(lev_hbm.at[:, last], tile_ref, sems.at[2]),
        pltpu.make_async_copy(rows_hbm.at[z], rows_ref, sems.at[3]),
    ]
    for copy in copies:
        copy.start()
    for copy in copies[1:]:
        copy.wait()
    to_x_ref[:, :COLS] = lev_ref[...].astype(F32)
    to_x_ref[:, COLS:] = jnp.concatenate([rows_ref[0, 8:, :], rows_ref[1, 8:, :]], axis=1)
    to_y_ref[:ROWS, :] = tile_ref[...].astype(F32)
    copies[0].wait()
    for i in range(Z):
        edge = cols_ref[i].reshape(2 * V, 128).T
        to_y_ref[ROWS + HALO * i : ROWS + HALO * (i + 1), :] = edge[128 - HALO :, :]


def pack(levels, rows_t, green_cols):
    return pl.pallas_call(
        pack_kernel,
        in_specs=[HBM] * 3,
        out_specs=[VMEM] * 2,
        out_shape=[
            jax.ShapeDtypeStruct((8, COLS + 128), F32),
            jax.ShapeDtypeStruct((ROWS + Z * HALO, 128), F32),
        ],
        scratch_shapes=[
            pltpu.VMEM((8, COLS), jnp.int32),
            pltpu.VMEM((ROWS, 128), jnp.int32),
            pltpu.VMEM((2, ROWS, U), F32),
            pltpu.VMEM((Z, 2, V, 128), F32),
            pltpu.SemaphoreType.DMA((4,)),
        ],
        compiler_params=params(4),
        name="pack",
    )(hbm(levels), hbm(rows_t), hbm(green_cols))


def one_hot(row, level_ids):
    row = jnp.broadcast_to(row, level_ids.shape)
    return jnp.where(row == level_ids, 1.0, 0.0).astype(BF16)


def features(window, conv, conv_bias, mix, mix_bias):
    pre = jnp.dot(conv, window, preferred_element_type=F32) + conv_bias
    hidden = twice_gelu(pre).astype(BF16)
    mixed = jnp.dot(mix, hidden, preferred_element_type=F32) + mix_bias
    return twice_gelu(mixed).astype(BF16)


def inner_kernel(
    lev_ref, conv_ref, cb_ref, mix_ref, mb_ref, cols_hbm, feat_ref, hi_ref, lo_ref,
    ext_ref, hot_ref, cols_ref, sems,
):
    z = lax.axis_index("py")
    copies = [
        pltpu.make_async_copy(cols_hbm.at[z ^ REL_ORDER[g]], cols_ref.at[g], sems.at[g])
        for g in range(Z)
    ]
    for copy in copies:
        copy.start()
    wide = COLS - 128
    lev = lev_ref[...].astype(F32)
    for b in range(3):
        ext_ref[b] = pltpu.roll(lev, 3 - b, 1)[:, 128:]
    level_ids = iota((LEVELS, wide), 0).astype(F32)

    def make_hot(q, _):
        for b in range(3):
            hot_ref[pl.ds(q * SLOT + b * LEVELS, LEVELS), :] = one_hot(
                ext_ref[b, pl.ds(q + 1, 1), :], level_ids
            )
        return 0

    lax.fori_loop(0, ROWS - 2, make_hot, 0, unroll=2)
    feat_ref[: BLOCK * HID, :] = jnp.zeros((BLOCK * HID, COLS), BF16)
    feat_ref[(BLOCK + ROWS) * HID :, :] = jnp.zeros((BLOCK * HID, COLS), BF16)
    conv_bias = jnp.broadcast_to(cb_ref[...], (2 * HID, wide))
    mix_bias = jnp.broadcast_to(mb_ref[...], (2 * HID, wide))
    for i in range(ROWS // 2 - 2):
        at = (2 * BLOCK + 2 * i) * HID
        feat_ref[at : at + 2 * HID, 128:] = features(
            hot_ref[i * 2 * SLOT : i * 2 * SLOT + WINDOW, :],
            conv_ref[...], conv_bias, mix_ref[...], mix_bias,
        )
    for copy in copies:
        copy.wait()

    def split(g, _):
        hi_ref[g], lo_ref[g] = split2(cols_ref[g].reshape(2 * V, COLS))
        return 0

    lax.fori_loop(0, Z, split, 0)


def inner(levels, conv_w, conv_b, mix_w, mix_b, green_cols):
    wide = COLS - 128
    return pl.pallas_call(
        inner_kernel,
        in_specs=[VMEM] * 5 + [HBM],
        out_specs=[VMEM] * 3,
        out_shape=[
            jax.ShapeDtypeStruct(((ROWS + 2 * BLOCK) * HID, COLS), BF16),
            jax.ShapeDtypeStruct((Z, 2 * V, COLS), BF16),
            jax.ShapeDtypeStruct((Z, 2 * V, COLS), BF16),
        ],
        scratch_shapes=[
            pltpu.VMEM((3, ROWS, wide), F32),
            pltpu.VMEM(((ROWS - 2) * SLOT, wide), BF16),
            pltpu.VMEM((Z, 2, V, COLS), F32),
            pltpu.SemaphoreType.DMA((Z,)),
        ],
        compiler_params=params(16),
        name="inner",
    )(levels, conv_w, conv_b, mix_w, mix_b, hbm(green_cols))


def outer_kernel(
    lev_ref, from_x_ref, from_y_ref, conv_ref, cb_ref, mix_ref, mb_ref, _, feat_ref, ext_ref, hot_ref
):
    first_x = lax.axis_index("px") == 0
    first_y = lax.axis_index("py") == 0
    ext = jnp.concatenate([from_x_ref[:, :COLS], lev_ref[...].astype(F32)], axis=0)
    left = jnp.concatenate([jnp.zeros((8, 128), F32), from_y_ref[:ROWS, :]], axis=0)
    lane = iota((24, 128), 1)
    for b in range(3):
        window = pltpu.roll(ext, 3 - b, 1)
        tile = pltpu.roll(jnp.concatenate([left, ext[:, :128]], axis=1), 3 - b, 1)[:, 128:]
        if b != 1:
            tile = jnp.where(first_y & (lane == (2 if b == 0 else 1)), -1.0, tile)
        ext_ref[b] = jnp.concatenate([tile, window[:, 128:]], axis=1)
    wide = COLS - 128
    level_ids = iota((LEVELS, wide), 0).astype(F32)
    for o in range(4):
        for b in range(3):
            at = pl.ds(o * SLOT + b * LEVELS, LEVELS)
            for w in range(2):
                q = 2 * w + o
                hot_ref[w, at, :] = one_hot(ext_ref[b, q + 5 : q + 6, 128:], level_ids)
            for t in range(6):
                q = 2 * t + 4 + o
                hot_ref[2, at, t * 128 : (t + 1) * 128] = one_hot(
                    ext_ref[b, q + 5 : q + 6, :128], level_ids[:, :128]
                )
    conv_bias = jnp.broadcast_to(cb_ref[...], (2 * HID, wide))
    mix_bias = jnp.broadcast_to(mb_ref[...], (2 * HID, wide))
    for w in range(2):
        at = (BLOCK + 2 * w) * HID
        feat_ref[at : at + 2 * HID, 128:] = features(
            hot_ref[w], cut_conv(conv_ref[...], w, first_x), conv_bias, mix_ref[...], mix_bias
        )
    tiles = features(
        hot_ref[2, :, :768], conv_ref[...], conv_bias[:, :768], mix_ref[...], mix_bias[:, :768]
    )
    for t in range(6):
        at = (2 * BLOCK + 2 * t) * HID
        feat_ref[at : at + 2 * HID, :128] = tiles[:, t * 128 : (t + 1) * 128]


def cut_conv(conv, w, first_x):
    slot = iota((1, WINDOW), 1) // SLOT
    keep = jnp.where(first_x & (slot == (3 if w == 0 else 0)), 0.0, 1.0)
    return conv * keep.astype(BF16)


def outer(levels, from_x, from_y, conv_w, conv_b, mix_w, mix_b, feat):
    return pl.pallas_call(
        outer_kernel,
        in_specs=[VMEM] * 8,
        out_specs=VMEM,
        out_shape=jax.ShapeDtypeStruct(feat.shape, BF16),
        input_output_aliases={7: 0},
        scratch_shapes=[
            pltpu.VMEM((3, 24, COLS), F32),
            pltpu.VMEM((3, WINDOW, COLS - 128), BF16),
        ],
        compiler_params=params(12),
        name="outer",
    )(levels, from_x, from_y, conv_w, conv_b, mix_w, mix_b, feat)


def column_sum(hi_ref, lo_ref, nf_ref, edge_ref, from_y_ref, out_ref, first, count):
    iy = lax.axis_index("py")
    n = 2 * PART
    sign = jnp.where(iota((1, 128), 1) < V, -1.0, 1.0)
    hi = hi_ref[first : first + count].reshape(2 * V * count, COLS)
    lo = lo_ref[first : first + count].reshape(2 * V * count, COLS)
    both = lax.dot_general(hi, nf_ref[:n, :], NT, preferred_element_type=F32)
    both = both + lax.dot_general(lo, nf_ref[:n, :], NT, preferred_element_type=F32)
    both = both + lax.dot_general(hi, nf_ref[n:, :], NT, preferred_element_type=F32)
    for g in range(count):
        out = both[2 * V * g : 2 * V * (g + 1)].T
        z = iy ^ REL_ORDER[first + g]
        green = from_y_ref[pl.ds(ROWS + HALO * z, HALO), :]
        green = jnp.concatenate([green, jnp.zeros((4, 128), F32)], axis=0)
        out = out + jnp.dot(edge_ref[:, :8], green, precision=HIGH, preferred_element_type=F32)
        out_ref[g] = out[:PART] + sign * pltpu.roll(out[PART:], V, 1)


def field_kernel(
    lev_ref, from_x_ref, from_y_ref, from_d_ref, conv_ref, cb_ref, mix_ref, mb_ref, dec_ref,
    hi_ref, lo_ref, _, send_ref, nf_ref, edge_ref, feat_ref, ext_ref, hot_ref,
):
    first_x = lax.axis_index("px") == 0
    first_y = lax.axis_index("py") == 0
    tile = jnp.concatenate([from_x_ref[:, :128], lev_ref[:8, :128].astype(F32)], axis=0)
    left = jnp.concatenate([from_d_ref[:, COLS - 128 : COLS], from_y_ref[:8, :]], axis=0)
    ext = jnp.concatenate([left, tile], axis=1)
    lane = iota((16, 128), 1)
    for b in range(3):
        window = pltpu.roll(ext, 3 - b, 1)[:, 128:]
        if b != 1:
            window = jnp.where(first_y & (lane == (2 if b == 0 else 1)), -1.0, window)
        ext_ref[b] = window
    level_ids = iota((LEVELS, 128), 0).astype(F32)
    for w in range(2):
        for o in range(4):
            for b in range(3):
                q = 2 * w + o
                at = o * SLOT + b * LEVELS
                hot_ref[w, at : at + LEVELS, :] = one_hot(ext_ref[b, q + 5 : q + 6, :], level_ids)
    for w in range(2):
        at = (BLOCK + 2 * w) * HID
        feat_ref[at : at + 2 * HID, :128] = features(
            hot_ref[w], cut_conv(conv_ref[...], w, first_x), cb_ref[...], mix_ref[...], mb_ref[...]
        )

    lane = iota((1, COLS), 1)
    near = iota((1, 128), 1)
    pillar = iota((1, 2 * BLOCK * HID), 1) // HID
    for i in reversed(range(ROWS_EXT // BLOCK)):
        dec = dec_ref[...]
        if i < 2:
            keep = jnp.where(first_x & ((pillar >= 6) if i == 0 else (pillar < 2)), 0.0, 1.0)
            dec = dec * keep.astype(BF16)
        at = i * BLOCK * HID
        taps = jnp.dot(
            dec, feat_ref[at : at + 2 * BLOCK * HID, :], preferred_element_type=F32
        )
        acc = jnp.zeros((2 * HALF, COLS), F32)
        edge = jnp.zeros((2 * HALF, 128), F32)
        for s in range(KS):
            part = taps[2 * HALF * s : 2 * HALF * (s + 1), :]
            k = KS - 1 - s
            ok = (lane < COLS - k) & ((lane + k >= 2) | jnp.logical_not(first_y))
            moved = part if k == 0 else pltpu.roll(part, COLS - k, 1)
            acc = acc + jnp.where(ok, moved, 0.0)
            ok = (near >= s) & (near < HALO) & ((near - s < 2) | jnp.logical_not(first_y))
            part = part[:, :128]
            moved = part if s == 0 else pltpu.roll(part, s, 1)
            edge = edge + jnp.where(ok, moved, 0.0)
        for part, values in enumerate(split2(acc)):
            for k in range(2):
                at = (2 * part + k) * PART + i * HALF
                nf_ref[at : at + HALF, :] = values[k * HALF : (k + 1) * HALF]
        for k in range(2):
            at = k * PART + i * HALF
            edge_ref[at : at + HALF, :] = edge[k * HALF : (k + 1) * HALF]

    column_sum(hi_ref, lo_ref, nf_ref, edge_ref, from_y_ref, send_ref, 4, 4)


def field(levels, from_x, from_y, from_d, conv_w, conv_b, mix_w, mix_b, dec_w, hi, lo, feat):
    return pl.pallas_call(
        field_kernel,
        in_specs=[VMEM] * 12,
        out_specs=[VMEM] * 4,
        out_shape=[
            jax.ShapeDtypeStruct((4, PART, 128), F32),
            jax.ShapeDtypeStruct((4 * PART, COLS), BF16),
            jax.ShapeDtypeStruct((2 * PART, 128), F32),
            jax.ShapeDtypeStruct(feat.shape, BF16),
        ],
        input_output_aliases={11: 3},
        scratch_shapes=[
            pltpu.VMEM((3, 16, 128), F32),
            pltpu.VMEM((2, WINDOW, 128), BF16),
        ],
        compiler_params=params(12),
        name="field",
    )(levels, from_x, from_y, from_d, conv_w, conv_b, mix_w, mix_b, dec_w, hi, lo, feat)


def keep_planes(hi, lo, nf, edge, from_y, first, count):
    def keep_kernel(hi_ref, lo_ref, nf_ref, edge_ref, from_y_ref, out_ref):
        column_sum(hi_ref, lo_ref, nf_ref, edge_ref, from_y_ref, out_ref, first, count)

    return pl.pallas_call(
        keep_kernel,
        in_specs=[VMEM] * 5,
        out_specs=VMEM,
        out_shape=jax.ShapeDtypeStruct((count, PART, 128), F32),
        compiler_params=params(8),
        name="keep_planes",
    )(hi, lo, nf, edge, from_y)


def rows_kernel(from_x_ref, rows_ref, order_ref, out_ref):
    z = lax.axis_index("py")
    green = jnp.concatenate([rows_ref[z, 0], rows_ref[z, 1]], axis=1)
    green = jnp.concatenate([from_x_ref[:, COLS:], green], axis=0)
    n = ROWS + 8
    green = jnp.concatenate(split2(green), axis=0)
    pick = (order_ref[...] == iota((U, U * 4), 0)).astype(BF16)
    row = iota((3 * PART, 2 * n), 0)
    source = (row % PART) // 4 + (8 - HALO) + jnp.where(row // PART == 1, n, 0)
    spread = (iota((3 * PART, 2 * n), 1) == source).astype(BF16)
    mask = iota((3 * PART, U * 4), 0) % 4 == iota((3 * PART, U * 4), 1) % 4
    for j in range(2):
        ordered = jnp.dot(green[:, j * U : (j + 1) * U], pick, preferred_element_type=F32)
        wide = jnp.dot(spread, ordered.astype(BF16), preferred_element_type=F32)
        out_ref[j * U * 4 : (j + 1) * U * 4, :] = jnp.where(mask, wide, 0.0).T.astype(BF16)


def row_factors(from_x, rows_t, order):
    return pl.pallas_call(
        rows_kernel,
        in_specs=[VMEM] * 3,
        out_specs=VMEM,
        out_shape=jax.ShapeDtypeStruct((2 * U * 4, 3 * PART), BF16),
        compiler_params=params(4),
        name="row_factors",
    )(from_x, rows_t, order)


def focal_kernel(factor_ref, keep_ref, got_ref, b_ref, c_ref, d_ref, out_ref):
    t = ((keep_ref[0] + got_ref[0]) + b_ref[...]) + (c_ref[...] + d_ref[...])
    hi, lo = split2(t)
    out = jnp.dot(
        factor_ref[...], jnp.concatenate([hi, hi, lo], axis=0), preferred_element_type=F32
    )
    n = U * 4
    sign = jnp.where(iota((1, 128), 1) < V, -1.0, 1.0)
    out_ref[...] = (out[:n] + sign * pltpu.roll(out[n:], V, 1)).reshape(out_ref.shape)


def focal_share(factors, keep, got, b, c, d):
    return pl.pallas_call(
        focal_kernel,
        in_specs=[VMEM] * 6,
        out_specs=VMEM,
        out_shape=jax.ShapeDtypeStruct((U // 2, 8, 128), F32),
        compiler_params=params(4),
        name="focal_share",
    )(factors, keep, got, b, c, d)


def total_kernel(x_ref, out_ref):
    s = jnp.sum(x_ref[...], axis=0)
    for u in range(2):
        for k in range(2):
            for p in range(4):
                at = (k * 4 + p) * V
                row = u * 4 + p
                out_ref[0, u : u + 1, at : at + V] = s[row : row + 1, k * V : (k + 1) * V]


def total(parts):
    return pl.pallas_call(
        total_kernel,
        in_specs=[VMEM],
        out_specs=VMEM,
        out_shape=jax.ShapeDtypeStruct((1, 2, 8 * V), F32),
        compiler_params=params(4),
        name="total",
    )(parts)


def conv_weights(conv_table):
    return jnp.concatenate(
        [jnp.pad(conv_table, ((0, 0), (0, SLOT))), jnp.pad(conv_table, ((0, 0), (SLOT, 0)))], axis=0
    )


def mix_weights(mix_weight):
    w = mix_weight * jnp.asarray(0.5, BF16)
    return jnp.concatenate(
        [jnp.pad(w, ((0, 0), (0, HID))), jnp.pad(w, ((0, 0), (HID, 0)))], axis=0
    )


def decoder_weights(decoder):
    d = decoder * jnp.asarray(0.5, BF16)
    d = d[::-1].reshape(KS, KS, 2, 4, HID).transpose(1, 2, 3, 0, 4)
    rows = [
        jnp.pad(d, ((0, 0), (0, 0), (0, 0), (r, BLOCK - 1 - r), (0, 0))) for r in range(BLOCK)
    ]
    return jnp.stack(rows, axis=2).reshape(KS * CH * BLOCK, 2 * BLOCK * HID)


def bias_column(bias):
    return jnp.concatenate([bias, bias])[:, None]


def on_device(
    levels, conv_table, conv_bias, mix_weight, mix_bias, decoder, green_rows, green_cols, focal_order
):
    count_px = lax.axis_size("px")
    count_py = lax.axis_size("py")
    rows_t = jnp.swapaxes(green_rows, 2, 3)
    next_x = [(i, (i + 1) % count_px) for i in range(count_px)]
    next_y = [(i, (i + 1) % count_py) for i in range(count_py)]
    conv_w = conv_weights(conv_table)
    mix_w = mix_weights(mix_weight)
    dec_w = decoder_weights(decoder)
    conv_b = bias_column(conv_bias)
    mix_b = bias_column(mix_bias)
    order = jnp.broadcast_to(focal_order[:, None], (U, 4)).reshape(1, U * 4)
    conv_w, conv_b, mix_w, mix_b, dec_w, order = lax.optimization_barrier(
        (conv_w, conv_b, mix_w, mix_b, dec_w, order)
    )

    to_x, to_y = pack(levels, rows_t, green_cols)
    from_x = lax.ppermute(to_x, "px", next_x)
    from_y = lax.ppermute(to_y, "py", next_y)
    feat, hi, lo = inner(levels, conv_w, conv_b, mix_w, mix_b, green_cols)
    from_x, from_y, feat = lax.optimization_barrier((from_x, from_y, feat))
    from_d = lax.ppermute(from_x, "py", next_y)
    feat = outer(levels, from_x, from_y, conv_w, conv_b, mix_w, mix_b, feat)
    send, nf, edge, _ = field(
        levels, from_x, from_y, from_d, conv_w, conv_b, mix_w, mix_b, dec_w, hi, lo, feat
    )

    def swap(x, mask):
        return lax.ppermute(x, "py", [(i, i ^ mask) for i in range(count_py)])

    got = swap(send, 1)
    keep = keep_planes(hi, lo, nf, edge, from_y, 1, 3)
    b, c, d = (swap(keep[i - 1] + got[i], 2 * i) for i in (1, 2, 3))
    keep = keep_planes(hi, lo, nf, edge, from_y, 0, 1)
    factors = row_factors(from_x, rows_t, order)
    share = focal_share(factors, keep, got, b, c, d)
    return total(lax.all_to_all(share, "px", 0, 0))


def solution(mesh):
    return jax.shard_map(
        on_device,
        mesh=mesh,
        in_specs=(
            P("px", "py"),
            P(),
            P(),
            P(),
            P(),
            P(),
            P(None, None, None, "px"),
            P(None, None, None, "py"),
            P(),
        ),
        out_specs=P("py", "px", None),
        check_vma=False,
    )
```

```python
import jax
import jax.numpy as jnp
from jax import lax
from jax.experimental import pallas as pl
from jax.experimental.pallas import tpu as pltpu
from jax.sharding import PartitionSpec as P

HIGH = lax.Precision.HIGHEST
F32 = jnp.float32
BF16 = jnp.bfloat16
NT = (((1,), (1,)), ((), ()))
TN = (((0,), (0,)), ((), ()))

ROWS = 16
COLS = 1024
HID = 64
LEVELS = 16
CH = 8
KS = 5
Z = 8
U = 64
V = 64
HALO = 4
SHIFT = 5
PILLAR_ROWS = ROWS + KS - 1
SLOT = 3 * LEVELS
WINDOW = 4 * SLOT
BLOCK = 4
REL_ORDER = (0, 2, 4, 6, 1, 3, 5, 7)
PART = ROWS * CH // 2
HALF = BLOCK * CH // 2
VMEM = pl.BlockSpec(memory_space=pltpu.VMEM)
HBM = pl.BlockSpec(memory_space=pltpu.HBM)


def params(mib):
    return pltpu.CompilerParams(vmem_limit_bytes=mib << 20)

GELU_A = 0.7978845608028654
GELU_B = GELU_A * 0.044715


def iota(shape, dim):
    return lax.broadcasted_iota(jnp.int32, shape, dim)


def twice_gelu(x):
    return x + x * jnp.tanh(x * (GELU_A + GELU_B * (x * x)))


def split2(x):
    hi = x.astype(BF16)
    return hi, (x - hi.astype(F32)).astype(BF16)


def hbm(x):
    return pltpu.with_memory_space_constraint(x, pltpu.HBM)


def pack_kernel(lev_hbm, rows_hbm, cols_hbm, to_x_ref, to_y_ref, lev_ref, tile_ref, rows_ref, cols_ref, sems):
    z = lax.axis_index("py")
    last = pl.ds(COLS - 128, 128)
    copies = [
        pltpu.make_async_copy(cols_hbm.at[:, :, :, last], cols_ref, sems.at[0]),
        pltpu.make_async_copy(lev_hbm.at[pl.ds(8, 8), :], lev_ref, sems.at[1]),
        pltpu.make_async_copy(lev_hbm.at[:, last], tile_ref, sems.at[2]),
        pltpu.make_async_copy(rows_hbm.at[z], rows_ref, sems.at[3]),
    ]
    for copy in copies:
        copy.start()
    for copy in copies[1:]:
        copy.wait()
    to_x_ref[:, :COLS] = lev_ref[...].astype(F32)
    to_x_ref[:, COLS:] = jnp.concatenate([rows_ref[0, 8:, :], rows_ref[1, 8:, :]], axis=1)
    to_y_ref[:ROWS, :] = tile_ref[...].astype(F32)
    copies[0].wait()
    for i in range(Z):
        edge = cols_ref[i].reshape(2 * V, 128).T
        to_y_ref[ROWS + HALO * i : ROWS + HALO * (i + 1), :] = edge[128 - HALO :, :]


def pack(levels, rows_t, green_cols):
    return pl.pallas_call(
        pack_kernel,
        in_specs=[HBM] * 3,
        out_specs=[VMEM] * 2,
        out_shape=[
            jax.ShapeDtypeStruct((8, COLS + 128), F32),
            jax.ShapeDtypeStruct((ROWS + Z * HALO, 128), F32),
        ],
        scratch_shapes=[
            pltpu.VMEM((8, COLS), jnp.int32),
            pltpu.VMEM((ROWS, 128), jnp.int32),
            pltpu.VMEM((2, ROWS, U), F32),
            pltpu.VMEM((Z, 2, V, 128), F32),
            pltpu.SemaphoreType.DMA((4,)),
        ],
        compiler_params=params(4),
        name="pack",
    )(hbm(levels), hbm(rows_t), hbm(green_cols))


def one_hot(row, level_ids):
    row = jnp.broadcast_to(row, level_ids.shape)
    return jnp.where(row == level_ids, 1.0, 0.0).astype(BF16)


def features(window, conv, conv_bias, mix, mix_bias):
    pre = jnp.dot(conv, window, preferred_element_type=F32) + conv_bias
    hidden = twice_gelu(pre).astype(BF16)
    mixed = jnp.dot(mix, hidden, preferred_element_type=F32) + mix_bias
    return twice_gelu(mixed).astype(BF16)


def inner_kernel(
    lev_ref, conv_ref, cb_ref, mix_ref, mb_ref, cols_hbm, feat_ref, hi_ref, lo_ref,
    ext_ref, hot_ref, cols_ref, sems,
):
    z = lax.axis_index("py")
    copies = [
        pltpu.make_async_copy(cols_hbm.at[z ^ REL_ORDER[g]], cols_ref.at[g], sems.at[g])
        for g in range(Z)
    ]
    for copy in copies:
        copy.start()
    wide = COLS - 128
    lev = lev_ref[...].astype(F32)
    for b in range(3):
        ext_ref[b] = pltpu.roll(lev, 3 - b, 1)[:, 128:]
    level_ids = iota((LEVELS, wide), 0).astype(F32)

    def make_hot(q, _):
        for b in range(3):
            hot_ref[pl.ds(q * SLOT + b * LEVELS, LEVELS), :] = one_hot(
                ext_ref[b, pl.ds(q, 1), :], level_ids
            )
        return 0

    lax.fori_loop(0, ROWS - 2, make_hot, 0, unroll=2)
    conv_bias = jnp.broadcast_to(cb_ref[...], (2 * HID, wide))
    mix_bias = jnp.broadcast_to(mb_ref[...], (2 * HID, wide))
    for i in range(ROWS // 2 - 2):
        at = (8 + 2 * i) * HID
        feat_ref[at : at + 2 * HID, 128:] = features(
            hot_ref[i * 2 * SLOT : i * 2 * SLOT + WINDOW, :],
            conv_ref[...], conv_bias, mix_ref[...], mix_bias,
        )
    for copy in copies:
        copy.wait()

    def split(g, _):
        hi_ref[g], lo_ref[g] = split2(cols_ref[g].reshape(2 * V, COLS))
        return 0

    lax.fori_loop(0, Z, split, 0)


def inner(levels, conv_w, conv_b, mix_w, mix_b, green_cols):
    wide = COLS - 128
    return pl.pallas_call(
        inner_kernel,
        in_specs=[VMEM] * 5 + [HBM],
        out_specs=[VMEM] * 3,
        out_shape=[
            jax.ShapeDtypeStruct((PILLAR_ROWS * HID, COLS), BF16),
            jax.ShapeDtypeStruct((Z, 2 * V, COLS), BF16),
            jax.ShapeDtypeStruct((Z, 2 * V, COLS), BF16),
        ],
        scratch_shapes=[
            pltpu.VMEM((3, ROWS, wide), F32),
            pltpu.VMEM(((ROWS - 2) * SLOT, wide), BF16),
            pltpu.VMEM((Z, 2, V, COLS), F32),
            pltpu.SemaphoreType.DMA((Z,)),
        ],
        compiler_params=params(16),
        name="inner",
    )(levels, conv_w, conv_b, mix_w, mix_b, hbm(green_cols))


def outer_kernel(
    lev_ref, from_x_ref, from_y_ref, conv_ref, cb_ref, mix_ref, mb_ref, _, feat_ref, ext_ref, hot_ref
):
    first_x = lax.axis_index("px") == 0
    first_y = lax.axis_index("py") == 0
    ext = jnp.concatenate([from_x_ref[:, :COLS], lev_ref[...].astype(F32)], axis=0)
    left = jnp.concatenate([jnp.zeros((8, 128), F32), from_y_ref[:ROWS, :]], axis=0)
    lane = iota((24, 128), 1)
    for b in range(3):
        window = pltpu.roll(ext, 3 - b, 1)
        tile = pltpu.roll(jnp.concatenate([left, ext[:, :128]], axis=1), 3 - b, 1)[:, 128:]
        if b != 1:
            tile = jnp.where(first_y & (lane == (2 if b == 0 else 1)), -1.0, tile)
        ext_ref[b] = jnp.concatenate([tile, window[:, 128:]], axis=1)
    wide = COLS - 128
    level_ids = iota((LEVELS, wide), 0).astype(F32)
    for o in range(4):
        for b in range(3):
            at = pl.ds(o * SLOT + b * LEVELS, LEVELS)
            for w in range(4):
                e = 2 * w + o
                hot_ref[w, at, :] = one_hot(ext_ref[b, e : e + 1, 128:], level_ids)
            for t in range(6):
                e = 2 * t + 8 + o
                hot_ref[4, at, t * 128 : (t + 1) * 128] = one_hot(
                    ext_ref[b, e : e + 1, :128], level_ids[:, :128]
                )
    conv_bias = jnp.broadcast_to(cb_ref[...], (2 * HID, wide))
    mix_bias = jnp.broadcast_to(mb_ref[...], (2 * HID, wide))
    for w in range(4):
        at = 2 * w * HID
        conv = cut_conv(conv_ref[...], first_x) if w == 3 else conv_ref[...]
        feat_ref[at : at + 2 * HID, 128:] = features(
            hot_ref[w], conv, conv_bias, mix_ref[...], mix_bias
        )
    tiles = features(
        hot_ref[4, :, :768], conv_ref[...], conv_bias[:, :768], mix_ref[...], mix_bias[:, :768]
    )
    for t in range(6):
        at = (8 + 2 * t) * HID
        feat_ref[at : at + 2 * HID, :128] = tiles[:, t * 128 : (t + 1) * 128]


def cut_conv(conv, first_x):
    slot = iota((2 * HID, WINDOW), 1) // SLOT
    row = iota((2 * HID, WINDOW), 0) // HID
    keep = jnp.where(first_x & (slot + row == 2) & (slot > 0), 0.0, 1.0)
    return conv * keep.astype(BF16)


def outer(levels, from_x, from_y, conv_w, conv_b, mix_w, mix_b, feat):
    return pl.pallas_call(
        outer_kernel,
        in_specs=[VMEM] * 8,
        out_specs=VMEM,
        out_shape=jax.ShapeDtypeStruct(feat.shape, BF16),
        input_output_aliases={7: 0},
        scratch_shapes=[
            pltpu.VMEM((3, 24, COLS), F32),
            pltpu.VMEM((5, WINDOW, COLS - 128), BF16),
        ],
        compiler_params=params(12),
        name="outer",
    )(levels, from_x, from_y, conv_w, conv_b, mix_w, mix_b, feat)


def column_sum(hi_ref, lo_ref, nf_ref, edge_ref, from_y_ref, out_ref, first, count):
    iy = lax.axis_index("py")
    n = 2 * PART
    sign = jnp.where(iota((1, 128), 1) < V, -1.0, 1.0)
    hi = hi_ref[first : first + count].reshape(2 * V * count, COLS)
    lo = lo_ref[first : first + count].reshape(2 * V * count, COLS)
    both = lax.dot_general(hi, nf_ref[...], NT, preferred_element_type=F32)
    both = both[:, :n] + both[:, n:]
    both = both + lax.dot_general(lo, nf_ref[:n, :], NT, preferred_element_type=F32)
    for g in range(count):
        out = both[2 * V * g : 2 * V * (g + 1)].T
        z = iy ^ REL_ORDER[first + g]
        green = from_y_ref[pl.ds(ROWS + HALO * z, HALO), :]
        green = jnp.concatenate([green, jnp.zeros((4, 128), F32)], axis=0)
        out = out + jnp.dot(edge_ref[:, :8], green, precision=HIGH, preferred_element_type=F32)
        out_ref[g] = out[:PART] + sign * pltpu.roll(out[PART:], V, 1)


def field_kernel(
    lev_ref, from_x_ref, from_y_ref, from_d_ref, conv_ref, cb_ref, mix_ref, mb_ref, dec_ref,
    hi_ref, lo_ref, _, send_ref, nf_ref, edge_ref, feat_ref, ext_ref, hot_ref,
):
    first_x = lax.axis_index("px") == 0
    first_y = lax.axis_index("py") == 0
    tile = jnp.concatenate([from_x_ref[:, :128], lev_ref[:8, :128].astype(F32)], axis=0)
    left = jnp.concatenate([from_d_ref[:, COLS - 128 : COLS], from_y_ref[:8, :]], axis=0)
    ext = jnp.concatenate([left, tile], axis=1)
    lane = iota((16, 128), 1)
    for b in range(3):
        window = pltpu.roll(ext, 3 - b, 1)[:, 128:]
        if b != 1:
            window = jnp.where(first_y & (lane == (2 if b == 0 else 1)), -1.0, window)
        ext_ref[b] = window
    level_ids = iota((LEVELS, 128), 0).astype(F32)
    for w in range(4):
        for o in range(4):
            for b in range(3):
                e = 2 * w + o
                at = o * SLOT + b * LEVELS
                hot_ref[at : at + LEVELS, w * 128 : (w + 1) * 128] = one_hot(
                    ext_ref[b, e : e + 1, :], level_ids
                )
    tiles = features(
        hot_ref[:, :384], conv_ref[...], cb_ref[...], mix_ref[...], mb_ref[...]
    )
    for w in range(3):
        feat_ref[2 * w * HID : (2 * w + 2) * HID, :128] = tiles[:, w * 128 : (w + 1) * 128]
    feat_ref[6 * HID : 8 * HID, :128] = features(
        hot_ref[:, 384:], cut_conv(conv_ref[...], first_x), cb_ref[...], mix_ref[...], mb_ref[...]
    )

    lane = iota((1, COLS), 1)
    near = iota((1, 128), 1)
    shape = (KS * CH * BLOCK, 2 * BLOCK * HID)
    sample = iota(shape, 0) // 4 % BLOCK - SHIFT
    pillar = iota(shape, 1) // HID - SHIFT - 2
    for i in reversed(range(ROWS // BLOCK)):
        dec = dec_ref[...]
        if i < 2:
            at = i * BLOCK
            apart = (sample + at >= 0) != (pillar + at >= 0)
            keep = jnp.where(first_x & apart, 0.0, 1.0)
            dec = dec * keep.astype(BF16)
        at = i * BLOCK * HID
        taps = jnp.dot(
            dec, feat_ref[at : at + 2 * BLOCK * HID, :], preferred_element_type=F32
        )
        acc = jnp.zeros((2 * HALF, COLS), F32)
        edge = jnp.zeros((2 * HALF, 128), F32)
        for s in range(KS):
            part = taps[2 * HALF * s : 2 * HALF * (s + 1), :]
            k = KS - 1 - s
            ok = (lane < COLS - k) & ((lane + k >= 2) | jnp.logical_not(first_y))
            moved = part if k == 0 else pltpu.roll(part, COLS - k, 1)
            acc = acc + jnp.where(ok, moved, 0.0)
            ok = (near >= s) & (near < HALO) & ((near - s < 2) | jnp.logical_not(first_y))
            part = part[:, :128]
            moved = part if s == 0 else pltpu.roll(part, s, 1)
            edge = edge + jnp.where(ok, moved, 0.0)
        for part, values in enumerate(split2(acc)):
            for k in range(2):
                at = (2 * part + k) * PART + i * HALF
                nf_ref[at : at + HALF, :] = values[k * HALF : (k + 1) * HALF]
        for k in range(2):
            at = k * PART + i * HALF
            edge_ref[at : at + HALF, :] = edge[k * HALF : (k + 1) * HALF]

    column_sum(hi_ref, lo_ref, nf_ref, edge_ref, from_y_ref, send_ref, 4, 4)


def field(levels, from_x, from_y, from_d, conv_w, conv_b, mix_w, mix_b, dec_w, hi, lo, feat):
    return pl.pallas_call(
        field_kernel,
        in_specs=[VMEM] * 12,
        out_specs=[VMEM] * 4,
        out_shape=[
            jax.ShapeDtypeStruct((4, PART, 128), F32),
            jax.ShapeDtypeStruct((4 * PART, COLS), BF16),
            jax.ShapeDtypeStruct((2 * PART, 128), F32),
            jax.ShapeDtypeStruct(feat.shape, BF16),
        ],
        input_output_aliases={11: 3},
        scratch_shapes=[
            pltpu.VMEM((3, 16, 128), F32),
            pltpu.VMEM((WINDOW, 512), BF16),
        ],
        compiler_params=params(12),
        name="field",
    )(levels, from_x, from_y, from_d, conv_w, conv_b, mix_w, mix_b, dec_w, hi, lo, feat)


def keep_planes(hi, lo, nf, edge, from_y, first, count):
    def keep_kernel(hi_ref, lo_ref, nf_ref, edge_ref, from_y_ref, out_ref):
        column_sum(hi_ref, lo_ref, nf_ref, edge_ref, from_y_ref, out_ref, first, count)

    return pl.pallas_call(
        keep_kernel,
        in_specs=[VMEM] * 5,
        out_specs=VMEM,
        out_shape=jax.ShapeDtypeStruct((count, PART, 128), F32),
        compiler_params=params(8),
        name="keep_planes",
    )(hi, lo, nf, edge, from_y)


def rows_kernel(from_x_ref, rows_ref, order_ref, out_ref):
    z = lax.axis_index("py")
    green = jnp.concatenate([rows_ref[z, 0], rows_ref[z, 1]], axis=1)
    green = jnp.concatenate([from_x_ref[:, COLS:], green], axis=0)
    n = ROWS + 8
    green = jnp.concatenate(split2(green), axis=0)
    pick = (order_ref[...] == iota((U, U * 4), 0)).astype(BF16)
    row = iota((3 * PART, 2 * n), 0)
    source = (row % PART) // 4 + (8 - SHIFT) + jnp.where(row // PART == 1, n, 0)
    spread = (iota((3 * PART, 2 * n), 1) == source).astype(BF16)
    mask = iota((3 * PART, U * 4), 0) % 4 == iota((3 * PART, U * 4), 1) % 4
    for j in range(2):
        ordered = jnp.dot(green[:, j * U : (j + 1) * U], pick, preferred_element_type=F32)
        wide = jnp.dot(spread, ordered.astype(BF16), preferred_element_type=F32)
        out_ref[j * U * 4 : (j + 1) * U * 4, :] = jnp.where(mask, wide, 0.0).T.astype(BF16)


def row_factors(from_x, rows_t, order):
    return pl.pallas_call(
        rows_kernel,
        in_specs=[VMEM] * 3,
        out_specs=VMEM,
        out_shape=jax.ShapeDtypeStruct((2 * U * 4, 3 * PART), BF16),
        compiler_params=params(4),
        name="row_factors",
    )(from_x, rows_t, order)


def focal_kernel(factor_ref, keep_ref, got_ref, b_ref, c_ref, d_ref, out_ref):
    t = ((keep_ref[0] + got_ref[0]) + b_ref[...]) + (c_ref[...] + d_ref[...])
    hi, lo = split2(t)
    out = jnp.dot(
        factor_ref[...], jnp.concatenate([hi, hi, lo], axis=0), preferred_element_type=F32
    )
    n = U * 4
    sign = jnp.where(iota((1, 128), 1) < V, -1.0, 1.0)
    out_ref[...] = (out[:n] + sign * pltpu.roll(out[n:], V, 1)).reshape(out_ref.shape)


def focal_share(factors, keep, got, b, c, d):
    return pl.pallas_call(
        focal_kernel,
        in_specs=[VMEM] * 6,
        out_specs=VMEM,
        out_shape=jax.ShapeDtypeStruct((U // 2, 8, 128), F32),
        compiler_params=params(4),
        name="focal_share",
    )(factors, keep, got, b, c, d)


def total_kernel(x_ref, out_ref):
    s = jnp.sum(x_ref[...], axis=0)
    for u in range(2):
        for k in range(2):
            for p in range(4):
                at = (k * 4 + p) * V
                row = u * 4 + p
                out_ref[0, u : u + 1, at : at + V] = s[row : row + 1, k * V : (k + 1) * V]


def total(parts):
    return pl.pallas_call(
        total_kernel,
        in_specs=[VMEM],
        out_specs=VMEM,
        out_shape=jax.ShapeDtypeStruct((1, 2, 8 * V), F32),
        compiler_params=params(4),
        name="total",
    )(parts)


def conv_weights(conv_table):
    return jnp.concatenate(
        [jnp.pad(conv_table, ((0, 0), (0, SLOT))), jnp.pad(conv_table, ((0, 0), (SLOT, 0)))], axis=0
    )


def mix_weights(mix_weight):
    w = mix_weight * jnp.asarray(0.5, BF16)
    return jnp.concatenate(
        [jnp.pad(w, ((0, 0), (0, HID))), jnp.pad(w, ((0, 0), (HID, 0)))], axis=0
    )


def decoder_weights(decoder):
    d = decoder * jnp.asarray(0.5, BF16)
    d = d[::-1].reshape(KS, KS, 2, 4, HID).transpose(1, 2, 3, 0, 4)
    rows = [
        jnp.pad(d, ((0, 0), (0, 0), (0, 0), (r, BLOCK - 1 - r), (0, 0))) for r in range(BLOCK)
    ]
    return jnp.stack(rows, axis=2).reshape(KS * CH * BLOCK, 2 * BLOCK * HID)


def bias_column(bias):
    return jnp.concatenate([bias, bias])[:, None]


def on_device(
    levels, conv_table, conv_bias, mix_weight, mix_bias, decoder, green_rows, green_cols, focal_order
):
    count_px = lax.axis_size("px")
    count_py = lax.axis_size("py")
    rows_t = jnp.swapaxes(green_rows, 2, 3)
    next_x = [(i, (i + 1) % count_px) for i in range(count_px)]
    next_y = [(i, (i + 1) % count_py) for i in range(count_py)]
    conv_w = conv_weights(conv_table)
    mix_w = mix_weights(mix_weight)
    dec_w = decoder_weights(decoder)
    conv_b = bias_column(conv_bias)
    mix_b = bias_column(mix_bias)
    order = jnp.broadcast_to(focal_order[:, None], (U, 4)).reshape(1, U * 4)
    conv_w, conv_b, mix_w, mix_b, dec_w, order = lax.optimization_barrier(
        (conv_w, conv_b, mix_w, mix_b, dec_w, order)
    )

    to_x, to_y = pack(levels, rows_t, green_cols)
    from_x = lax.ppermute(to_x, "px", next_x)
    from_y = lax.ppermute(to_y, "py", next_y)
    feat, hi, lo = inner(levels, conv_w, conv_b, mix_w, mix_b, green_cols)
    from_x, from_y, feat = lax.optimization_barrier((from_x, from_y, feat))
    from_d = lax.ppermute(from_x, "py", next_y)
    feat = outer(levels, from_x, from_y, conv_w, conv_b, mix_w, mix_b, feat)
    send, nf, edge, _ = field(
        levels, from_x, from_y, from_d, conv_w, conv_b, mix_w, mix_b, dec_w, hi, lo, feat
    )

    def swap(x, mask):
        return lax.ppermute(x, "py", [(i, i ^ mask) for i in range(count_py)])

    got = swap(send, 1)
    keep = keep_planes(hi, lo, nf, edge, from_y, 1, 3)
    b, c, d = (swap(keep[i - 1] + got[i], 2 * i) for i in (1, 2, 3))
    keep = keep_planes(hi, lo, nf, edge, from_y, 0, 1)
    factors = row_factors(from_x, rows_t, order)
    share = focal_share(factors, keep, got, b, c, d)
    return total(lax.all_to_all(share, "px", 0, 0))


def solution(mesh):
    return jax.shard_map(
        on_device,
        mesh=mesh,
        in_specs=(
            P("px", "py"),
            P(),
            P(),
            P(),
            P(),
            P(),
            P(None, None, None, "px"),
            P(None, None, None, "py"),
            P(),
        ),
        out_specs=P("py", "px", None),
        check_vma=False,
    )
```

```python
import jax
import jax.numpy as jnp
from jax import lax
from jax.experimental import pallas as pl
from jax.experimental.pallas import tpu as pltpu
from jax.sharding import PartitionSpec as P

HIGH = lax.Precision.HIGHEST
F32 = jnp.float32
BF16 = jnp.bfloat16
NT = (((1,), (1,)), ((), ()))
TN = (((0,), (0,)), ((), ()))

ROWS = 16
COLS = 1024
HID = 64
LEVELS = 16
CH = 8
KS = 5
Z = 8
U = 64
V = 64
HALO = 4
SHIFT = 5
PILLAR_ROWS = ROWS + KS - 1
SLOT = 3 * LEVELS
WINDOW = 4 * SLOT
BLOCK = 4
REL_ORDER = (0, 2, 4, 6, 1, 3, 5, 7)
PART = ROWS * CH // 2
HALF = BLOCK * CH // 2
VMEM = pl.BlockSpec(memory_space=pltpu.VMEM)
HBM = pl.BlockSpec(memory_space=pltpu.HBM)


def params(mib):
    return pltpu.CompilerParams(vmem_limit_bytes=mib << 20)

GELU_A = 0.7978845608028654
GELU_B = GELU_A * 0.044715


def iota(shape, dim):
    return lax.broadcasted_iota(jnp.int32, shape, dim)


def twice_gelu(x):
    return x + x * jnp.tanh(x * (GELU_A + GELU_B * (x * x)))


def split2(x):
    hi = x.astype(BF16)
    return hi, (x - hi.astype(F32)).astype(BF16)


def hbm(x):
    return pltpu.with_memory_space_constraint(x, pltpu.HBM)


def pack_kernel(lev_hbm, rows_hbm, to_x_ref, to_y_ref, lev_ref, tile_ref, rows_ref, sems):
    z = lax.axis_index("py")
    copies = [
        pltpu.make_async_copy(lev_hbm.at[pl.ds(8, 8), :], lev_ref, sems.at[0]),
        pltpu.make_async_copy(lev_hbm.at[:, pl.ds(COLS - 128, 128)], tile_ref, sems.at[1]),
        pltpu.make_async_copy(rows_hbm.at[z], rows_ref, sems.at[2]),
    ]
    for copy in copies:
        copy.start()
    for copy in copies:
        copy.wait()
    to_x_ref[:, :COLS] = lev_ref[...].astype(F32)
    to_x_ref[:, COLS:] = jnp.concatenate([rows_ref[0, 8:, :], rows_ref[1, 8:, :]], axis=1)
    to_y_ref[...] = tile_ref[...].astype(F32)


def pack(levels, rows_t):
    return pl.pallas_call(
        pack_kernel,
        in_specs=[HBM] * 2,
        out_specs=[VMEM] * 2,
        out_shape=[
            jax.ShapeDtypeStruct((8, COLS + 128), F32),
            jax.ShapeDtypeStruct((ROWS, 128), F32),
        ],
        scratch_shapes=[
            pltpu.VMEM((8, COLS), jnp.int32),
            pltpu.VMEM((ROWS, 128), jnp.int32),
            pltpu.VMEM((2, ROWS, U), F32),
            pltpu.SemaphoreType.DMA((3,)),
        ],
        compiler_params=params(4),
        name="pack",
    )(hbm(levels), hbm(rows_t))


def relay_kernel(from_x_ref, green_ref, out_ref):
    out_ref[:8, :] = from_x_ref[:, COLS - 128 : COLS]
    out_ref[8:, :] = green_ref[...]


def relay(from_x, green):
    return pl.pallas_call(
        relay_kernel,
        in_specs=[VMEM] * 2,
        out_specs=VMEM,
        out_shape=jax.ShapeDtypeStruct((8 + Z * HALO, 128), F32),
        compiler_params=params(4),
        name="relay",
    )(from_x, green)


def one_hot(row, level_ids):
    row = jnp.broadcast_to(row, level_ids.shape)
    return jnp.where(row == level_ids, 1.0, 0.0).astype(BF16)


def features(window, conv, conv_bias, mix, mix_bias):
    pre = jnp.dot(conv, window, preferred_element_type=F32) + conv_bias
    hidden = twice_gelu(pre).astype(BF16)
    mixed = jnp.dot(mix, hidden, preferred_element_type=F32) + mix_bias
    return twice_gelu(mixed).astype(BF16)


def inner_kernel(
    lev_ref, conv_ref, cb_ref, mix_ref, mb_ref, cols_hbm, feat_ref, hi_ref, lo_ref, green_ref,
    ext_ref, hot_ref, cols_ref, sems,
):
    z = lax.axis_index("py")
    copies = [
        pltpu.make_async_copy(cols_hbm.at[z ^ REL_ORDER[g]], cols_ref.at[g], sems.at[g])
        for g in range(Z)
    ]
    for copy in copies:
        copy.start()
    wide = COLS - 128
    lev = lev_ref[...].astype(F32)
    for b in range(3):
        ext_ref[b] = pltpu.roll(lev, 3 - b, 1)[:, 128:]
    level_ids = iota((LEVELS, wide), 0).astype(F32)

    def make_hot(q, _):
        for b in range(3):
            hot_ref[pl.ds(q * SLOT + b * LEVELS, LEVELS), :] = one_hot(
                ext_ref[b, pl.ds(q, 1), :], level_ids
            )
        return 0

    lax.fori_loop(0, ROWS - 2, make_hot, 0, unroll=2)
    conv_bias = jnp.broadcast_to(cb_ref[...], (2 * HID, wide))
    mix_bias = jnp.broadcast_to(mb_ref[...], (2 * HID, wide))
    for i in range(ROWS // 2 - 2):
        at = (8 + 2 * i) * HID
        feat_ref[at : at + 2 * HID, 128:] = features(
            hot_ref[i * 2 * SLOT : i * 2 * SLOT + WINDOW, :],
            conv_ref[...], conv_bias, mix_ref[...], mix_bias,
        )
    for copy in copies:
        copy.wait()

    def split(g, _):
        hi_ref[g], lo_ref[g] = split2(cols_ref[g].reshape(2 * V, COLS))
        return 0

    lax.fori_loop(0, Z, split, 0)
    for g in range(Z):
        edge = cols_ref[g, :, :, COLS - 128 :].reshape(2 * V, 128).T
        green_ref[HALO * g : HALO * (g + 1), :] = edge[128 - HALO :, :]


def inner(levels, conv_w, conv_b, mix_w, mix_b, green_cols):
    wide = COLS - 128
    return pl.pallas_call(
        inner_kernel,
        in_specs=[VMEM] * 5 + [HBM],
        out_specs=[VMEM] * 4,
        out_shape=[
            jax.ShapeDtypeStruct((PILLAR_ROWS * HID, COLS), BF16),
            jax.ShapeDtypeStruct((Z, 2 * V, COLS), BF16),
            jax.ShapeDtypeStruct((Z, 2 * V, COLS), BF16),
            jax.ShapeDtypeStruct((Z * HALO, 128), F32),
        ],
        scratch_shapes=[
            pltpu.VMEM((3, ROWS, wide), F32),
            pltpu.VMEM(((ROWS - 2) * SLOT, wide), BF16),
            pltpu.VMEM((Z, 2, V, COLS), F32),
            pltpu.SemaphoreType.DMA((Z,)),
        ],
        compiler_params=params(16),
        name="inner",
    )(levels, conv_w, conv_b, mix_w, mix_b, hbm(green_cols))


def tile_windows(left, tile, first_y, ext_ref):
    ext = jnp.concatenate([left, tile], axis=1)
    lane = iota(tile.shape, 1)
    for b in range(3):
        window = pltpu.roll(ext, 3 - b, 1)[:, 128:]
        if b != 1:
            window = jnp.where(first_y & (lane == (2 if b == 0 else 1)), -1.0, window)
        ext_ref[b] = window


def near_field(i, dec, feat_ref, nf_ref, edge_ref, first_y):
    lane = iota((1, COLS), 1)
    near = iota((1, 128), 1)
    at = i * BLOCK * HID
    taps = jnp.dot(dec, feat_ref[at : at + 2 * BLOCK * HID, :], preferred_element_type=F32)
    acc = jnp.zeros((2 * HALF, COLS), F32)
    edge = jnp.zeros((2 * HALF, 128), F32)
    for s in range(KS):
        part = taps[2 * HALF * s : 2 * HALF * (s + 1), :]
        k = KS - 1 - s
        ok = (lane < COLS - k) & ((lane + k >= 2) | jnp.logical_not(first_y))
        moved = part if k == 0 else pltpu.roll(part, COLS - k, 1)
        acc = acc + jnp.where(ok, moved, 0.0)
        ok = (near >= s) & (near < HALO) & ((near - s < 2) | jnp.logical_not(first_y))
        part = part[:, :128]
        moved = part if s == 0 else pltpu.roll(part, s, 1)
        edge = edge + jnp.where(ok, moved, 0.0)
    for part, values in enumerate(split2(acc)):
        for k in range(2):
            at = (2 * part + k) * PART + i * HALF
            nf_ref[at : at + HALF, :] = values[k * HALF : (k + 1) * HALF]
    for k in range(2):
        at = k * PART + i * HALF
        edge_ref[at : at + HALF, :] = edge[k * HALF : (k + 1) * HALF]


def middle_kernel(
    lev_ref, from_y_ref, conv_ref, cb_ref, mix_ref, mb_ref, dec_ref, _,
    nf_ref, edge_ref, feat_ref, ext_ref, hot_ref,
):
    first_y = lax.axis_index("py") == 0
    tile_windows(from_y_ref[...], lev_ref[:, :128].astype(F32), first_y, ext_ref)
    level_ids = iota((LEVELS, 128), 0).astype(F32)
    for q in range(ROWS - 2):
        for b in range(3):
            row = one_hot(ext_ref[b, q : q + 1, :], level_ids)
            for t in range(6):
                if 0 <= q - 2 * t < 4:
                    at = (q - 2 * t) * SLOT + b * LEVELS
                    hot_ref[at : at + LEVELS, t * 128 : (t + 1) * 128] = row
    tiles = features(hot_ref[...], conv_ref[...], cb_ref[...], mix_ref[...], mb_ref[...])
    for t in range(6):
        at = (8 + 2 * t) * HID
        feat_ref[at : at + 2 * HID, :128] = tiles[:, t * 128 : (t + 1) * 128]
    for i in (2, 3):
        near_field(i, dec_ref[...], feat_ref, nf_ref, edge_ref, first_y)


def middle(levels, from_y, conv_w, conv_b, mix_w, mix_b, dec_w, feat):
    return pl.pallas_call(
        middle_kernel,
        in_specs=[VMEM] * 8,
        out_specs=[VMEM] * 3,
        out_shape=[
            jax.ShapeDtypeStruct((4 * PART, COLS), BF16),
            jax.ShapeDtypeStruct((2 * PART, 128), F32),
            jax.ShapeDtypeStruct(feat.shape, BF16),
        ],
        input_output_aliases={7: 2},
        scratch_shapes=[pltpu.VMEM((3, ROWS, 128), F32), pltpu.VMEM((WINDOW, 768), BF16)],
        compiler_params=params(8),
        name="middle",
    )(levels, from_y, conv_w, conv_b, mix_w, mix_b, dec_w, feat)


def outer_kernel(
    lev_ref, from_x_ref, conv_ref, cb_ref, mix_ref, mb_ref, _, feat_ref, ext_ref, hot_ref
):
    first_x = lax.axis_index("px") == 0
    ext = jnp.concatenate([from_x_ref[:, :COLS], lev_ref[:8, :].astype(F32)], axis=0)
    for b in range(3):
        ext_ref[b] = pltpu.roll(ext, 3 - b, 1)[:, 128:]
    wide = COLS - 128
    level_ids = iota((LEVELS, wide), 0).astype(F32)
    for e in range(10):
        for b in range(3):
            at = e * SLOT + b * LEVELS
            hot_ref[at : at + LEVELS, :] = one_hot(ext_ref[b, e : e + 1, :], level_ids)
    conv_bias = jnp.broadcast_to(cb_ref[...], (2 * HID, wide))
    mix_bias = jnp.broadcast_to(mb_ref[...], (2 * HID, wide))
    for w in range(4):
        at = 2 * w * HID
        conv = cut_conv(conv_ref[...], first_x) if w == 3 else conv_ref[...]
        feat_ref[at : at + 2 * HID, 128:] = features(
            hot_ref[2 * w * SLOT : 2 * w * SLOT + WINDOW, :],
            conv, conv_bias, mix_ref[...], mix_bias,
        )


def cut_conv(conv, first_x):
    slot = iota((2 * HID, WINDOW), 1) // SLOT
    row = iota((2 * HID, WINDOW), 0) // HID
    keep = jnp.where(first_x & (slot + row == 2) & (slot > 0), 0.0, 1.0)
    return conv * keep.astype(BF16)


def outer(levels, from_x, conv_w, conv_b, mix_w, mix_b, feat):
    wide = COLS - 128
    return pl.pallas_call(
        outer_kernel,
        in_specs=[VMEM] * 7,
        out_specs=VMEM,
        out_shape=jax.ShapeDtypeStruct(feat.shape, BF16),
        input_output_aliases={6: 0},
        scratch_shapes=[
            pltpu.VMEM((3, 16, wide), F32),
            pltpu.VMEM((10 * SLOT, wide), BF16),
        ],
        compiler_params=params(8),
        name="outer",
    )(levels, from_x, conv_w, conv_b, mix_w, mix_b, feat)


def column_sum(hi_ref, lo_ref, nf_ref, edge_ref, from_d_ref, out_ref, first, count):
    iy = lax.axis_index("py")
    before = (iy + lax.axis_size("py") - 1) % lax.axis_size("py")
    n = 2 * PART
    sign = jnp.where(iota((1, 128), 1) < V, -1.0, 1.0)
    hi = hi_ref[first : first + count].reshape(2 * V * count, COLS)
    lo = lo_ref[first : first + count].reshape(2 * V * count, COLS)
    both = lax.dot_general(hi, nf_ref[...], NT, preferred_element_type=F32)
    both = both[:, :n] + both[:, n:]
    both = both + lax.dot_general(lo, nf_ref[:n, :], NT, preferred_element_type=F32)
    for g in range(count):
        out = both[2 * V * g : 2 * V * (g + 1)].T
        rel = (iy ^ REL_ORDER[first + g]) ^ before
        at = 8 + HALO * (rel // 2 + 4 * (rel % 2))
        green = from_d_ref[pl.ds(at, HALO), :]
        green = jnp.concatenate([green, jnp.zeros((4, 128), F32)], axis=0)
        out = out + jnp.dot(edge_ref[:, :8], green, precision=HIGH, preferred_element_type=F32)
        out_ref[g] = out[:PART] + sign * pltpu.roll(out[PART:], V, 1)


def field_kernel(
    lev_ref, from_x_ref, from_y_ref, from_d_ref, conv_ref, cb_ref, mix_ref, mb_ref, dec_ref,
    hi_ref, lo_ref, _nf, _edge, _feat, send_ref, nf_ref, edge_ref, feat_ref, ext_ref, hot_ref,
):
    first_x = lax.axis_index("px") == 0
    first_y = lax.axis_index("py") == 0
    tile = jnp.concatenate([from_x_ref[:, :128], lev_ref[:8, :128].astype(F32)], axis=0)
    left = jnp.concatenate([from_d_ref[:8, :], from_y_ref[:8, :]], axis=0)
    tile_windows(left, tile, first_y, ext_ref)
    level_ids = iota((LEVELS, 128), 0).astype(F32)
    for w in range(4):
        for o in range(4):
            for b in range(3):
                e = 2 * w + o
                at = o * SLOT + b * LEVELS
                hot_ref[at : at + LEVELS, w * 128 : (w + 1) * 128] = one_hot(
                    ext_ref[b, e : e + 1, :], level_ids
                )
    tiles = features(
        hot_ref[:, :384], conv_ref[...], cb_ref[...], mix_ref[...], mb_ref[...]
    )
    for w in range(3):
        feat_ref[2 * w * HID : (2 * w + 2) * HID, :128] = tiles[:, w * 128 : (w + 1) * 128]
    feat_ref[6 * HID : 8 * HID, :128] = features(
        hot_ref[:, 384:], cut_conv(conv_ref[...], first_x), cb_ref[...], mix_ref[...], mb_ref[...]
    )

    shape = (KS * CH * BLOCK, 2 * BLOCK * HID)
    sample = iota(shape, 0) // 4 % BLOCK - SHIFT
    pillar = iota(shape, 1) // HID - SHIFT - 2
    for i in range(2):
        at = i * BLOCK
        apart = (sample + at >= 0) != (pillar + at >= 0)
        keep = jnp.where(first_x & apart, 0.0, 1.0)
        near_field(i, dec_ref[...] * keep.astype(BF16), feat_ref, nf_ref, edge_ref, first_y)

    column_sum(hi_ref, lo_ref, nf_ref, edge_ref, from_d_ref, send_ref, 4, 4)


def field(
    levels, from_x, from_y, from_d, conv_w, conv_b, mix_w, mix_b, dec_w, hi, lo, nf, edge, feat
):
    return pl.pallas_call(
        field_kernel,
        in_specs=[VMEM] * 14,
        out_specs=[VMEM] * 4,
        out_shape=[
            jax.ShapeDtypeStruct((4, PART, 128), F32),
            jax.ShapeDtypeStruct((4 * PART, COLS), BF16),
            jax.ShapeDtypeStruct((2 * PART, 128), F32),
            jax.ShapeDtypeStruct(feat.shape, BF16),
        ],
        input_output_aliases={11: 1, 12: 2, 13: 3},
        scratch_shapes=[
            pltpu.VMEM((3, 16, 128), F32),
            pltpu.VMEM((WINDOW, 512), BF16),
        ],
        compiler_params=params(12),
        name="field",
    )(
        levels, from_x, from_y, from_d, conv_w, conv_b, mix_w, mix_b, dec_w, hi, lo, nf, edge, feat
    )


def keep_planes(hi, lo, nf, edge, from_d, first, count):
    def keep_kernel(hi_ref, lo_ref, nf_ref, edge_ref, from_d_ref, out_ref):
        column_sum(hi_ref, lo_ref, nf_ref, edge_ref, from_d_ref, out_ref, first, count)

    return pl.pallas_call(
        keep_kernel,
        in_specs=[VMEM] * 5,
        out_specs=VMEM,
        out_shape=jax.ShapeDtypeStruct((count, PART, 128), F32),
        compiler_params=params(8),
        name="keep_planes",
    )(hi, lo, nf, edge, from_d)


def rows_kernel(from_x_ref, rows_ref, order_ref, out_ref):
    z = lax.axis_index("py")
    green = jnp.concatenate([rows_ref[z, 0], rows_ref[z, 1]], axis=1)
    green = jnp.concatenate([from_x_ref[:, COLS:], green], axis=0)
    n = ROWS + 8
    green = jnp.concatenate(split2(green), axis=0)
    pick = (order_ref[...] == iota((U, U * 4), 0)).astype(BF16)
    row = iota((3 * PART, 2 * n), 0)
    source = (row % PART) // 4 + (8 - SHIFT) + jnp.where(row // PART == 1, n, 0)
    spread = (iota((3 * PART, 2 * n), 1) == source).astype(BF16)
    mask = iota((3 * PART, U * 4), 0) % 4 == iota((3 * PART, U * 4), 1) % 4
    for j in range(2):
        ordered = jnp.dot(green[:, j * U : (j + 1) * U], pick, preferred_element_type=F32)
        wide = jnp.dot(spread, ordered.astype(BF16), preferred_element_type=F32)
        out_ref[j * U * 4 : (j + 1) * U * 4, :] = jnp.where(mask, wide, 0.0).T.astype(BF16)


def row_factors(from_x, rows_t, order):
    return pl.pallas_call(
        rows_kernel,
        in_specs=[VMEM] * 3,
        out_specs=VMEM,
        out_shape=jax.ShapeDtypeStruct((2 * U * 4, 3 * PART), BF16),
        compiler_params=params(4),
        name="row_factors",
    )(from_x, rows_t, order)


def focal_kernel(factor_ref, keep_ref, got_ref, b_ref, c_ref, d_ref, out_ref):
    t = ((keep_ref[0] + got_ref[0]) + b_ref[...]) + (c_ref[...] + d_ref[...])
    hi, lo = split2(t)
    out = jnp.dot(
        factor_ref[...], jnp.concatenate([hi, hi, lo], axis=0), preferred_element_type=F32
    )
    n = U * 4
    sign = jnp.where(iota((1, 128), 1) < V, -1.0, 1.0)
    out_ref[...] = (out[:n] + sign * pltpu.roll(out[n:], V, 1)).reshape(out_ref.shape)


def focal_share(factors, keep, got, b, c, d):
    return pl.pallas_call(
        focal_kernel,
        in_specs=[VMEM] * 6,
        out_specs=VMEM,
        out_shape=jax.ShapeDtypeStruct((U // 2, 8, 128), F32),
        compiler_params=params(4),
        name="focal_share",
    )(factors, keep, got, b, c, d)


def total_kernel(x_ref, out_ref):
    s = jnp.sum(x_ref[...], axis=0)
    for u in range(2):
        for k in range(2):
            for p in range(4):
                at = (k * 4 + p) * V
                row = u * 4 + p
                out_ref[0, u : u + 1, at : at + V] = s[row : row + 1, k * V : (k + 1) * V]


def total(parts):
    return pl.pallas_call(
        total_kernel,
        in_specs=[VMEM],
        out_specs=VMEM,
        out_shape=jax.ShapeDtypeStruct((1, 2, 8 * V), F32),
        compiler_params=params(4),
        name="total",
    )(parts)


def conv_weights(conv_table):
    return jnp.concatenate(
        [jnp.pad(conv_table, ((0, 0), (0, SLOT))), jnp.pad(conv_table, ((0, 0), (SLOT, 0)))], axis=0
    )


def mix_weights(mix_weight):
    w = mix_weight * jnp.asarray(0.5, BF16)
    return jnp.concatenate(
        [jnp.pad(w, ((0, 0), (0, HID))), jnp.pad(w, ((0, 0), (HID, 0)))], axis=0
    )


def decoder_weights(decoder):
    d = decoder * jnp.asarray(0.5, BF16)
    d = d[::-1].reshape(KS, KS, 2, 4, HID).transpose(1, 2, 3, 0, 4)
    rows = [
        jnp.pad(d, ((0, 0), (0, 0), (0, 0), (r, BLOCK - 1 - r), (0, 0))) for r in range(BLOCK)
    ]
    return jnp.stack(rows, axis=2).reshape(KS * CH * BLOCK, 2 * BLOCK * HID)


def bias_column(bias):
    return jnp.concatenate([bias, bias])[:, None]


def on_device(
    levels, conv_table, conv_bias, mix_weight, mix_bias, decoder, green_rows, green_cols, focal_order
):
    count_px = lax.axis_size("px")
    count_py = lax.axis_size("py")
    rows_t = jnp.swapaxes(green_rows, 2, 3)
    next_x = [(i, (i + 1) % count_px) for i in range(count_px)]
    next_y = [(i, (i + 1) % count_py) for i in range(count_py)]
    conv_w = conv_weights(conv_table)
    mix_w = mix_weights(mix_weight)
    dec_w = decoder_weights(decoder)
    conv_b = bias_column(conv_bias)
    mix_b = bias_column(mix_bias)
    order = jnp.broadcast_to(focal_order[:, None], (U, 4)).reshape(1, U * 4)
    conv_w, conv_b, mix_w, mix_b, dec_w, order = lax.optimization_barrier(
        (conv_w, conv_b, mix_w, mix_b, dec_w, order)
    )

    to_x, to_y = pack(levels, rows_t)
    from_x = lax.ppermute(to_x, "px", next_x)
    from_y = lax.ppermute(to_y, "py", next_y)
    feat, hi, lo, green = inner(levels, conv_w, conv_b, mix_w, mix_b, green_cols)
    from_y, feat = lax.optimization_barrier((from_y, feat))
    nf, edge, feat = middle(levels, from_y, conv_w, conv_b, mix_w, mix_b, dec_w, feat)
    from_x, feat, nf, edge = lax.optimization_barrier((from_x, feat, nf, edge))
    from_d = lax.ppermute(relay(from_x, green), "py", next_y)
    feat = outer(levels, from_x, conv_w, conv_b, mix_w, mix_b, feat)
    send, nf, edge, _ = field(
        levels, from_x, from_y, from_d, conv_w, conv_b, mix_w, mix_b, dec_w, hi, lo, nf, edge, feat
    )

    def swap(x, mask):
        return lax.ppermute(x, "py", [(i, i ^ mask) for i in range(count_py)])

    got = swap(send, 1)
    keep = keep_planes(hi, lo, nf, edge, from_d, 1, 3)
    b, c, d = (swap(keep[i - 1] + got[i], 2 * i) for i in (1, 2, 3))
    keep = keep_planes(hi, lo, nf, edge, from_d, 0, 1)
    factors = row_factors(from_x, rows_t, order)
    share = focal_share(factors, keep, got, b, c, d)
    return total(lax.all_to_all(share, "px", 0, 0))


def solution(mesh):
    return jax.shard_map(
        on_device,
        mesh=mesh,
        in_specs=(
            P("px", "py"),
            P(),
            P(),
            P(),
            P(),
            P(),
            P(None, None, None, "px"),
            P(None, None, None, "py"),
            P(),
        ),
        out_specs=P("py", "px", None),
        check_vma=False,
    )
```

```python
import jax
import jax.numpy as jnp
from jax import lax
from jax.experimental import pallas as pl
from jax.experimental.pallas import tpu as pltpu
from jax.sharding import PartitionSpec as P

HIGH = lax.Precision.HIGHEST
F32 = jnp.float32
BF16 = jnp.bfloat16
NT = (((1,), (1,)), ((), ()))
TN = (((0,), (0,)), ((), ()))

ROWS = 16
COLS = 1024
HID = 64
LEVELS = 16
CH = 8
KS = 5
Z = 8
U = 64
V = 64
HALO = 4
SHIFT = 5
PILLAR_ROWS = ROWS + KS - 1
SLOT = 3 * LEVELS
WINDOW = 4 * SLOT
BLOCK = 4
REL_ORDER = (0, 2, 4, 6, 1, 3, 5, 7)
PART = ROWS * CH // 2
HALF = BLOCK * CH // 2
VMEM = pl.BlockSpec(memory_space=pltpu.VMEM)
HBM = pl.BlockSpec(memory_space=pltpu.HBM)


def params(mib):
    return pltpu.CompilerParams(vmem_limit_bytes=mib << 20)

GELU_A = 0.7978845608028654
GELU_B = GELU_A * 0.044715


def iota(shape, dim):
    return lax.broadcasted_iota(jnp.int32, shape, dim)


def twice_gelu(x):
    return x + x * jnp.tanh(x * (GELU_A + GELU_B * (x * x)))


def split2(x):
    hi = x.astype(BF16)
    return hi, (x - hi.astype(F32)).astype(BF16)


def hbm(x):
    return pltpu.with_memory_space_constraint(x, pltpu.HBM)


def pack_kernel(lev_hbm, rows_hbm, to_x_ref, to_y_ref, lev_ref, tile_ref, rows_ref, sems):
    z = lax.axis_index("py")
    copies = [
        pltpu.make_async_copy(lev_hbm.at[pl.ds(8, 8), :], lev_ref, sems.at[0]),
        pltpu.make_async_copy(lev_hbm.at[:, pl.ds(COLS - 128, 128)], tile_ref, sems.at[1]),
        pltpu.make_async_copy(rows_hbm.at[z], rows_ref, sems.at[2]),
    ]
    for copy in copies:
        copy.start()
    for copy in copies:
        copy.wait()
    to_x_ref[:, :COLS] = lev_ref[...].astype(F32)
    to_x_ref[:, COLS:] = jnp.concatenate([rows_ref[0, 8:, :], rows_ref[1, 8:, :]], axis=1)
    to_y_ref[...] = tile_ref[...].astype(F32)


def pack(levels, rows_t):
    return pl.pallas_call(
        pack_kernel,
        in_specs=[HBM] * 2,
        out_specs=[VMEM] * 2,
        out_shape=[
            jax.ShapeDtypeStruct((8, COLS + 128), F32),
            jax.ShapeDtypeStruct((ROWS, 128), F32),
        ],
        scratch_shapes=[
            pltpu.VMEM((8, COLS), jnp.int32),
            pltpu.VMEM((ROWS, 128), jnp.int32),
            pltpu.VMEM((2, ROWS, U), F32),
            pltpu.SemaphoreType.DMA((3,)),
        ],
        compiler_params=params(4),
        name="pack",
    )(hbm(levels), hbm(rows_t))


def relay_kernel(from_x_ref, green_ref, out_ref):
    out_ref[:8, :] = from_x_ref[:, COLS - 128 : COLS]
    out_ref[8:, :] = green_ref[...]


def relay(from_x, green):
    return pl.pallas_call(
        relay_kernel,
        in_specs=[VMEM] * 2,
        out_specs=VMEM,
        out_shape=jax.ShapeDtypeStruct((8 + Z * HALO, 128), F32),
        compiler_params=params(4),
        name="relay",
    )(from_x, green)


def one_hot(row, level_ids):
    row = jnp.broadcast_to(row, level_ids.shape)
    return jnp.where(row == level_ids, 1.0, 0.0).astype(BF16)


def features(window, conv, conv_bias, mix, mix_bias):
    pre = jnp.dot(conv, window, preferred_element_type=F32) + conv_bias
    hidden = twice_gelu(pre).astype(BF16)
    mixed = jnp.dot(mix, hidden, preferred_element_type=F32) + mix_bias
    return twice_gelu(mixed).astype(BF16)


def lanes_from(x, count, offset):
    shape = (x.shape[1], count)
    move = (iota(shape, 1) == iota(shape, 0) + offset).astype(BF16)
    return jnp.dot(x, move, preferred_element_type=F32)


def bias_column(row):
    shape = (2 * HID, HID)
    own = iota(shape, 1) == iota(shape, 0) % HID
    return jnp.sum(jnp.where(own, row, 0.0), axis=1, keepdims=True)


def lay_out_decoder(dec_ref, out_ref):
    n = KS * CH * BLOCK
    row = iota((n, n), 0)
    source = row // 4 % BLOCK * (KS * CH) + row // (4 * BLOCK) * 4 + row % 4
    move = (iota((n, n), 1) == source).astype(BF16)
    dec = dec_ref[...].astype(F32)
    none = jnp.zeros((KS * CH, HID), F32)

    def column(pillar):
        taps = [r - pillar + KS - 1 for r in range(BLOCK)]
        return jnp.concatenate([dec[t] if 0 <= t < KS else none for t in taps], axis=0)

    for i in range(BLOCK):
        pair = jnp.concatenate([column(2 * i), column(2 * i + 1)], axis=1).astype(BF16)
        wide = jnp.dot(move, pair, preferred_element_type=F32)
        out_ref[:, 2 * i * HID : (2 * i + 2) * HID] = (0.5 * wide).astype(BF16)


def inner_kernel(
    lev_hbm, table_hbm, cb_hbm, mix_hbm, mb_hbm, dec_hbm, cols_hbm,
    feat_ref, hi_ref, lo_ref, green_ref, conv_ref, cb_ref, mixer_ref, mb_ref, dec_ref,
    ext_ref, hot_ref, cols_ref, lev_ref, table_ref, cbr_ref, mix_ref, mbr_ref, raw_ref, sems,
):
    z = lax.axis_index("py")
    small = [
        pltpu.make_async_copy(lev_hbm, lev_ref, sems.at[Z]),
        pltpu.make_async_copy(table_hbm, table_ref, sems.at[Z + 1]),
        pltpu.make_async_copy(cb_hbm, cbr_ref, sems.at[Z + 2]),
        pltpu.make_async_copy(mix_hbm, mix_ref, sems.at[Z + 3]),
        pltpu.make_async_copy(mb_hbm, mbr_ref, sems.at[Z + 4]),
        pltpu.make_async_copy(dec_hbm, raw_ref, sems.at[Z + 5]),
    ]
    copies = [
        pltpu.make_async_copy(cols_hbm.at[z ^ REL_ORDER[g]], cols_ref.at[g], sems.at[g])
        for g in range(Z)
    ]
    for copy in small + copies:
        copy.start()
    for copy in small:
        copy.wait()
    conv_ref[:HID, :] = lanes_from(table_ref[...], WINDOW, 0).astype(BF16)
    conv_ref[HID:, :] = lanes_from(table_ref[...], WINDOW, SLOT).astype(BF16)
    mixer_ref[:HID, :] = (0.5 * lanes_from(mix_ref[...], 2 * HID, 0)).astype(BF16)
    mixer_ref[HID:, :] = (0.5 * lanes_from(mix_ref[...], 2 * HID, HID)).astype(BF16)
    cb_ref[...] = bias_column(cbr_ref[...])
    mb_ref[...] = bias_column(mbr_ref[...])
    lay_out_decoder(raw_ref, dec_ref)
    wide = COLS - 128
    lev = lev_ref[...].astype(F32)
    for b in range(3):
        ext_ref[b] = pltpu.roll(lev, 3 - b, 1)[:, 128:]
    level_ids = iota((LEVELS, wide), 0).astype(F32)

    def make_hot(q, _):
        for b in range(3):
            hot_ref[pl.ds(q * SLOT + b * LEVELS, LEVELS), :] = one_hot(
                ext_ref[b, pl.ds(q, 1), :], level_ids
            )
        return 0

    lax.fori_loop(0, ROWS - 2, make_hot, 0, unroll=2)
    conv_bias = jnp.broadcast_to(cb_ref[...], (2 * HID, wide))
    mix_bias = jnp.broadcast_to(mb_ref[...], (2 * HID, wide))
    for i in range(ROWS // 2 - 2):
        at = (8 + 2 * i) * HID
        feat_ref[at : at + 2 * HID, 128:] = features(
            hot_ref[i * 2 * SLOT : i * 2 * SLOT + WINDOW, :],
            conv_ref[...], conv_bias, mixer_ref[...], mix_bias,
        )
    for copy in copies:
        copy.wait()

    def split(g, _):
        hi_ref[g], lo_ref[g] = split2(cols_ref[g].reshape(2 * V, COLS))
        return 0

    lax.fori_loop(0, Z, split, 0)
    for g in range(Z):
        edge = cols_ref[g, :, :, COLS - 128 :].reshape(2 * V, 128).T
        green_ref[HALO * g : HALO * (g + 1), :] = edge[128 - HALO :, :]


def inner(levels, table, conv_bias, mix, mix_bias, decoder, green_cols):
    wide = COLS - 128
    return pl.pallas_call(
        inner_kernel,
        in_specs=[HBM] * 7,
        out_specs=[VMEM] * 9,
        out_shape=[
            jax.ShapeDtypeStruct((PILLAR_ROWS * HID, COLS), BF16),
            jax.ShapeDtypeStruct((Z, 2 * V, COLS), BF16),
            jax.ShapeDtypeStruct((Z, 2 * V, COLS), BF16),
            jax.ShapeDtypeStruct((Z * HALO, 128), F32),
            jax.ShapeDtypeStruct((2 * HID, WINDOW), BF16),
            jax.ShapeDtypeStruct((2 * HID, 1), F32),
            jax.ShapeDtypeStruct((2 * HID, 2 * HID), BF16),
            jax.ShapeDtypeStruct((2 * HID, 1), F32),
            jax.ShapeDtypeStruct((KS * CH * BLOCK, 2 * BLOCK * HID), BF16),
        ],
        scratch_shapes=[
            pltpu.VMEM((3, ROWS, wide), F32),
            pltpu.VMEM(((ROWS - 2) * SLOT, wide), BF16),
            pltpu.VMEM((Z, 2, V, COLS), F32),
            pltpu.VMEM((ROWS, COLS), jnp.int32),
            pltpu.VMEM(table.shape, BF16),
            pltpu.VMEM((1, HID), F32),
            pltpu.VMEM((HID, HID), BF16),
            pltpu.VMEM((1, HID), F32),
            pltpu.VMEM(decoder.shape, BF16),
            pltpu.SemaphoreType.DMA((Z + 6,)),
        ],
        compiler_params=params(16),
        name="inner",
    )(*map(hbm, (
        levels, table, conv_bias.reshape(1, HID), mix, mix_bias.reshape(1, HID), decoder, green_cols,
    )))


def tile_windows(left, tile, first_y, ext_ref):
    ext = jnp.concatenate([left, tile], axis=1)
    lane = iota(tile.shape, 1)
    for b in range(3):
        window = pltpu.roll(ext, 3 - b, 1)[:, 128:]
        if b != 1:
            window = jnp.where(first_y & (lane == (2 if b == 0 else 1)), -1.0, window)
        ext_ref[b] = window


def near_field(i, dec, feat_ref, nf_ref, edge_ref, first_y):
    lane = iota((1, COLS), 1)
    near = iota((1, 128), 1)
    at = i * BLOCK * HID
    taps = jnp.dot(dec, feat_ref[at : at + 2 * BLOCK * HID, :], preferred_element_type=F32)
    acc = jnp.zeros((2 * HALF, COLS), F32)
    edge = jnp.zeros((2 * HALF, 128), F32)
    for s in range(KS):
        part = taps[2 * HALF * s : 2 * HALF * (s + 1), :]
        k = KS - 1 - s
        ok = (lane < COLS - k) & ((lane + k >= 2) | jnp.logical_not(first_y))
        moved = part if k == 0 else pltpu.roll(part, COLS - k, 1)
        acc = acc + jnp.where(ok, moved, 0.0)
        ok = (near >= s) & (near < HALO) & ((near - s < 2) | jnp.logical_not(first_y))
        part = part[:, :128]
        moved = part if s == 0 else pltpu.roll(part, s, 1)
        edge = edge + jnp.where(ok, moved, 0.0)
    for part, values in enumerate(split2(acc)):
        for k in range(2):
            at = (2 * part + k) * PART + i * HALF
            nf_ref[at : at + HALF, :] = values[k * HALF : (k + 1) * HALF]
    for k in range(2):
        at = k * PART + i * HALF
        edge_ref[at : at + HALF, :] = edge[k * HALF : (k + 1) * HALF]


def middle_kernel(
    lev_ref, from_y_ref, conv_ref, cb_ref, mix_ref, mb_ref, dec_ref, _,
    nf_ref, edge_ref, feat_ref, ext_ref, hot_ref,
):
    first_y = lax.axis_index("py") == 0
    tile_windows(from_y_ref[...], lev_ref[:, :128].astype(F32), first_y, ext_ref)
    level_ids = iota((LEVELS, 128), 0).astype(F32)
    for q in range(ROWS - 2):
        for b in range(3):
            row = one_hot(ext_ref[b, q : q + 1, :], level_ids)
            for t in range(6):
                if 0 <= q - 2 * t < 4:
                    at = (q - 2 * t) * SLOT + b * LEVELS
                    hot_ref[at : at + LEVELS, t * 128 : (t + 1) * 128] = row
    tiles = features(hot_ref[...], conv_ref[...], cb_ref[...], mix_ref[...], mb_ref[...])
    for t in range(6):
        at = (8 + 2 * t) * HID
        feat_ref[at : at + 2 * HID, :128] = tiles[:, t * 128 : (t + 1) * 128]
    for i in (2, 3):
        near_field(i, dec_ref[...], feat_ref, nf_ref, edge_ref, first_y)


def middle(levels, from_y, conv_w, conv_b, mix_w, mix_b, dec_w, feat):
    return pl.pallas_call(
        middle_kernel,
        in_specs=[VMEM] * 8,
        out_specs=[VMEM] * 3,
        out_shape=[
            jax.ShapeDtypeStruct((4 * PART, COLS), BF16),
            jax.ShapeDtypeStruct((2 * PART, 128), F32),
            jax.ShapeDtypeStruct(feat.shape, BF16),
        ],
        input_output_aliases={7: 2},
        scratch_shapes=[pltpu.VMEM((3, ROWS, 128), F32), pltpu.VMEM((WINDOW, 768), BF16)],
        compiler_params=params(8),
        name="middle",
    )(levels, from_y, conv_w, conv_b, mix_w, mix_b, dec_w, feat)


def outer_kernel(
    lev_ref, from_x_ref, conv_ref, cb_ref, mix_ref, mb_ref, _, feat_ref, ext_ref, hot_ref
):
    first_x = lax.axis_index("px") == 0
    ext = jnp.concatenate([from_x_ref[:, :COLS], lev_ref[:8, :].astype(F32)], axis=0)
    for b in range(3):
        ext_ref[b] = pltpu.roll(ext, 3 - b, 1)[:, 128:]
    wide = COLS - 128
    level_ids = iota((LEVELS, wide), 0).astype(F32)
    for e in range(10):
        for b in range(3):
            at = e * SLOT + b * LEVELS
            hot_ref[at : at + LEVELS, :] = one_hot(ext_ref[b, e : e + 1, :], level_ids)
    conv_bias = jnp.broadcast_to(cb_ref[...], (2 * HID, wide))
    mix_bias = jnp.broadcast_to(mb_ref[...], (2 * HID, wide))
    for w in range(4):
        at = 2 * w * HID
        conv = cut_conv(conv_ref[...], first_x) if w == 3 else conv_ref[...]
        feat_ref[at : at + 2 * HID, 128:] = features(
            hot_ref[2 * w * SLOT : 2 * w * SLOT + WINDOW, :],
            conv, conv_bias, mix_ref[...], mix_bias,
        )


def cut_conv(conv, first_x):
    slot = iota((2 * HID, WINDOW), 1) // SLOT
    row = iota((2 * HID, WINDOW), 0) // HID
    keep = jnp.where(first_x & (slot + row == 2) & (slot > 0), 0.0, 1.0)
    return conv * keep.astype(BF16)


def outer(levels, from_x, conv_w, conv_b, mix_w, mix_b, feat):
    wide = COLS - 128
    return pl.pallas_call(
        outer_kernel,
        in_specs=[VMEM] * 7,
        out_specs=VMEM,
        out_shape=jax.ShapeDtypeStruct(feat.shape, BF16),
        input_output_aliases={6: 0},
        scratch_shapes=[
            pltpu.VMEM((3, 16, wide), F32),
            pltpu.VMEM((10 * SLOT, wide), BF16),
        ],
        compiler_params=params(8),
        name="outer",
    )(levels, from_x, conv_w, conv_b, mix_w, mix_b, feat)


def column_sum(hi_ref, lo_ref, nf_ref, edge_ref, from_d_ref, out_ref, first, count):
    iy = lax.axis_index("py")
    before = (iy + lax.axis_size("py") - 1) % lax.axis_size("py")
    n = 2 * PART
    sign = jnp.where(iota((1, 128), 1) < V, -1.0, 1.0)
    hi = hi_ref[first : first + count].reshape(2 * V * count, COLS)
    lo = lo_ref[first : first + count].reshape(2 * V * count, COLS)
    both = lax.dot_general(hi, nf_ref[...], NT, preferred_element_type=F32)
    both = both[:, :n] + both[:, n:]
    both = both + lax.dot_general(lo, nf_ref[:n, :], NT, preferred_element_type=F32)
    for g in range(count):
        out = both[2 * V * g : 2 * V * (g + 1)].T
        rel = (iy ^ REL_ORDER[first + g]) ^ before
        at = 8 + HALO * (rel // 2 + 4 * (rel % 2))
        green = from_d_ref[pl.ds(at, HALO), :]
        green = jnp.concatenate([green, jnp.zeros((4, 128), F32)], axis=0)
        out = out + jnp.dot(edge_ref[:, :8], green, precision=HIGH, preferred_element_type=F32)
        out_ref[g] = out[:PART] + sign * pltpu.roll(out[PART:], V, 1)


def field_kernel(
    lev_ref, from_x_ref, from_y_ref, from_d_ref, conv_ref, cb_ref, mix_ref, mb_ref, dec_ref,
    hi_ref, lo_ref, _nf, _edge, _feat, send_ref, nf_ref, edge_ref, feat_ref, ext_ref, hot_ref,
):
    first_x = lax.axis_index("px") == 0
    first_y = lax.axis_index("py") == 0
    tile = jnp.concatenate([from_x_ref[:, :128], lev_ref[:8, :128].astype(F32)], axis=0)
    left = jnp.concatenate([from_d_ref[:8, :], from_y_ref[:8, :]], axis=0)
    tile_windows(left, tile, first_y, ext_ref)
    level_ids = iota((LEVELS, 128), 0).astype(F32)
    for w in range(4):
        for o in range(4):
            for b in range(3):
                e = 2 * w + o
                at = o * SLOT + b * LEVELS
                hot_ref[at : at + LEVELS, w * 128 : (w + 1) * 128] = one_hot(
                    ext_ref[b, e : e + 1, :], level_ids
                )
    tiles = features(
        hot_ref[:, :384], conv_ref[...], cb_ref[...], mix_ref[...], mb_ref[...]
    )
    for w in range(3):
        feat_ref[2 * w * HID : (2 * w + 2) * HID, :128] = tiles[:, w * 128 : (w + 1) * 128]
    feat_ref[6 * HID : 8 * HID, :128] = features(
        hot_ref[:, 384:], cut_conv(conv_ref[...], first_x), cb_ref[...], mix_ref[...], mb_ref[...]
    )

    shape = (KS * CH * BLOCK, 2 * BLOCK * HID)
    sample = iota(shape, 0) // 4 % BLOCK - SHIFT
    pillar = iota(shape, 1) // HID - SHIFT - 2
    for i in range(2):
        at = i * BLOCK
        apart = (sample + at >= 0) != (pillar + at >= 0)
        keep = jnp.where(first_x & apart, 0.0, 1.0)
        near_field(i, dec_ref[...] * keep.astype(BF16), feat_ref, nf_ref, edge_ref, first_y)

    column_sum(hi_ref, lo_ref, nf_ref, edge_ref, from_d_ref, send_ref, 4, 4)


def field(
    levels, from_x, from_y, from_d, conv_w, conv_b, mix_w, mix_b, dec_w, hi, lo, nf, edge, feat
):
    return pl.pallas_call(
        field_kernel,
        in_specs=[VMEM] * 14,
        out_specs=[VMEM] * 4,
        out_shape=[
            jax.ShapeDtypeStruct((4, PART, 128), F32),
            jax.ShapeDtypeStruct((4 * PART, COLS), BF16),
            jax.ShapeDtypeStruct((2 * PART, 128), F32),
            jax.ShapeDtypeStruct(feat.shape, BF16),
        ],
        input_output_aliases={11: 1, 12: 2, 13: 3},
        scratch_shapes=[
            pltpu.VMEM((3, 16, 128), F32),
            pltpu.VMEM((WINDOW, 512), BF16),
        ],
        compiler_params=params(12),
        name="field",
    )(
        levels, from_x, from_y, from_d, conv_w, conv_b, mix_w, mix_b, dec_w, hi, lo, nf, edge, feat
    )


def keep_planes(hi, lo, nf, edge, from_d, first, count):
    def keep_kernel(hi_ref, lo_ref, nf_ref, edge_ref, from_d_ref, out_ref):
        column_sum(hi_ref, lo_ref, nf_ref, edge_ref, from_d_ref, out_ref, first, count)

    return pl.pallas_call(
        keep_kernel,
        in_specs=[VMEM] * 5,
        out_specs=VMEM,
        out_shape=jax.ShapeDtypeStruct((count, PART, 128), F32),
        compiler_params=params(8),
        name="keep_planes",
    )(hi, lo, nf, edge, from_d)


def rows_kernel(from_x_ref, rows_ref, order_ref, out_ref):
    z = lax.axis_index("py")
    green = jnp.concatenate([rows_ref[z, 0], rows_ref[z, 1]], axis=1)
    green = jnp.concatenate([from_x_ref[:, COLS:], green], axis=0)
    n = ROWS + 8
    green = jnp.concatenate(split2(green), axis=0)
    pick = (order_ref[...] == iota((U, U), 0)).astype(BF16)
    copies = (iota((U, U * 4), 1) // 4 == iota((U, U * 4), 0)).astype(BF16)
    pick = jnp.dot(pick, copies, preferred_element_type=F32).astype(BF16)
    row = iota((3 * PART, 2 * n), 0)
    source = (row % PART) // 4 + (8 - SHIFT) + jnp.where(row // PART == 1, n, 0)
    spread = (iota((3 * PART, 2 * n), 1) == source).astype(BF16)
    mask = iota((3 * PART, U * 4), 0) % 4 == iota((3 * PART, U * 4), 1) % 4
    for j in range(2):
        ordered = jnp.dot(green[:, j * U : (j + 1) * U], pick, preferred_element_type=F32)
        wide = jnp.dot(spread, ordered.astype(BF16), preferred_element_type=F32)
        out_ref[j * U * 4 : (j + 1) * U * 4, :] = jnp.where(mask, wide, 0.0).T.astype(BF16)


def row_factors(from_x, rows_t, order):
    return pl.pallas_call(
        rows_kernel,
        in_specs=[VMEM] * 3,
        out_specs=VMEM,
        out_shape=jax.ShapeDtypeStruct((2 * U * 4, 3 * PART), BF16),
        compiler_params=params(4),
        name="row_factors",
    )(from_x, rows_t, order)


def focal_kernel(factor_ref, keep_ref, got_ref, b_ref, c_ref, d_ref, out_ref):
    t = ((keep_ref[0] + got_ref[0]) + b_ref[...]) + (c_ref[...] + d_ref[...])
    hi, lo = split2(t)
    out = jnp.dot(
        factor_ref[...], jnp.concatenate([hi, hi, lo], axis=0), preferred_element_type=F32
    )
    n = U * 4
    sign = jnp.where(iota((1, 128), 1) < V, -1.0, 1.0)
    out_ref[...] = (out[:n] + sign * pltpu.roll(out[n:], V, 1)).reshape(out_ref.shape)


def focal_share(factors, keep, got, b, c, d):
    return pl.pallas_call(
        focal_kernel,
        in_specs=[VMEM] * 6,
        out_specs=VMEM,
        out_shape=jax.ShapeDtypeStruct((U // 2, 8, 128), F32),
        compiler_params=params(4),
        name="focal_share",
    )(factors, keep, got, b, c, d)


def total_kernel(x_ref, out_ref):
    s = jnp.sum(x_ref[...], axis=0)
    for u in range(2):
        for k in range(2):
            for p in range(4):
                at = (k * 4 + p) * V
                row = u * 4 + p
                out_ref[0, u : u + 1, at : at + V] = s[row : row + 1, k * V : (k + 1) * V]


def total(parts):
    return pl.pallas_call(
        total_kernel,
        in_specs=[VMEM],
        out_specs=VMEM,
        out_shape=jax.ShapeDtypeStruct((1, 2, 8 * V), F32),
        compiler_params=params(4),
        name="total",
    )(parts)


def on_device(
    levels, conv_table, conv_bias, mix_weight, mix_bias, decoder, green_rows, green_cols, focal_order
):
    count_px = lax.axis_size("px")
    count_py = lax.axis_size("py")
    rows_t = jnp.swapaxes(green_rows, 2, 3)
    next_x = [(i, (i + 1) % count_px) for i in range(count_px)]
    next_y = [(i, (i + 1) % count_py) for i in range(count_py)]
    order = focal_order.reshape(1, U)

    to_x, to_y = pack(levels, rows_t)
    from_x = lax.ppermute(to_x, "px", next_x)
    from_y = lax.ppermute(to_y, "py", next_y)
    feat, hi, lo, green, conv_w, conv_b, mix_w, mix_b, dec_w = inner(
        levels, conv_table, conv_bias, mix_weight, mix_bias, decoder, green_cols
    )
    from_y, feat = lax.optimization_barrier((from_y, feat))
    nf, edge, feat = middle(levels, from_y, conv_w, conv_b, mix_w, mix_b, dec_w, feat)
    from_x, feat, nf, edge = lax.optimization_barrier((from_x, feat, nf, edge))
    from_d = lax.ppermute(relay(from_x, green), "py", next_y)
    feat = outer(levels, from_x, conv_w, conv_b, mix_w, mix_b, feat)
    send, nf, edge, _ = field(
        levels, from_x, from_y, from_d, conv_w, conv_b, mix_w, mix_b, dec_w, hi, lo, nf, edge, feat
    )

    def swap(x, mask):
        return lax.ppermute(x, "py", [(i, i ^ mask) for i in range(count_py)])

    got = swap(send, 1)
    keep = keep_planes(hi, lo, nf, edge, from_d, 1, 3)
    b, c, d = (swap(keep[i - 1] + got[i], 2 * i) for i in (1, 2, 3))
    keep = keep_planes(hi, lo, nf, edge, from_d, 0, 1)
    factors = row_factors(from_x, rows_t, order)
    share = focal_share(factors, keep, got, b, c, d)
    return total(lax.all_to_all(share, "px", 0, 0))


def solution(mesh):
    return jax.shard_map(
        on_device,
        mesh=mesh,
        in_specs=(
            P("px", "py"),
            P(),
            P(),
            P(),
            P(),
            P(),
            P(None, None, None, "px"),
            P(None, None, None, "py"),
            P(),
        ),
        out_specs=P("py", "px", None),
        check_vma=False,
    )
```

```python
import jax
import jax.numpy as jnp
from jax import lax
from jax.experimental import pallas as pl
from jax.experimental.pallas import tpu as pltpu
from jax.sharding import PartitionSpec as P

HIGH = lax.Precision.HIGHEST
F32 = jnp.float32
BF16 = jnp.bfloat16
NT = (((1,), (1,)), ((), ()))
TN = (((0,), (0,)), ((), ()))

ROWS = 16
COLS = 1024
HID = 64
LEVELS = 16
CH = 8
KS = 5
Z = 8
U = 64
V = 64
HALO = 4
SHIFT = 5
PILLAR_ROWS = ROWS + KS - 1
SLOT = 3 * LEVELS
WINDOW = 4 * SLOT
BLOCK = 4
REL_ORDER = (0, 2, 4, 6, 1, 3, 5, 7)
PART = ROWS * CH // 2
HALF = BLOCK * CH // 2
VMEM = pl.BlockSpec(memory_space=pltpu.VMEM)
HBM = pl.BlockSpec(memory_space=pltpu.HBM)


def params(mib):
    return pltpu.CompilerParams(vmem_limit_bytes=mib << 20)

GELU_A = 0.7978845608028654
GELU_B = GELU_A * 0.044715


def iota(shape, dim):
    return lax.broadcasted_iota(jnp.int32, shape, dim)


def twice_gelu(x):
    return x + x * jnp.tanh(x * (GELU_A + GELU_B * (x * x)))


def split2(x):
    hi = x.astype(BF16)
    return hi, (x - hi.astype(F32)).astype(BF16)


def hbm(x):
    return pltpu.with_memory_space_constraint(x, pltpu.HBM)


def pack_kernel(lev_hbm, rows_hbm, to_x_ref, to_y_ref, out_ref, lev_ref, rows_ref, sems):
    z = lax.axis_index("py")
    copies = [
        pltpu.make_async_copy(lev_hbm, lev_ref, sems.at[0]),
        pltpu.make_async_copy(rows_hbm.at[z], rows_ref, sems.at[1]),
    ]
    for copy in copies:
        copy.start()
    for copy in copies:
        copy.wait()
    lev = lev_ref[...].astype(F32)
    out_ref[...] = lev
    to_x_ref[:, :COLS] = lev[8:, :]
    to_x_ref[:, COLS:] = jnp.concatenate([rows_ref[0, 8:, :], rows_ref[1, 8:, :]], axis=1)
    to_y_ref[...] = lev[:, COLS - 128 :]


def pack(levels, rows_t):
    return pl.pallas_call(
        pack_kernel,
        in_specs=[HBM] * 2,
        out_specs=[VMEM] * 3,
        out_shape=[
            jax.ShapeDtypeStruct((8, COLS + 128), F32),
            jax.ShapeDtypeStruct((ROWS, 128), F32),
            jax.ShapeDtypeStruct((ROWS, COLS), F32),
        ],
        scratch_shapes=[
            pltpu.VMEM((ROWS, COLS), jnp.int32),
            pltpu.VMEM((2, ROWS, U), F32),
            pltpu.SemaphoreType.DMA((2,)),
        ],
        compiler_params=params(4),
        name="pack",
    )(hbm(levels), hbm(rows_t))


def relay_kernel(from_x_ref, green_ref, out_ref):
    out_ref[:8, :] = from_x_ref[:, COLS - 128 : COLS]
    out_ref[8:, :] = green_ref[...]


def relay(from_x, green):
    return pl.pallas_call(
        relay_kernel,
        in_specs=[VMEM] * 2,
        out_specs=VMEM,
        out_shape=jax.ShapeDtypeStruct((8 + Z * HALO, 128), F32),
        compiler_params=params(4),
        name="relay",
    )(from_x, green)


def one_hot(row, level_ids):
    row = jnp.broadcast_to(row, level_ids.shape)
    return jnp.where(row == level_ids, 1.0, 0.0).astype(BF16)


def features(window, conv, conv_bias, mix, mix_bias):
    pre = jnp.dot(conv, window, preferred_element_type=F32) + conv_bias
    hidden = twice_gelu(pre).astype(BF16)
    mixed = jnp.dot(mix, hidden, preferred_element_type=F32) + mix_bias
    return twice_gelu(mixed).astype(BF16)


def lanes_from(x, count, offset):
    shape = (x.shape[1], count)
    move = (iota(shape, 1) == iota(shape, 0) + offset).astype(BF16)
    return jnp.dot(x, move, preferred_element_type=F32)


def bias_column(row):
    shape = (2 * HID, HID)
    own = iota(shape, 1) == iota(shape, 0) % HID
    return jnp.sum(jnp.where(own, row, 0.0), axis=1, keepdims=True)


def lay_out_decoder(dec_ref, out_ref):
    n = KS * CH * BLOCK
    row = iota((n, n), 0)
    source = row // 4 % BLOCK * (KS * CH) + row // (4 * BLOCK) * 4 + row % 4
    move = (iota((n, n), 1) == source).astype(BF16)
    dec = dec_ref[...].astype(F32)
    none = jnp.zeros((KS * CH, HID), F32)

    def column(pillar):
        taps = [r - pillar + KS - 1 for r in range(BLOCK)]
        return jnp.concatenate([dec[t] if 0 <= t < KS else none for t in taps], axis=0)

    for i in range(BLOCK):
        pair = jnp.concatenate([column(2 * i), column(2 * i + 1)], axis=1).astype(BF16)
        wide = jnp.dot(move, pair, preferred_element_type=F32)
        out_ref[:, 2 * i * HID : (2 * i + 2) * HID] = (0.5 * wide).astype(BF16)


def inner_kernel(
    lev_ref, table_hbm, cb_hbm, mix_hbm, mb_hbm, dec_hbm, cols_hbm,
    feat_ref, hi_ref, lo_ref, green_ref, conv_ref, cb_ref, mixer_ref, mb_ref, dec_ref,
    ext_ref, hot_ref, cols_ref, table_ref, cbr_ref, mix_ref, mbr_ref, raw_ref, sems,
):
    z = lax.axis_index("py")
    small = [
        pltpu.make_async_copy(table_hbm, table_ref, sems.at[Z]),
        pltpu.make_async_copy(cb_hbm, cbr_ref, sems.at[Z + 1]),
        pltpu.make_async_copy(mix_hbm, mix_ref, sems.at[Z + 2]),
        pltpu.make_async_copy(mb_hbm, mbr_ref, sems.at[Z + 3]),
        pltpu.make_async_copy(dec_hbm, raw_ref, sems.at[Z + 4]),
    ]
    copies = [
        pltpu.make_async_copy(cols_hbm.at[z ^ REL_ORDER[g]], cols_ref.at[g], sems.at[g])
        for g in range(Z)
    ]
    for copy in small + copies:
        copy.start()
    wide = COLS - 128
    lev = lev_ref[...]
    for b in range(3):
        ext_ref[b] = pltpu.roll(lev, 3 - b, 1)[:, 128:]
    level_ids = iota((LEVELS, wide), 0).astype(F32)

    def make_hot(q, _):
        for b in range(3):
            hot_ref[pl.ds(q * SLOT + b * LEVELS, LEVELS), :] = one_hot(
                ext_ref[b, pl.ds(q, 1), :], level_ids
            )
        return 0

    lax.fori_loop(0, ROWS - 2, make_hot, 0, unroll=2)
    for copy in small:
        copy.wait()
    conv_ref[:HID, :] = lanes_from(table_ref[...], WINDOW, 0).astype(BF16)
    conv_ref[HID:, :] = lanes_from(table_ref[...], WINDOW, SLOT).astype(BF16)
    mixer_ref[:HID, :] = (0.5 * lanes_from(mix_ref[...], 2 * HID, 0)).astype(BF16)
    mixer_ref[HID:, :] = (0.5 * lanes_from(mix_ref[...], 2 * HID, HID)).astype(BF16)
    cb_ref[...] = bias_column(cbr_ref[...])
    mb_ref[...] = bias_column(mbr_ref[...])
    lay_out_decoder(raw_ref, dec_ref)
    conv_bias = jnp.broadcast_to(cb_ref[...], (2 * HID, wide))
    mix_bias = jnp.broadcast_to(mb_ref[...], (2 * HID, wide))
    for i in range(ROWS // 2 - 2):
        at = (8 + 2 * i) * HID
        feat_ref[at : at + 2 * HID, 128:] = features(
            hot_ref[i * 2 * SLOT : i * 2 * SLOT + WINDOW, :],
            conv_ref[...], conv_bias, mixer_ref[...], mix_bias,
        )
    for copy in copies:
        copy.wait()

    def split(g, _):
        hi_ref[g], lo_ref[g] = split2(cols_ref[g].reshape(2 * V, COLS))
        return 0

    lax.fori_loop(0, Z, split, 0)
    for g in range(Z):
        edge = cols_ref[g, :, :, COLS - 128 :].reshape(2 * V, 128).T
        green_ref[HALO * g : HALO * (g + 1), :] = edge[128 - HALO :, :]


def inner(levels, table, conv_bias, mix, mix_bias, decoder, green_cols):
    wide = COLS - 128
    return pl.pallas_call(
        inner_kernel,
        in_specs=[VMEM] + [HBM] * 6,
        out_specs=[VMEM] * 9,
        out_shape=[
            jax.ShapeDtypeStruct((PILLAR_ROWS * HID, COLS), BF16),
            jax.ShapeDtypeStruct((Z, 2 * V, COLS), BF16),
            jax.ShapeDtypeStruct((Z, 2 * V, COLS), BF16),
            jax.ShapeDtypeStruct((Z * HALO, 128), F32),
            jax.ShapeDtypeStruct((2 * HID, WINDOW), BF16),
            jax.ShapeDtypeStruct((2 * HID, 1), F32),
            jax.ShapeDtypeStruct((2 * HID, 2 * HID), BF16),
            jax.ShapeDtypeStruct((2 * HID, 1), F32),
            jax.ShapeDtypeStruct((KS * CH * BLOCK, 2 * BLOCK * HID), BF16),
        ],
        scratch_shapes=[
            pltpu.VMEM((3, ROWS, wide), F32),
            pltpu.VMEM(((ROWS - 2) * SLOT, wide), BF16),
            pltpu.VMEM((Z, 2, V, COLS), F32),
            pltpu.VMEM(table.shape, BF16),
            pltpu.VMEM((1, HID), F32),
            pltpu.VMEM((HID, HID), BF16),
            pltpu.VMEM((1, HID), F32),
            pltpu.VMEM(decoder.shape, BF16),
            pltpu.SemaphoreType.DMA((Z + 5,)),
        ],
        compiler_params=params(16),
        name="inner",
    )(levels, *map(hbm, (
        table, conv_bias.reshape(1, HID), mix, mix_bias.reshape(1, HID), decoder, green_cols,
    )))


def tile_windows(left, tile, first_y, ext_ref):
    ext = jnp.concatenate([left, tile], axis=1)
    lane = iota(tile.shape, 1)
    for b in range(3):
        window = pltpu.roll(ext, 3 - b, 1)[:, 128:]
        if b != 1:
            window = jnp.where(first_y & (lane == (2 if b == 0 else 1)), -1.0, window)
        ext_ref[b] = window


def near_field(i, dec, feat_ref, nf_ref, edge_ref, first_y):
    lane = iota((1, COLS), 1)
    near = iota((1, 128), 1)
    at = i * BLOCK * HID
    taps = jnp.dot(dec, feat_ref[at : at + 2 * BLOCK * HID, :], preferred_element_type=F32)
    acc = jnp.zeros((2 * HALF, COLS), F32)
    edge = jnp.zeros((2 * HALF, 128), F32)
    for s in range(KS):
        part = taps[2 * HALF * s : 2 * HALF * (s + 1), :]
        k = KS - 1 - s
        ok = (lane < COLS - k) & ((lane + k >= 2) | jnp.logical_not(first_y))
        moved = part if k == 0 else pltpu.roll(part, COLS - k, 1)
        acc = acc + jnp.where(ok, moved, 0.0)
        ok = (near >= s) & (near < HALO) & ((near - s < 2) | jnp.logical_not(first_y))
        part = part[:, :128]
        moved = part if s == 0 else pltpu.roll(part, s, 1)
        edge = edge + jnp.where(ok, moved, 0.0)
    for part, values in enumerate(split2(acc)):
        for k in range(2):
            at = (2 * part + k) * PART + i * HALF
            nf_ref[at : at + HALF, :] = values[k * HALF : (k + 1) * HALF]
    for k in range(2):
        at = k * PART + i * HALF
        edge_ref[at : at + HALF, :] = edge[k * HALF : (k + 1) * HALF]


def middle_kernel(
    lev_ref, from_y_ref, conv_ref, cb_ref, mix_ref, mb_ref, dec_ref, _,
    nf_ref, edge_ref, feat_ref, ext_ref, hot_ref,
):
    first_y = lax.axis_index("py") == 0
    tile_windows(from_y_ref[...], lev_ref[:, :128], first_y, ext_ref)
    level_ids = iota((LEVELS, 128), 0).astype(F32)
    for q in range(ROWS - 2):
        for b in range(3):
            row = one_hot(ext_ref[b, q : q + 1, :], level_ids)
            for t in range(6):
                if 0 <= q - 2 * t < 4:
                    at = (q - 2 * t) * SLOT + b * LEVELS
                    hot_ref[at : at + LEVELS, t * 128 : (t + 1) * 128] = row
    tiles = features(hot_ref[...], conv_ref[...], cb_ref[...], mix_ref[...], mb_ref[...])
    for t in range(6):
        at = (8 + 2 * t) * HID
        feat_ref[at : at + 2 * HID, :128] = tiles[:, t * 128 : (t + 1) * 128]
    for i in (2, 3):
        near_field(i, dec_ref[...], feat_ref, nf_ref, edge_ref, first_y)


def middle(levels, from_y, conv_w, conv_b, mix_w, mix_b, dec_w, feat):
    return pl.pallas_call(
        middle_kernel,
        in_specs=[VMEM] * 8,
        out_specs=[VMEM] * 3,
        out_shape=[
            jax.ShapeDtypeStruct((4 * PART, COLS), BF16),
            jax.ShapeDtypeStruct((2 * PART, 128), F32),
            jax.ShapeDtypeStruct(feat.shape, BF16),
        ],
        input_output_aliases={7: 2},
        scratch_shapes=[pltpu.VMEM((3, ROWS, 128), F32), pltpu.VMEM((WINDOW, 768), BF16)],
        compiler_params=params(8),
        name="middle",
    )(levels, from_y, conv_w, conv_b, mix_w, mix_b, dec_w, feat)


def outer_kernel(
    lev_ref, from_x_ref, conv_ref, cb_ref, mix_ref, mb_ref, _, feat_ref, ext_ref, hot_ref
):
    first_x = lax.axis_index("px") == 0
    ext = jnp.concatenate([from_x_ref[:, :COLS], lev_ref[:8, :]], axis=0)
    for b in range(3):
        ext_ref[b] = pltpu.roll(ext, 3 - b, 1)[:, 128:]
    wide = COLS - 128
    level_ids = iota((LEVELS, wide), 0).astype(F32)
    for e in range(10):
        for b in range(3):
            at = e * SLOT + b * LEVELS
            hot_ref[at : at + LEVELS, :] = one_hot(ext_ref[b, e : e + 1, :], level_ids)
    conv_bias = jnp.broadcast_to(cb_ref[...], (2 * HID, wide))
    mix_bias = jnp.broadcast_to(mb_ref[...], (2 * HID, wide))
    for w in range(4):
        at = 2 * w * HID
        conv = cut_conv(conv_ref[...], first_x) if w == 3 else conv_ref[...]
        feat_ref[at : at + 2 * HID, 128:] = features(
            hot_ref[2 * w * SLOT : 2 * w * SLOT + WINDOW, :],
            conv, conv_bias, mix_ref[...], mix_bias,
        )


def cut_conv(conv, first_x):
    slot = iota((2 * HID, WINDOW), 1) // SLOT
    row = iota((2 * HID, WINDOW), 0) // HID
    keep = jnp.where(first_x & (slot + row == 2) & (slot > 0), 0.0, 1.0)
    return conv * keep.astype(BF16)


def outer(levels, from_x, conv_w, conv_b, mix_w, mix_b, feat):
    wide = COLS - 128
    return pl.pallas_call(
        outer_kernel,
        in_specs=[VMEM] * 7,
        out_specs=VMEM,
        out_shape=jax.ShapeDtypeStruct(feat.shape, BF16),
        input_output_aliases={6: 0},
        scratch_shapes=[
            pltpu.VMEM((3, 16, wide), F32),
            pltpu.VMEM((10 * SLOT, wide), BF16),
        ],
        compiler_params=params(8),
        name="outer",
    )(levels, from_x, conv_w, conv_b, mix_w, mix_b, feat)


def column_sum(hi_ref, lo_ref, nf_ref, edge_ref, from_d_ref, out_ref, first, count):
    iy = lax.axis_index("py")
    before = (iy + lax.axis_size("py") - 1) % lax.axis_size("py")
    n = 2 * PART
    sign = jnp.where(iota((1, 128), 1) < V, -1.0, 1.0)
    hi = hi_ref[first : first + count].reshape(2 * V * count, COLS)
    lo = lo_ref[first : first + count].reshape(2 * V * count, COLS)
    both = lax.dot_general(hi, nf_ref[...], NT, preferred_element_type=F32)
    both = both[:, :n] + both[:, n:]
    both = both + lax.dot_general(lo, nf_ref[:n, :], NT, preferred_element_type=F32)
    greens = []
    for g in range(count):
        rel = (iy ^ REL_ORDER[first + g]) ^ before
        at = 8 + HALO * (rel // 2 + 4 * (rel % 2))
        greens.append(from_d_ref[pl.ds(at, HALO), :])
    green = jnp.concatenate(greens, axis=1)
    green = jnp.concatenate([green, jnp.zeros((4, 2 * V * count), F32)], axis=0)
    edge = jnp.dot(edge_ref[:, :8], green, precision=HIGH, preferred_element_type=F32)
    for g in range(count):
        at = 2 * V * g
        out = both[at : at + 2 * V].T + edge[:, at : at + 2 * V]
        out_ref[g] = out[:PART] + sign * pltpu.roll(out[PART:], V, 1)


def field_kernel(
    lev_ref, from_x_ref, from_y_ref, from_d_ref, conv_ref, cb_ref, mix_ref, mb_ref, dec_ref,
    hi_ref, lo_ref, _nf, _edge, _feat, send_ref, nf_ref, edge_ref, feat_ref, ext_ref, hot_ref,
):
    first_x = lax.axis_index("px") == 0
    first_y = lax.axis_index("py") == 0
    tile = jnp.concatenate([from_x_ref[:, :128], lev_ref[:8, :128]], axis=0)
    left = jnp.concatenate([from_d_ref[:8, :], from_y_ref[:8, :]], axis=0)
    tile_windows(left, tile, first_y, ext_ref)
    level_ids = iota((LEVELS, 128), 0).astype(F32)
    for w in range(4):
        for o in range(4):
            for b in range(3):
                e = 2 * w + o
                at = o * SLOT + b * LEVELS
                hot_ref[at : at + LEVELS, w * 128 : (w + 1) * 128] = one_hot(
                    ext_ref[b, e : e + 1, :], level_ids
                )
    tiles = features(
        hot_ref[:, :384], conv_ref[...], cb_ref[...], mix_ref[...], mb_ref[...]
    )
    for w in range(3):
        feat_ref[2 * w * HID : (2 * w + 2) * HID, :128] = tiles[:, w * 128 : (w + 1) * 128]
    feat_ref[6 * HID : 8 * HID, :128] = features(
        hot_ref[:, 384:], cut_conv(conv_ref[...], first_x), cb_ref[...], mix_ref[...], mb_ref[...]
    )

    shape = (KS * CH * BLOCK, 2 * BLOCK * HID)
    sample = iota(shape, 0) // 4 % BLOCK - SHIFT
    pillar = iota(shape, 1) // HID - SHIFT - 2
    for i in range(2):
        at = i * BLOCK
        apart = (sample + at >= 0) != (pillar + at >= 0)
        keep = jnp.where(first_x & apart, 0.0, 1.0)
        near_field(i, dec_ref[...] * keep.astype(BF16), feat_ref, nf_ref, edge_ref, first_y)

    column_sum(hi_ref, lo_ref, nf_ref, edge_ref, from_d_ref, send_ref, 4, 4)


def field(
    levels, from_x, from_y, from_d, conv_w, conv_b, mix_w, mix_b, dec_w, hi, lo, nf, edge, feat
):
    return pl.pallas_call(
        field_kernel,
        in_specs=[VMEM] * 14,
        out_specs=[VMEM] * 4,
        out_shape=[
            jax.ShapeDtypeStruct((4, PART, 128), F32),
            jax.ShapeDtypeStruct((4 * PART, COLS), BF16),
            jax.ShapeDtypeStruct((2 * PART, 128), F32),
            jax.ShapeDtypeStruct(feat.shape, BF16),
        ],
        input_output_aliases={11: 1, 12: 2, 13: 3},
        scratch_shapes=[
            pltpu.VMEM((3, 16, 128), F32),
            pltpu.VMEM((WINDOW, 512), BF16),
        ],
        compiler_params=params(12),
        name="field",
    )(
        levels, from_x, from_y, from_d, conv_w, conv_b, mix_w, mix_b, dec_w, hi, lo, nf, edge, feat
    )


def keep_planes(hi, lo, nf, edge, from_d, first, count):
    def keep_kernel(hi_ref, lo_ref, nf_ref, edge_ref, from_d_ref, out_ref):
        column_sum(hi_ref, lo_ref, nf_ref, edge_ref, from_d_ref, out_ref, first, count)

    return pl.pallas_call(
        keep_kernel,
        in_specs=[VMEM] * 5,
        out_specs=VMEM,
        out_shape=jax.ShapeDtypeStruct((count, PART, 128), F32),
        compiler_params=params(8),
        name="keep_planes",
    )(hi, lo, nf, edge, from_d)


def rows_kernel(from_x_ref, rows_ref, order_ref, out_ref):
    z = lax.axis_index("py")
    green = jnp.concatenate([rows_ref[z, 0], rows_ref[z, 1]], axis=1)
    green = jnp.concatenate([from_x_ref[:, COLS:], green], axis=0)
    n = ROWS + 8
    green = jnp.concatenate(split2(green), axis=0)
    pick = (order_ref[...] == iota((U, U), 0)).astype(BF16)
    copies = (iota((U, U * 4), 1) // 4 == iota((U, U * 4), 0)).astype(BF16)
    pick = jnp.dot(pick, copies, preferred_element_type=F32).astype(BF16)
    row = iota((3 * PART, 2 * n), 0)
    source = (row % PART) // 4 + (8 - SHIFT) + jnp.where(row // PART == 1, n, 0)
    spread = (iota((3 * PART, 2 * n), 1) == source).astype(BF16)
    mask = iota((3 * PART, U * 4), 0) % 4 == iota((3 * PART, U * 4), 1) % 4
    for j in range(2):
        ordered = jnp.dot(green[:, j * U : (j + 1) * U], pick, preferred_element_type=F32)
        wide = jnp.dot(spread, ordered.astype(BF16), preferred_element_type=F32)
        out_ref[j * U * 4 : (j + 1) * U * 4, :] = jnp.where(mask, wide, 0.0).T.astype(BF16)


def row_factors(from_x, rows_t, order):
    return pl.pallas_call(
        rows_kernel,
        in_specs=[VMEM] * 3,
        out_specs=VMEM,
        out_shape=jax.ShapeDtypeStruct((2 * U * 4, 3 * PART), BF16),
        compiler_params=params(4),
        name="row_factors",
    )(from_x, rows_t, order)


def focal_kernel(factor_ref, keep_ref, got_ref, b_ref, c_ref, d_ref, out_ref):
    t = ((keep_ref[0] + got_ref[0]) + b_ref[...]) + (c_ref[...] + d_ref[...])
    hi, lo = split2(t)
    out = jnp.dot(
        factor_ref[...], jnp.concatenate([hi, hi, lo], axis=0), preferred_element_type=F32
    )
    n = U * 4
    sign = jnp.where(iota((1, 128), 1) < V, -1.0, 1.0)
    out_ref[...] = (out[:n] + sign * pltpu.roll(out[n:], V, 1)).reshape(out_ref.shape)


def focal_share(factors, keep, got, b, c, d):
    return pl.pallas_call(
        focal_kernel,
        in_specs=[VMEM] * 6,
        out_specs=VMEM,
        out_shape=jax.ShapeDtypeStruct((U // 2, 8, 128), F32),
        compiler_params=params(4),
        name="focal_share",
    )(factors, keep, got, b, c, d)


def total_kernel(x_ref, out_ref):
    s = jnp.sum(x_ref[...], axis=0)
    for u in range(2):
        for k in range(2):
            for p in range(4):
                at = (k * 4 + p) * V
                row = u * 4 + p
                out_ref[0, u : u + 1, at : at + V] = s[row : row + 1, k * V : (k + 1) * V]


def total(parts):
    return pl.pallas_call(
        total_kernel,
        in_specs=[VMEM],
        out_specs=VMEM,
        out_shape=jax.ShapeDtypeStruct((1, 2, 8 * V), F32),
        compiler_params=params(4),
        name="total",
    )(parts)


def on_device(
    levels, conv_table, conv_bias, mix_weight, mix_bias, decoder, green_rows, green_cols, focal_order
):
    count_px = lax.axis_size("px")
    count_py = lax.axis_size("py")
    rows_t = jnp.swapaxes(green_rows, 2, 3)
    next_x = [(i, (i + 1) % count_px) for i in range(count_px)]
    next_y = [(i, (i + 1) % count_py) for i in range(count_py)]
    order = focal_order.reshape(1, U)

    to_x, to_y, levels = pack(levels, rows_t)
    from_x = lax.ppermute(to_x, "px", next_x)
    from_y = lax.ppermute(to_y, "py", next_y)
    feat, hi, lo, green, conv_w, conv_b, mix_w, mix_b, dec_w = inner(
        levels, conv_table, conv_bias, mix_weight, mix_bias, decoder, green_cols
    )
    from_y, feat = lax.optimization_barrier((from_y, feat))
    nf, edge, feat = middle(levels, from_y, conv_w, conv_b, mix_w, mix_b, dec_w, feat)
    from_x, feat, nf, edge = lax.optimization_barrier((from_x, feat, nf, edge))
    from_d = lax.ppermute(relay(from_x, green), "py", next_y)
    feat = outer(levels, from_x, conv_w, conv_b, mix_w, mix_b, feat)
    send, nf, edge, _ = field(
        levels, from_x, from_y, from_d, conv_w, conv_b, mix_w, mix_b, dec_w, hi, lo, nf, edge, feat
    )

    def swap(x, mask):
        return lax.ppermute(x, "py", [(i, i ^ mask) for i in range(count_py)])

    got = swap(send, 1)
    keep = keep_planes(hi, lo, nf, edge, from_d, 1, 3)
    b, c, d = (swap(keep[i - 1] + got[i], 2 * i) for i in (1, 2, 3))
    keep = keep_planes(hi, lo, nf, edge, from_d, 0, 1)
    factors = row_factors(from_x, rows_t, order)
    share = focal_share(factors, keep, got, b, c, d)
    return total(lax.all_to_all(share, "px", 0, 0))


def solution(mesh):
    return jax.shard_map(
        on_device,
        mesh=mesh,
        in_specs=(
            P("px", "py"),
            P(),
            P(),
            P(),
            P(),
            P(),
            P(None, None, None, "px"),
            P(None, None, None, "py"),
            P(),
        ),
        out_specs=P("py", "px", None),
        check_vma=False,
    )
```

```python
import jax
import jax.numpy as jnp
from jax import lax
from jax.experimental import pallas as pl
from jax.experimental.pallas import tpu as pltpu
from jax.sharding import PartitionSpec as P

HIGH = lax.Precision.HIGHEST
F32 = jnp.float32
BF16 = jnp.bfloat16
NT = (((1,), (1,)), ((), ()))
TN = (((0,), (0,)), ((), ()))

ROWS = 16
COLS = 1024
HID = 64
LEVELS = 16
CH = 8
KS = 5
Z = 8
U = 64
V = 64
HALO = 4
SHIFT = 5
PILLAR_ROWS = ROWS + KS - 1
SLOT = 3 * LEVELS
WINDOW = 4 * SLOT
BLOCK = 4
REL_ORDER = (0, 2, 4, 6, 1, 3, 5, 7)
PART = ROWS * CH // 2
HALF = BLOCK * CH // 2
VMEM = pl.BlockSpec(memory_space=pltpu.VMEM)
HBM = pl.BlockSpec(memory_space=pltpu.HBM)


def params(mib):
    return pltpu.CompilerParams(vmem_limit_bytes=mib << 20)

GELU_A = 0.7978845608028654
GELU_B = GELU_A * 0.044715


def iota(shape, dim):
    return lax.broadcasted_iota(jnp.int32, shape, dim)


def twice_gelu(x):
    return x + x * jnp.tanh(x * (GELU_A + GELU_B * (x * x)))


def split2(x):
    hi = x.astype(BF16)
    return hi, (x - hi.astype(F32)).astype(BF16)


def hbm(x):
    return pltpu.with_memory_space_constraint(x, pltpu.HBM)


def pack_kernel(lev_hbm, rows_hbm, to_x_ref, to_y_ref, out_ref, lev_ref, rows_ref, sems):
    z = lax.axis_index("py")
    copies = [
        pltpu.make_async_copy(lev_hbm, lev_ref, sems.at[0]),
        pltpu.make_async_copy(rows_hbm.at[z], rows_ref, sems.at[1]),
    ]
    for copy in copies:
        copy.start()
    for copy in copies:
        copy.wait()
    lev = lev_ref[...].astype(F32)
    out_ref[...] = lev
    to_x_ref[:, :COLS] = lev[8:, :]
    to_x_ref[:, COLS:] = jnp.concatenate([rows_ref[0, 8:, :], rows_ref[1, 8:, :]], axis=1)
    to_y_ref[...] = lev[:, COLS - 128 :]


def pack(levels, rows_t):
    return pl.pallas_call(
        pack_kernel,
        in_specs=[HBM] * 2,
        out_specs=[VMEM] * 3,
        out_shape=[
            jax.ShapeDtypeStruct((8, COLS + 128), F32),
            jax.ShapeDtypeStruct((ROWS, 128), F32),
            jax.ShapeDtypeStruct((ROWS, COLS), F32),
        ],
        scratch_shapes=[
            pltpu.VMEM((ROWS, COLS), jnp.int32),
            pltpu.VMEM((2, ROWS, U), F32),
            pltpu.SemaphoreType.DMA((2,)),
        ],
        compiler_params=params(4),
        name="pack",
    )(hbm(levels), hbm(rows_t))


def relay_kernel(from_x_ref, green_ref, out_ref):
    out_ref[:8, :] = from_x_ref[:, COLS - 128 : COLS]
    out_ref[8:, :] = green_ref[...]


def relay(from_x, green):
    return pl.pallas_call(
        relay_kernel,
        in_specs=[VMEM] * 2,
        out_specs=VMEM,
        out_shape=jax.ShapeDtypeStruct((8 + Z * HALO, 128), F32),
        compiler_params=params(4),
        name="relay",
    )(from_x, green)


def one_hot(row, level_ids):
    row = jnp.broadcast_to(row, level_ids.shape)
    return jnp.where(row == level_ids, 1.0, 0.0).astype(BF16)


def features(window, conv, conv_bias, mix, mix_bias):
    pre = jnp.dot(conv, window, preferred_element_type=F32) + conv_bias
    hidden = twice_gelu(pre).astype(BF16)
    mixed = jnp.dot(mix, hidden, preferred_element_type=F32) + mix_bias
    return twice_gelu(mixed).astype(BF16)


def lanes_from(x, count, offset):
    shape = (x.shape[1], count)
    move = (iota(shape, 1) == iota(shape, 0) + offset).astype(BF16)
    return jnp.dot(x, move, preferred_element_type=F32)


def bias_column(row):
    shape = (2 * HID, HID)
    own = iota(shape, 1) == iota(shape, 0) % HID
    return jnp.sum(jnp.where(own, row, 0.0), axis=1, keepdims=True)


def lay_out_decoder(dec_ref, out_ref):
    n = KS * CH * BLOCK
    row = iota((n, n), 0)
    source = row // 4 % BLOCK * (KS * CH) + row // (4 * BLOCK) * 4 + row % 4
    move = (iota((n, n), 1) == source).astype(BF16)
    dec = dec_ref[...].astype(F32)
    none = jnp.zeros((KS * CH, HID), F32)

    def column(pillar):
        taps = [r - pillar + KS - 1 for r in range(BLOCK)]
        return jnp.concatenate([dec[t] if 0 <= t < KS else none for t in taps], axis=0)

    for i in range(BLOCK):
        pair = jnp.concatenate([column(2 * i), column(2 * i + 1)], axis=1).astype(BF16)
        wide = jnp.dot(move, pair, preferred_element_type=F32)
        out_ref[:, 2 * i * HID : (2 * i + 2) * HID] = (0.5 * wide).astype(BF16)


def inner_kernel(
    lev_ref, table_hbm, cb_hbm, mix_hbm, mb_hbm, dec_hbm, cols_hbm,
    feat_ref, hi_ref, lo_ref, green_ref, conv_ref, cb_ref, mixer_ref, mb_ref, dec_ref,
    ext_ref, hot_ref, cols_ref, table_ref, cbr_ref, mix_ref, mbr_ref, raw_ref, sems,
):
    z = lax.axis_index("py")
    small = [
        pltpu.make_async_copy(table_hbm, table_ref, sems.at[Z]),
        pltpu.make_async_copy(cb_hbm, cbr_ref, sems.at[Z + 1]),
        pltpu.make_async_copy(mix_hbm, mix_ref, sems.at[Z + 2]),
        pltpu.make_async_copy(mb_hbm, mbr_ref, sems.at[Z + 3]),
        pltpu.make_async_copy(dec_hbm, raw_ref, sems.at[Z + 4]),
    ]
    copies = [
        pltpu.make_async_copy(cols_hbm.at[z ^ REL_ORDER[g]], cols_ref.at[g], sems.at[g])
        for g in range(Z)
    ]
    for copy in small + copies:
        copy.start()
    wide = COLS - 128
    lev = lev_ref[...]
    for b in range(3):
        ext_ref[b] = pltpu.roll(lev, 3 - b, 1)[:, 128:]
    level_ids = iota((LEVELS, wide), 0).astype(F32)

    def make_hot(q, _):
        for b in range(3):
            hot_ref[pl.ds(q * SLOT + b * LEVELS, LEVELS), :] = one_hot(
                ext_ref[b, pl.ds(q, 1), :], level_ids
            )
        return 0

    lax.fori_loop(0, ROWS - 2, make_hot, 0, unroll=2)
    for copy in small:
        copy.wait()
    conv_ref[:HID, :] = lanes_from(table_ref[...], WINDOW, 0).astype(BF16)
    conv_ref[HID:, :] = lanes_from(table_ref[...], WINDOW, SLOT).astype(BF16)
    mixer_ref[:HID, :] = (0.5 * lanes_from(mix_ref[...], 2 * HID, 0)).astype(BF16)
    mixer_ref[HID:, :] = (0.5 * lanes_from(mix_ref[...], 2 * HID, HID)).astype(BF16)
    cb_ref[...] = bias_column(cbr_ref[...])
    mb_ref[...] = bias_column(mbr_ref[...])
    lay_out_decoder(raw_ref, dec_ref)
    conv_bias = jnp.broadcast_to(cb_ref[...], (2 * HID, wide))
    mix_bias = jnp.broadcast_to(mb_ref[...], (2 * HID, wide))
    for i in range(ROWS // 2 - 2):
        at = (8 + 2 * i) * HID
        feat_ref[at : at + 2 * HID, 128:] = features(
            hot_ref[i * 2 * SLOT : i * 2 * SLOT + WINDOW, :],
            conv_ref[...], conv_bias, mixer_ref[...], mix_bias,
        )
    for copy in copies:
        copy.wait()

    def split(g, _):
        hi_ref[g], lo_ref[g] = split2(cols_ref[g].reshape(2 * V, COLS))
        return 0

    lax.fori_loop(0, Z, split, 0)
    for g in range(Z):
        edge = cols_ref[g, :, :, COLS - 128 :].reshape(2 * V, 128).T
        green_ref[HALO * g : HALO * (g + 1), :] = edge[128 - HALO :, :]


def inner(levels, table, conv_bias, mix, mix_bias, decoder, green_cols):
    wide = COLS - 128
    return pl.pallas_call(
        inner_kernel,
        in_specs=[VMEM] + [HBM] * 6,
        out_specs=[VMEM] * 9,
        out_shape=[
            jax.ShapeDtypeStruct((PILLAR_ROWS * HID, COLS), BF16),
            jax.ShapeDtypeStruct((Z, 2 * V, COLS), BF16),
            jax.ShapeDtypeStruct((Z, 2 * V, COLS), BF16),
            jax.ShapeDtypeStruct((Z * HALO, 128), F32),
            jax.ShapeDtypeStruct((2 * HID, WINDOW), BF16),
            jax.ShapeDtypeStruct((2 * HID, 1), F32),
            jax.ShapeDtypeStruct((2 * HID, 2 * HID), BF16),
            jax.ShapeDtypeStruct((2 * HID, 1), F32),
            jax.ShapeDtypeStruct((KS * CH * BLOCK, 2 * BLOCK * HID), BF16),
        ],
        scratch_shapes=[
            pltpu.VMEM((3, ROWS, wide), F32),
            pltpu.VMEM(((ROWS - 2) * SLOT, wide), BF16),
            pltpu.VMEM((Z, 2, V, COLS), F32),
            pltpu.VMEM(table.shape, BF16),
            pltpu.VMEM((1, HID), F32),
            pltpu.VMEM((HID, HID), BF16),
            pltpu.VMEM((1, HID), F32),
            pltpu.VMEM(decoder.shape, BF16),
            pltpu.SemaphoreType.DMA((Z + 5,)),
        ],
        compiler_params=params(16),
        name="inner",
    )(levels, *map(hbm, (
        table, conv_bias.reshape(1, HID), mix, mix_bias.reshape(1, HID), decoder, green_cols,
    )))


def tile_windows(left, tile, first_y, ext_ref):
    ext = jnp.concatenate([left, tile], axis=1)
    lane = iota(tile.shape, 1)
    for b in range(3):
        window = pltpu.roll(ext, 3 - b, 1)[:, 128:]
        if b != 1:
            window = jnp.where(first_y & (lane == (2 if b == 0 else 1)), -1.0, window)
        ext_ref[b] = window


def near_field(i, dec, feat_ref, nf_ref, edge_ref, first_y):
    lane = iota((1, COLS), 1)
    near = iota((1, 128), 1)
    at = i * BLOCK * HID
    taps = jnp.dot(dec, feat_ref[at : at + 2 * BLOCK * HID, :], preferred_element_type=F32)
    acc = jnp.zeros((2 * HALF, COLS), F32)
    edge = jnp.zeros((2 * HALF, 128), F32)
    for s in range(KS):
        part = taps[2 * HALF * s : 2 * HALF * (s + 1), :]
        k = KS - 1 - s
        ok = (lane < COLS - k) & ((lane + k >= 2) | jnp.logical_not(first_y))
        moved = part if k == 0 else pltpu.roll(part, COLS - k, 1)
        acc = acc + jnp.where(ok, moved, 0.0)
        ok = (near >= s) & (near < HALO) & ((near - s < 2) | jnp.logical_not(first_y))
        part = part[:, :128]
        moved = part if s == 0 else pltpu.roll(part, s, 1)
        edge = edge + jnp.where(ok, moved, 0.0)
    for part, values in enumerate(split2(acc)):
        for k in range(2):
            at = (2 * part + k) * PART + i * HALF
            nf_ref[at : at + HALF, :] = values[k * HALF : (k + 1) * HALF]
    for k in range(2):
        at = k * PART + i * HALF
        edge_ref[at : at + HALF, :] = edge[k * HALF : (k + 1) * HALF]


def middle_kernel(
    lev_ref, from_y_ref, conv_ref, cb_ref, mix_ref, mb_ref, dec_ref, _,
    nf_ref, edge_ref, feat_ref, ext_ref, hot_ref,
):
    first_y = lax.axis_index("py") == 0
    tile_windows(from_y_ref[...], lev_ref[:, :128], first_y, ext_ref)
    level_ids = iota((LEVELS, 128), 0).astype(F32)
    for q in range(ROWS - 2):
        for b in range(3):
            row = one_hot(ext_ref[b, q : q + 1, :], level_ids)
            for t in range(6):
                if 0 <= q - 2 * t < 4:
                    at = (q - 2 * t) * SLOT + b * LEVELS
                    hot_ref[at : at + LEVELS, t * 128 : (t + 1) * 128] = row
    tiles = features(hot_ref[...], conv_ref[...], cb_ref[...], mix_ref[...], mb_ref[...])
    for t in range(6):
        at = (8 + 2 * t) * HID
        feat_ref[at : at + 2 * HID, :128] = tiles[:, t * 128 : (t + 1) * 128]
    for i in (2, 3):
        near_field(i, dec_ref[...], feat_ref, nf_ref, edge_ref, first_y)


def middle(levels, from_y, conv_w, conv_b, mix_w, mix_b, dec_w, feat):
    return pl.pallas_call(
        middle_kernel,
        in_specs=[VMEM] * 8,
        out_specs=[VMEM] * 3,
        out_shape=[
            jax.ShapeDtypeStruct((4 * PART, COLS), BF16),
            jax.ShapeDtypeStruct((2 * PART, 128), F32),
            jax.ShapeDtypeStruct(feat.shape, BF16),
        ],
        input_output_aliases={7: 2},
        scratch_shapes=[pltpu.VMEM((3, ROWS, 128), F32), pltpu.VMEM((WINDOW, 768), BF16)],
        compiler_params=params(8),
        name="middle",
    )(levels, from_y, conv_w, conv_b, mix_w, mix_b, dec_w, feat)


def outer_kernel(
    lev_ref, from_x_ref, conv_ref, cb_ref, mix_ref, mb_ref, _, feat_ref, ext_ref, hot_ref
):
    first_x = lax.axis_index("px") == 0
    ext = jnp.concatenate([from_x_ref[:, :COLS], lev_ref[:8, :]], axis=0)
    for b in range(3):
        ext_ref[b] = pltpu.roll(ext, 3 - b, 1)[:, 128:]
    wide = COLS - 128
    level_ids = iota((LEVELS, wide), 0).astype(F32)
    for e in range(10):
        for b in range(3):
            at = e * SLOT + b * LEVELS
            hot_ref[at : at + LEVELS, :] = one_hot(ext_ref[b, e : e + 1, :], level_ids)
    conv_bias = jnp.broadcast_to(cb_ref[...], (2 * HID, wide))
    mix_bias = jnp.broadcast_to(mb_ref[...], (2 * HID, wide))
    for w in range(4):
        at = 2 * w * HID
        conv = cut_conv(conv_ref[...], first_x) if w == 3 else conv_ref[...]
        feat_ref[at : at + 2 * HID, 128:] = features(
            hot_ref[2 * w * SLOT : 2 * w * SLOT + WINDOW, :],
            conv, conv_bias, mix_ref[...], mix_bias,
        )


def cut_conv(conv, first_x):
    slot = iota((2 * HID, WINDOW), 1) // SLOT
    row = iota((2 * HID, WINDOW), 0) // HID
    keep = jnp.where(first_x & (slot + row == 2) & (slot > 0), 0.0, 1.0)
    return conv * keep.astype(BF16)


def outer(levels, from_x, conv_w, conv_b, mix_w, mix_b, feat):
    wide = COLS - 128
    return pl.pallas_call(
        outer_kernel,
        in_specs=[VMEM] * 7,
        out_specs=VMEM,
        out_shape=jax.ShapeDtypeStruct(feat.shape, BF16),
        input_output_aliases={6: 0},
        scratch_shapes=[
            pltpu.VMEM((3, 16, wide), F32),
            pltpu.VMEM((10 * SLOT, wide), BF16),
        ],
        compiler_params=params(8),
        name="outer",
    )(levels, from_x, conv_w, conv_b, mix_w, mix_b, feat)


def column_sum(hi_ref, lo_ref, nf_ref, edge_ref, from_d_ref, out_ref, first, count):
    iy = lax.axis_index("py")
    before = (iy + lax.axis_size("py") - 1) % lax.axis_size("py")
    n = 2 * PART
    sign = jnp.where(iota((1, 128), 1) < V, -1.0, 1.0)
    hi = hi_ref[first : first + count].reshape(2 * V * count, COLS)
    lo = lo_ref[first : first + count].reshape(2 * V * count, COLS)
    both = lax.dot_general(hi, nf_ref[...], NT, preferred_element_type=F32)
    both = both[:, :n] + both[:, n:]
    both = both + lax.dot_general(lo, nf_ref[:n, :], NT, preferred_element_type=F32)
    greens = []
    for g in range(count):
        rel = (iy ^ REL_ORDER[first + g]) ^ before
        at = 8 + HALO * (rel // 2 + 4 * (rel % 2))
        greens.append(from_d_ref[pl.ds(at, HALO), :])
    green = jnp.concatenate(greens, axis=1)
    green = jnp.concatenate([green, jnp.zeros((4, 2 * V * count), F32)], axis=0)
    edge = jnp.dot(edge_ref[:, :8], green, precision=HIGH, preferred_element_type=F32)
    for g in range(count):
        at = 2 * V * g
        out = both[at : at + 2 * V].T + edge[:, at : at + 2 * V]
        out_ref[g] = out[:PART] + sign * pltpu.roll(out[PART:], V, 1)


def field_kernel(
    lev_ref, from_x_ref, from_y_ref, from_d_ref, conv_ref, cb_ref, mix_ref, mb_ref, dec_ref,
    hi_ref, lo_ref, _nf, _edge, _feat, send_ref, nf_ref, edge_ref, feat_ref, ext_ref, hot_ref,
):
    first_x = lax.axis_index("px") == 0
    first_y = lax.axis_index("py") == 0
    tile = jnp.concatenate([from_x_ref[:, :128], lev_ref[:8, :128]], axis=0)
    left = jnp.concatenate([from_d_ref[:8, :], from_y_ref[:8, :]], axis=0)
    tile_windows(left, tile, first_y, ext_ref)
    level_ids = iota((LEVELS, 128), 0).astype(F32)
    for w in range(4):
        for o in range(4):
            for b in range(3):
                e = 2 * w + o
                at = o * SLOT + b * LEVELS
                hot_ref[at : at + LEVELS, w * 128 : (w + 1) * 128] = one_hot(
                    ext_ref[b, e : e + 1, :], level_ids
                )
    tiles = features(
        hot_ref[:, :384], conv_ref[...], cb_ref[...], mix_ref[...], mb_ref[...]
    )
    for w in range(3):
        feat_ref[2 * w * HID : (2 * w + 2) * HID, :128] = tiles[:, w * 128 : (w + 1) * 128]
    feat_ref[6 * HID : 8 * HID, :128] = features(
        hot_ref[:, 384:], cut_conv(conv_ref[...], first_x), cb_ref[...], mix_ref[...], mb_ref[...]
    )

    shape = (KS * CH * BLOCK, 2 * BLOCK * HID)
    sample = iota(shape, 0) // 4 % BLOCK - SHIFT
    pillar = iota(shape, 1) // HID - SHIFT - 2
    for i in range(2):
        at = i * BLOCK
        apart = (sample + at >= 0) != (pillar + at >= 0)
        keep = jnp.where(first_x & apart, 0.0, 1.0)
        near_field(i, dec_ref[...] * keep.astype(BF16), feat_ref, nf_ref, edge_ref, first_y)

    column_sum(hi_ref, lo_ref, nf_ref, edge_ref, from_d_ref, send_ref, 4, 4)


def field(
    levels, from_x, from_y, from_d, conv_w, conv_b, mix_w, mix_b, dec_w, hi, lo, nf, edge, feat
):
    return pl.pallas_call(
        field_kernel,
        in_specs=[VMEM] * 14,
        out_specs=[VMEM] * 4,
        out_shape=[
            jax.ShapeDtypeStruct((4, PART, 128), F32),
            jax.ShapeDtypeStruct((4 * PART, COLS), BF16),
            jax.ShapeDtypeStruct((2 * PART, 128), F32),
            jax.ShapeDtypeStruct(feat.shape, BF16),
        ],
        input_output_aliases={11: 1, 12: 2, 13: 3},
        scratch_shapes=[
            pltpu.VMEM((3, 16, 128), F32),
            pltpu.VMEM((WINDOW, 512), BF16),
        ],
        compiler_params=params(12),
        name="field",
    )(
        levels, from_x, from_y, from_d, conv_w, conv_b, mix_w, mix_b, dec_w, hi, lo, nf, edge, feat
    )


def keep_planes(hi, lo, nf, edge, from_d, first, count):
    def keep_kernel(hi_ref, lo_ref, nf_ref, edge_ref, from_d_ref, out_ref):
        column_sum(hi_ref, lo_ref, nf_ref, edge_ref, from_d_ref, out_ref, first, count)

    return pl.pallas_call(
        keep_kernel,
        in_specs=[VMEM] * 5,
        out_specs=VMEM,
        out_shape=jax.ShapeDtypeStruct((count, PART, 128), F32),
        compiler_params=params(8),
        name="keep_planes",
    )(hi, lo, nf, edge, from_d)


def rows_kernel(from_x_ref, rows_ref, order_ref, out_ref):
    z = lax.axis_index("py")
    green = jnp.concatenate([rows_ref[z, 0], rows_ref[z, 1]], axis=1)
    green = jnp.concatenate([from_x_ref[:, COLS:], green], axis=0)
    n = ROWS + 8
    green = jnp.concatenate(split2(green), axis=0)
    pick = (order_ref[...] == iota((U, U), 0)).astype(BF16)
    copies = (iota((U, U * 4), 1) // 4 == iota((U, U * 4), 0)).astype(BF16)
    pick = jnp.dot(pick, copies, preferred_element_type=F32).astype(BF16)
    row = iota((3 * PART, 2 * n), 0)
    source = (row % PART) // 4 + (8 - SHIFT) + jnp.where(row // PART == 1, n, 0)
    spread = (iota((3 * PART, 2 * n), 1) == source).astype(BF16)
    mask = iota((3 * PART, U * 4), 0) % 4 == iota((3 * PART, U * 4), 1) % 4
    for j in range(2):
        ordered = jnp.dot(green[:, j * U : (j + 1) * U], pick, preferred_element_type=F32)
        wide = jnp.dot(spread, ordered.astype(BF16), preferred_element_type=F32)
        out_ref[j * U * 4 : (j + 1) * U * 4, :] = jnp.where(mask, wide, 0.0).T.astype(BF16)


def row_factors(from_x, rows_t, order):
    return pl.pallas_call(
        rows_kernel,
        in_specs=[VMEM] * 3,
        out_specs=VMEM,
        out_shape=jax.ShapeDtypeStruct((2 * U * 4, 3 * PART), BF16),
        compiler_params=params(4),
        name="row_factors",
    )(from_x, rows_t, order)


def focal_kernel(factor_ref, keep_ref, got_ref, b_ref, c_ref, d_ref, out_ref):
    t = ((keep_ref[0] + got_ref[0]) + b_ref[...]) + (c_ref[...] + d_ref[...])
    hi, lo = split2(t)
    out = jnp.dot(
        factor_ref[...], jnp.concatenate([hi, hi, lo], axis=0), preferred_element_type=F32
    )
    n = U * 4
    sign = jnp.where(iota((1, 128), 1) < V, -1.0, 1.0)
    out_ref[...] = (out[:n] + sign * pltpu.roll(out[n:], V, 1)).reshape(out_ref.shape)


def focal_share(factors, keep, got, b, c, d):
    return pl.pallas_call(
        focal_kernel,
        in_specs=[VMEM] * 6,
        out_specs=VMEM,
        out_shape=jax.ShapeDtypeStruct((U // 2, 8, 128), F32),
        compiler_params=params(4),
        name="focal_share",
    )(factors, keep, got, b, c, d)


def total_kernel(x_ref, out_ref):
    s = jnp.sum(x_ref[...], axis=0)
    for u in range(2):
        for k in range(2):
            for p in range(4):
                at = (k * 4 + p) * V
                row = u * 4 + p
                out_ref[0, u : u + 1, at : at + V] = s[row : row + 1, k * V : (k + 1) * V]


def total(parts):
    return pl.pallas_call(
        total_kernel,
        in_specs=[VMEM],
        out_specs=VMEM,
        out_shape=jax.ShapeDtypeStruct((1, 2, 8 * V), F32),
        compiler_params=params(4),
        name="total",
    )(parts)


def on_device(
    levels, conv_table, conv_bias, mix_weight, mix_bias, decoder, green_rows, green_cols, focal_order
):
    count_px = lax.axis_size("px")
    count_py = lax.axis_size("py")
    rows_t = jnp.swapaxes(green_rows, 2, 3)
    next_x = [(i, (i + 1) % count_px) for i in range(count_px)]
    next_y = [(i, (i + 1) % count_py) for i in range(count_py)]
    order = focal_order.reshape(1, U)

    to_x, to_y, levels = pack(levels, rows_t)
    from_x = lax.ppermute(to_x, "px", next_x)
    from_y = lax.ppermute(to_y, "py", next_y)
    feat, hi, lo, green, conv_w, conv_b, mix_w, mix_b, dec_w = inner(
        levels, conv_table, conv_bias, mix_weight, mix_bias, decoder, green_cols
    )
    from_y, feat = lax.optimization_barrier((from_y, feat))
    nf, edge, feat = middle(levels, from_y, conv_w, conv_b, mix_w, mix_b, dec_w, feat)
    from_x, feat, nf, edge = lax.optimization_barrier((from_x, feat, nf, edge))
    from_d = lax.ppermute(relay(from_x, green), "py", next_y)
    feat = outer(levels, from_x, conv_w, conv_b, mix_w, mix_b, feat)
    send, nf, edge, _ = field(
        levels, from_x, from_y, from_d, conv_w, conv_b, mix_w, mix_b, dec_w, hi, lo, nf, edge, feat
    )

    def swap(x, mask):
        return lax.ppermute(x, "py", [(i, i ^ mask) for i in range(count_py)])

    got = swap(send, 1)
    keep = keep_planes(hi, lo, nf, edge, from_d, 1, 3)
    b, c, d = (swap(keep[i - 1] + got[i], 2 * i) for i in (3, 2, 1))
    keep = keep_planes(hi, lo, nf, edge, from_d, 0, 1)
    factors = row_factors(from_x, rows_t, order)
    share = focal_share(factors, keep, got, b, c, d)
    return total(lax.all_to_all(share, "px", 0, 0))


def solution(mesh):
    return jax.shard_map(
        on_device,
        mesh=mesh,
        in_specs=(
            P("px", "py"),
            P(),
            P(),
            P(),
            P(),
            P(),
            P(None, None, None, "px"),
            P(None, None, None, "py"),
            P(),
        ),
        out_specs=P("py", "px", None),
        check_vma=False,
    )
```

```python
import jax
import jax.numpy as jnp
from jax import lax
from jax.experimental import pallas as pl
from jax.experimental.pallas import tpu as pltpu
from jax.sharding import PartitionSpec as P

HIGH = lax.Precision.HIGHEST
F32 = jnp.float32
BF16 = jnp.bfloat16
NT = (((1,), (1,)), ((), ()))
TN = (((0,), (0,)), ((), ()))

ROWS = 16
COLS = 1024
HID = 64
LEVELS = 16
CH = 8
KS = 5
Z = 8
U = 64
V = 64
HALO = 4
SHIFT = 5
PILLAR_ROWS = ROWS + KS - 1
SLOT = 3 * LEVELS
WINDOW = 4 * SLOT
BLOCK = 4
REL_ORDER = (0, 2, 4, 6, 1, 3, 5, 7)
PART = ROWS * CH // 2
HALF = BLOCK * CH // 2
VMEM = pl.BlockSpec(memory_space=pltpu.VMEM)
HBM = pl.BlockSpec(memory_space=pltpu.HBM)


def params(mib):
    return pltpu.CompilerParams(vmem_limit_bytes=mib << 20)

GELU_A = 0.7978845608028654
GELU_B = GELU_A * 0.044715


def iota(shape, dim):
    return lax.broadcasted_iota(jnp.int32, shape, dim)


def twice_gelu(x):
    return x + x * jnp.tanh(x * (GELU_A + GELU_B * (x * x)))


def split2(x):
    hi = x.astype(BF16)
    return hi, (x - hi.astype(F32)).astype(BF16)


def hbm(x):
    return pltpu.with_memory_space_constraint(x, pltpu.HBM)


def pack_kernel(lev_hbm, rows_hbm, to_x_ref, to_y_ref, out_ref, lev_ref, rows_ref, sems):
    z = lax.axis_index("py")
    copies = [
        pltpu.make_async_copy(lev_hbm, lev_ref, sems.at[0]),
        pltpu.make_async_copy(rows_hbm.at[z], rows_ref, sems.at[1]),
    ]
    for copy in copies:
        copy.start()
    for copy in copies:
        copy.wait()
    lev = lev_ref[...].astype(F32)
    out_ref[...] = lev
    to_x_ref[:, :COLS] = lev[8:, :]
    to_x_ref[:, COLS:] = jnp.concatenate([rows_ref[0, 8:, :], rows_ref[1, 8:, :]], axis=1)
    to_y_ref[...] = lev[:, COLS - 128 :]


def pack(levels, rows_t):
    return pl.pallas_call(
        pack_kernel,
        in_specs=[HBM] * 2,
        out_specs=[VMEM] * 3,
        out_shape=[
            jax.ShapeDtypeStruct((8, COLS + 128), F32),
            jax.ShapeDtypeStruct((ROWS, 128), F32),
            jax.ShapeDtypeStruct((ROWS, COLS), F32),
        ],
        scratch_shapes=[
            pltpu.VMEM((ROWS, COLS), jnp.int32),
            pltpu.VMEM((2, ROWS, U), F32),
            pltpu.SemaphoreType.DMA((2,)),
        ],
        compiler_params=params(4),
        name="pack",
    )(hbm(levels), hbm(rows_t))


def relay_kernel(from_x_ref, green_ref, out_ref):
    out_ref[:8, :] = from_x_ref[:, COLS - 128 : COLS]
    out_ref[8:, :] = green_ref[...]


def relay(from_x, green):
    return pl.pallas_call(
        relay_kernel,
        in_specs=[VMEM] * 2,
        out_specs=VMEM,
        out_shape=jax.ShapeDtypeStruct((8 + Z * HALO, 128), F32),
        compiler_params=params(4),
        name="relay",
    )(from_x, green)


def one_hot(row, level_ids):
    row = jnp.broadcast_to(row, level_ids.shape)
    return jnp.where(row == level_ids, 1.0, 0.0).astype(BF16)


def features(window, conv, conv_bias, mix, mix_bias):
    pre = jnp.dot(conv, window, preferred_element_type=F32) + conv_bias
    hidden = twice_gelu(pre).astype(BF16)
    mixed = jnp.dot(mix, hidden, preferred_element_type=F32) + mix_bias
    return twice_gelu(mixed).astype(BF16)


def lanes_from(x, count, offset):
    shape = (x.shape[1], count)
    move = (iota(shape, 1) == iota(shape, 0) + offset).astype(BF16)
    return jnp.dot(x, move, preferred_element_type=F32)


def bias_column(row):
    shape = (2 * HID, HID)
    own = iota(shape, 1) == iota(shape, 0) % HID
    return jnp.sum(jnp.where(own, row, 0.0), axis=1, keepdims=True)


def lay_out_decoder(dec_ref, out_ref):
    n = KS * CH * BLOCK
    row = iota((n, n), 0)
    source = row // 4 % BLOCK * (KS * CH) + row // (4 * BLOCK) * 4 + row % 4
    move = (iota((n, n), 1) == source).astype(BF16)
    dec = dec_ref[...].astype(F32)
    none = jnp.zeros((KS * CH, HID), F32)

    def column(pillar):
        taps = [r - pillar + KS - 1 for r in range(BLOCK)]
        return jnp.concatenate([dec[t] if 0 <= t < KS else none for t in taps], axis=0)

    for i in range(BLOCK):
        pair = jnp.concatenate([column(2 * i), column(2 * i + 1)], axis=1).astype(BF16)
        wide = jnp.dot(move, pair, preferred_element_type=F32)
        out_ref[:, 2 * i * HID : (2 * i + 2) * HID] = (0.5 * wide).astype(BF16)


def inner_kernel(
    lev_ref, table_hbm, cb_hbm, mix_hbm, mb_hbm, dec_hbm, cols_hbm,
    feat_ref, hi_ref, lo_ref, green_ref, conv_ref, cb_ref, mixer_ref, mb_ref, dec_ref,
    ext_ref, hot_ref, cols_ref, table_ref, cbr_ref, mix_ref, mbr_ref, raw_ref, sems,
):
    z = lax.axis_index("py")
    small = [
        pltpu.make_async_copy(table_hbm, table_ref, sems.at[Z]),
        pltpu.make_async_copy(cb_hbm, cbr_ref, sems.at[Z + 1]),
        pltpu.make_async_copy(mix_hbm, mix_ref, sems.at[Z + 2]),
        pltpu.make_async_copy(mb_hbm, mbr_ref, sems.at[Z + 3]),
        pltpu.make_async_copy(dec_hbm, raw_ref, sems.at[Z + 4]),
    ]
    copies = [
        pltpu.make_async_copy(cols_hbm.at[z ^ REL_ORDER[g]], cols_ref.at[g], sems.at[g])
        for g in range(Z)
    ]
    for copy in small + copies:
        copy.start()
    wide = COLS - 128
    lev = lev_ref[...]
    for b in range(3):
        ext_ref[b] = pltpu.roll(lev, 3 - b, 1)[:, 128:]
    level_ids = iota((LEVELS, wide), 0).astype(F32)

    def make_hot(q, _):
        for b in range(3):
            hot_ref[pl.ds(q * SLOT + b * LEVELS, LEVELS), :] = one_hot(
                ext_ref[b, pl.ds(q, 1), :], level_ids
            )
        return 0

    lax.fori_loop(0, ROWS - 2, make_hot, 0, unroll=2)
    for copy in small:
        copy.wait()
    conv_ref[:HID, :] = lanes_from(table_ref[...], WINDOW, 0).astype(BF16)
    conv_ref[HID:, :] = lanes_from(table_ref[...], WINDOW, SLOT).astype(BF16)
    mixer_ref[:HID, :] = (0.5 * lanes_from(mix_ref[...], 2 * HID, 0)).astype(BF16)
    mixer_ref[HID:, :] = (0.5 * lanes_from(mix_ref[...], 2 * HID, HID)).astype(BF16)
    cb_ref[...] = bias_column(cbr_ref[...])
    mb_ref[...] = bias_column(mbr_ref[...])
    lay_out_decoder(raw_ref, dec_ref)
    conv_bias = jnp.broadcast_to(cb_ref[...], (2 * HID, wide))
    mix_bias = jnp.broadcast_to(mb_ref[...], (2 * HID, wide))
    for i in range(ROWS // 2 - 2):
        at = (8 + 2 * i) * HID
        feat_ref[at : at + 2 * HID, 128:] = features(
            hot_ref[i * 2 * SLOT : i * 2 * SLOT + WINDOW, :],
            conv_ref[...], conv_bias, mixer_ref[...], mix_bias,
        )
    for copy in copies:
        copy.wait()

    def split(g, _):
        hi_ref[g], lo_ref[g] = split2(cols_ref[g].reshape(2 * V, COLS))
        return 0

    lax.fori_loop(0, Z, split, 0)
    for g in range(Z):
        edge = cols_ref[g, :, :, COLS - 128 :].reshape(2 * V, 128).T
        green_ref[HALO * g : HALO * (g + 1), :] = edge[128 - HALO :, :]


def inner(levels, table, conv_bias, mix, mix_bias, decoder, green_cols):
    wide = COLS - 128
    return pl.pallas_call(
        inner_kernel,
        in_specs=[VMEM] + [HBM] * 6,
        out_specs=[VMEM] * 9,
        out_shape=[
            jax.ShapeDtypeStruct((PILLAR_ROWS * HID, COLS), BF16),
            jax.ShapeDtypeStruct((Z, 2 * V, COLS), BF16),
            jax.ShapeDtypeStruct((Z, 2 * V, COLS), BF16),
            jax.ShapeDtypeStruct((Z * HALO, 128), F32),
            jax.ShapeDtypeStruct((2 * HID, WINDOW), BF16),
            jax.ShapeDtypeStruct((2 * HID, 1), F32),
            jax.ShapeDtypeStruct((2 * HID, 2 * HID), BF16),
            jax.ShapeDtypeStruct((2 * HID, 1), F32),
            jax.ShapeDtypeStruct((KS * CH * BLOCK, 2 * BLOCK * HID), BF16),
        ],
        scratch_shapes=[
            pltpu.VMEM((3, ROWS, wide), F32),
            pltpu.VMEM(((ROWS - 2) * SLOT, wide), BF16),
            pltpu.VMEM((Z, 2, V, COLS), F32),
            pltpu.VMEM(table.shape, BF16),
            pltpu.VMEM((1, HID), F32),
            pltpu.VMEM((HID, HID), BF16),
            pltpu.VMEM((1, HID), F32),
            pltpu.VMEM(decoder.shape, BF16),
            pltpu.SemaphoreType.DMA((Z + 5,)),
        ],
        compiler_params=params(16),
        name="inner",
    )(levels, *map(hbm, (
        table, conv_bias.reshape(1, HID), mix, mix_bias.reshape(1, HID), decoder, green_cols,
    )))


def tile_windows(left, tile, first_y, ext_ref):
    ext = jnp.concatenate([left, tile], axis=1)
    lane = iota(tile.shape, 1)
    for b in range(3):
        window = pltpu.roll(ext, 3 - b, 1)[:, 128:]
        if b != 1:
            window = jnp.where(first_y & (lane == (2 if b == 0 else 1)), -1.0, window)
        ext_ref[b] = window


def near_field(i, dec, feat_ref, nf_ref, edge_ref, first_y):
    lane = iota((1, COLS), 1)
    near = iota((1, 128), 1)
    at = i * BLOCK * HID
    taps = jnp.dot(dec, feat_ref[at : at + 2 * BLOCK * HID, :], preferred_element_type=F32)
    acc = jnp.zeros((2 * HALF, COLS), F32)
    edge = jnp.zeros((2 * HALF, 128), F32)
    for s in range(KS):
        part = taps[2 * HALF * s : 2 * HALF * (s + 1), :]
        k = KS - 1 - s
        ok = (lane < COLS - k) & ((lane + k >= 2) | jnp.logical_not(first_y))
        moved = part if k == 0 else pltpu.roll(part, COLS - k, 1)
        acc = acc + jnp.where(ok, moved, 0.0)
        ok = (near >= s) & (near < HALO) & ((near - s < 2) | jnp.logical_not(first_y))
        part = part[:, :128]
        moved = part if s == 0 else pltpu.roll(part, s, 1)
        edge = edge + jnp.where(ok, moved, 0.0)
    for part, values in enumerate(split2(acc)):
        for k in range(2):
            at = (2 * part + k) * PART + i * HALF
            nf_ref[at : at + HALF, :] = values[k * HALF : (k + 1) * HALF]
    for k in range(2):
        at = k * PART + i * HALF
        edge_ref[at : at + HALF, :] = edge[k * HALF : (k + 1) * HALF]


def middle_kernel(
    lev_ref, from_y_ref, conv_ref, cb_ref, mix_ref, mb_ref, _, feat_ref, ext_ref, hot_ref
):
    first_y = lax.axis_index("py") == 0
    tile_windows(from_y_ref[...], lev_ref[:, :128], first_y, ext_ref)
    level_ids = iota((LEVELS, 128), 0).astype(F32)
    for q in range(ROWS - 2):
        for b in range(3):
            row = one_hot(ext_ref[b, q : q + 1, :], level_ids)
            for t in range(6):
                if 0 <= q - 2 * t < 4:
                    at = (q - 2 * t) * SLOT + b * LEVELS
                    hot_ref[at : at + LEVELS, t * 128 : (t + 1) * 128] = row
    tiles = features(hot_ref[...], conv_ref[...], cb_ref[...], mix_ref[...], mb_ref[...])
    for t in range(6):
        at = (8 + 2 * t) * HID
        feat_ref[at : at + 2 * HID, :128] = tiles[:, t * 128 : (t + 1) * 128]


def middle(levels, from_y, conv_w, conv_b, mix_w, mix_b, feat):
    return pl.pallas_call(
        middle_kernel,
        in_specs=[VMEM] * 7,
        out_specs=VMEM,
        out_shape=jax.ShapeDtypeStruct(feat.shape, BF16),
        input_output_aliases={6: 0},
        scratch_shapes=[pltpu.VMEM((3, ROWS, 128), F32), pltpu.VMEM((WINDOW, 768), BF16)],
        compiler_params=params(8),
        name="middle",
    )(levels, from_y, conv_w, conv_b, mix_w, mix_b, feat)


def outer_kernel(
    lev_ref, from_x_ref, conv_ref, cb_ref, mix_ref, mb_ref, dec_ref, _,
    nf_ref, edge_ref, feat_ref, ext_ref, hot_ref,
):
    first_x = lax.axis_index("px") == 0
    ext = jnp.concatenate([from_x_ref[:, :COLS], lev_ref[:8, :]], axis=0)
    for b in range(3):
        ext_ref[b] = pltpu.roll(ext, 3 - b, 1)[:, 128:]
    wide = COLS - 128
    level_ids = iota((LEVELS, wide), 0).astype(F32)
    for e in range(10):
        for b in range(3):
            at = e * SLOT + b * LEVELS
            hot_ref[at : at + LEVELS, :] = one_hot(ext_ref[b, e : e + 1, :], level_ids)
    conv_bias = jnp.broadcast_to(cb_ref[...], (2 * HID, wide))
    mix_bias = jnp.broadcast_to(mb_ref[...], (2 * HID, wide))
    for w in range(4):
        at = 2 * w * HID
        conv = cut_conv(conv_ref[...], first_x) if w == 3 else conv_ref[...]
        feat_ref[at : at + 2 * HID, 128:] = features(
            hot_ref[2 * w * SLOT : 2 * w * SLOT + WINDOW, :],
            conv, conv_bias, mix_ref[...], mix_bias,
        )
    for i in (2, 3):
        near_field(i, dec_ref[...], feat_ref, nf_ref, edge_ref, lax.axis_index("py") == 0)


def cut_conv(conv, first_x):
    slot = iota((2 * HID, WINDOW), 1) // SLOT
    row = iota((2 * HID, WINDOW), 0) // HID
    keep = jnp.where(first_x & (slot + row == 2) & (slot > 0), 0.0, 1.0)
    return conv * keep.astype(BF16)


def outer(levels, from_x, conv_w, conv_b, mix_w, mix_b, dec_w, feat):
    wide = COLS - 128
    return pl.pallas_call(
        outer_kernel,
        in_specs=[VMEM] * 8,
        out_specs=[VMEM] * 3,
        out_shape=[
            jax.ShapeDtypeStruct((4 * PART, COLS), BF16),
            jax.ShapeDtypeStruct((2 * PART, 128), F32),
            jax.ShapeDtypeStruct(feat.shape, BF16),
        ],
        input_output_aliases={7: 2},
        scratch_shapes=[
            pltpu.VMEM((3, 16, wide), F32),
            pltpu.VMEM((10 * SLOT, wide), BF16),
        ],
        compiler_params=params(8),
        name="outer",
    )(levels, from_x, conv_w, conv_b, mix_w, mix_b, dec_w, feat)


def column_sum(hi_ref, lo_ref, nf_ref, edge_ref, from_d_ref, out_ref, first, count):
    iy = lax.axis_index("py")
    before = (iy + lax.axis_size("py") - 1) % lax.axis_size("py")
    n = 2 * PART
    sign = jnp.where(iota((1, 128), 1) < V, -1.0, 1.0)
    hi = hi_ref[first : first + count].reshape(2 * V * count, COLS)
    lo = lo_ref[first : first + count].reshape(2 * V * count, COLS)
    both = lax.dot_general(hi, nf_ref[...], NT, preferred_element_type=F32)
    both = both[:, :n] + both[:, n:]
    both = both + lax.dot_general(lo, nf_ref[:n, :], NT, preferred_element_type=F32)
    greens = []
    for g in range(count):
        rel = (iy ^ REL_ORDER[first + g]) ^ before
        at = 8 + HALO * (rel // 2 + 4 * (rel % 2))
        greens.append(from_d_ref[pl.ds(at, HALO), :])
    green = jnp.concatenate(greens, axis=1)
    green = jnp.concatenate([green, jnp.zeros((4, 2 * V * count), F32)], axis=0)
    edge = jnp.dot(edge_ref[:, :8], green, precision=HIGH, preferred_element_type=F32)
    for g in range(count):
        at = 2 * V * g
        out = both[at : at + 2 * V].T + edge[:, at : at + 2 * V]
        out_ref[g] = out[:PART] + sign * pltpu.roll(out[PART:], V, 1)


def field_kernel(
    lev_ref, from_x_ref, from_y_ref, from_d_ref, conv_ref, cb_ref, mix_ref, mb_ref, dec_ref,
    hi_ref, lo_ref, _nf, _edge, _feat, send_ref, nf_ref, edge_ref, feat_ref, ext_ref, hot_ref,
):
    first_x = lax.axis_index("px") == 0
    first_y = lax.axis_index("py") == 0
    tile = jnp.concatenate([from_x_ref[:, :128], lev_ref[:8, :128]], axis=0)
    left = jnp.concatenate([from_d_ref[:8, :], from_y_ref[:8, :]], axis=0)
    tile_windows(left, tile, first_y, ext_ref)
    level_ids = iota((LEVELS, 128), 0).astype(F32)
    for w in range(4):
        for o in range(4):
            for b in range(3):
                e = 2 * w + o
                at = o * SLOT + b * LEVELS
                hot_ref[at : at + LEVELS, w * 128 : (w + 1) * 128] = one_hot(
                    ext_ref[b, e : e + 1, :], level_ids
                )
    tiles = features(
        hot_ref[:, :384], conv_ref[...], cb_ref[...], mix_ref[...], mb_ref[...]
    )
    for w in range(3):
        feat_ref[2 * w * HID : (2 * w + 2) * HID, :128] = tiles[:, w * 128 : (w + 1) * 128]
    feat_ref[6 * HID : 8 * HID, :128] = features(
        hot_ref[:, 384:], cut_conv(conv_ref[...], first_x), cb_ref[...], mix_ref[...], mb_ref[...]
    )

    shape = (KS * CH * BLOCK, 2 * BLOCK * HID)
    sample = iota(shape, 0) // 4 % BLOCK - SHIFT
    pillar = iota(shape, 1) // HID - SHIFT - 2
    for i in range(2):
        at = i * BLOCK
        apart = (sample + at >= 0) != (pillar + at >= 0)
        keep = jnp.where(first_x & apart, 0.0, 1.0)
        near_field(i, dec_ref[...] * keep.astype(BF16), feat_ref, nf_ref, edge_ref, first_y)

    column_sum(hi_ref, lo_ref, nf_ref, edge_ref, from_d_ref, send_ref, 4, 4)


def field(
    levels, from_x, from_y, from_d, conv_w, conv_b, mix_w, mix_b, dec_w, hi, lo, nf, edge, feat
):
    return pl.pallas_call(
        field_kernel,
        in_specs=[VMEM] * 14,
        out_specs=[VMEM] * 4,
        out_shape=[
            jax.ShapeDtypeStruct((4, PART, 128), F32),
            jax.ShapeDtypeStruct((4 * PART, COLS), BF16),
            jax.ShapeDtypeStruct((2 * PART, 128), F32),
            jax.ShapeDtypeStruct(feat.shape, BF16),
        ],
        input_output_aliases={11: 1, 12: 2, 13: 3},
        scratch_shapes=[
            pltpu.VMEM((3, 16, 128), F32),
            pltpu.VMEM((WINDOW, 512), BF16),
        ],
        compiler_params=params(12),
        name="field",
    )(
        levels, from_x, from_y, from_d, conv_w, conv_b, mix_w, mix_b, dec_w, hi, lo, nf, edge, feat
    )


def keep_planes(hi, lo, nf, edge, from_d, first, count):
    def keep_kernel(hi_ref, lo_ref, nf_ref, edge_ref, from_d_ref, out_ref):
        column_sum(hi_ref, lo_ref, nf_ref, edge_ref, from_d_ref, out_ref, first, count)

    return pl.pallas_call(
        keep_kernel,
        in_specs=[VMEM] * 5,
        out_specs=VMEM,
        out_shape=jax.ShapeDtypeStruct((count, PART, 128), F32),
        compiler_params=params(8),
        name="keep_planes",
    )(hi, lo, nf, edge, from_d)


def rows_kernel(from_x_ref, rows_ref, order_ref, out_ref):
    z = lax.axis_index("py")
    green = jnp.concatenate([rows_ref[z, 0], rows_ref[z, 1]], axis=1)
    green = jnp.concatenate([from_x_ref[:, COLS:], green], axis=0)
    n = ROWS + 8
    green = jnp.concatenate(split2(green), axis=0)
    pick = (order_ref[...] == iota((U, U), 0)).astype(BF16)
    copies = (iota((U, U * 4), 1) // 4 == iota((U, U * 4), 0)).astype(BF16)
    pick = jnp.dot(pick, copies, preferred_element_type=F32).astype(BF16)
    row = iota((3 * PART, 2 * n), 0)
    source = (row % PART) // 4 + (8 - SHIFT) + jnp.where(row // PART == 1, n, 0)
    spread = (iota((3 * PART, 2 * n), 1) == source).astype(BF16)
    mask = iota((3 * PART, U * 4), 0) % 4 == iota((3 * PART, U * 4), 1) % 4
    for j in range(2):
        ordered = jnp.dot(green[:, j * U : (j + 1) * U], pick, preferred_element_type=F32)
        wide = jnp.dot(spread, ordered.astype(BF16), preferred_element_type=F32)
        out_ref[j * U * 4 : (j + 1) * U * 4, :] = jnp.where(mask, wide, 0.0).T.astype(BF16)


def row_factors(from_x, rows_t, order):
    return pl.pallas_call(
        rows_kernel,
        in_specs=[VMEM] * 3,
        out_specs=VMEM,
        out_shape=jax.ShapeDtypeStruct((2 * U * 4, 3 * PART), BF16),
        compiler_params=params(4),
        name="row_factors",
    )(from_x, rows_t, order)


def focal_kernel(factor_ref, keep_ref, got_ref, b_ref, c_ref, d_ref, out_ref):
    t = ((keep_ref[0] + got_ref[0]) + b_ref[...]) + (c_ref[...] + d_ref[...])
    hi, lo = split2(t)
    out = jnp.dot(
        factor_ref[...], jnp.concatenate([hi, hi, lo], axis=0), preferred_element_type=F32
    )
    n = U * 4
    sign = jnp.where(iota((1, 128), 1) < V, -1.0, 1.0)
    out_ref[...] = (out[:n] + sign * pltpu.roll(out[n:], V, 1)).reshape(out_ref.shape)


def focal_share(factors, keep, got, b, c, d):
    return pl.pallas_call(
        focal_kernel,
        in_specs=[VMEM] * 6,
        out_specs=VMEM,
        out_shape=jax.ShapeDtypeStruct((U // 2, 8, 128), F32),
        compiler_params=params(4),
        name="focal_share",
    )(factors, keep, got, b, c, d)


def total_kernel(x_ref, out_ref):
    s = jnp.sum(x_ref[...], axis=0)
    for u in range(2):
        for k in range(2):
            for p in range(4):
                at = (k * 4 + p) * V
                row = u * 4 + p
                out_ref[0, u : u + 1, at : at + V] = s[row : row + 1, k * V : (k + 1) * V]


def total(parts):
    return pl.pallas_call(
        total_kernel,
        in_specs=[VMEM],
        out_specs=VMEM,
        out_shape=jax.ShapeDtypeStruct((1, 2, 8 * V), F32),
        compiler_params=params(4),
        name="total",
    )(parts)


def on_device(
    levels, conv_table, conv_bias, mix_weight, mix_bias, decoder, green_rows, green_cols, focal_order
):
    count_px = lax.axis_size("px")
    count_py = lax.axis_size("py")
    rows_t = jnp.swapaxes(green_rows, 2, 3)
    next_x = [(i, (i + 1) % count_px) for i in range(count_px)]
    next_y = [(i, (i + 1) % count_py) for i in range(count_py)]
    order = focal_order.reshape(1, U)

    to_x, to_y, levels = pack(levels, rows_t)
    from_x = lax.ppermute(to_x, "px", next_x)
    from_y = lax.ppermute(to_y, "py", next_y)
    feat, hi, lo, green, conv_w, conv_b, mix_w, mix_b, dec_w = inner(
        levels, conv_table, conv_bias, mix_weight, mix_bias, decoder, green_cols
    )
    from_y, feat = lax.optimization_barrier((from_y, feat))
    feat = middle(levels, from_y, conv_w, conv_b, mix_w, mix_b, feat)
    from_x, feat = lax.optimization_barrier((from_x, feat))
    from_d = lax.ppermute(relay(from_x, green), "py", next_y)
    nf, edge, feat = outer(levels, from_x, conv_w, conv_b, mix_w, mix_b, dec_w, feat)
    send, nf, edge, _ = field(
        levels, from_x, from_y, from_d, conv_w, conv_b, mix_w, mix_b, dec_w, hi, lo, nf, edge, feat
    )

    def swap(x, mask):
        return lax.ppermute(x, "py", [(i, i ^ mask) for i in range(count_py)])

    got = swap(send, 1)
    keep = keep_planes(hi, lo, nf, edge, from_d, 1, 3)
    b, c, d = (swap(keep[i - 1] + got[i], 2 * i) for i in (1, 2, 3))
    keep = keep_planes(hi, lo, nf, edge, from_d, 0, 1)
    factors = row_factors(from_x, rows_t, order)
    share = focal_share(factors, keep, got, b, c, d)
    return total(lax.all_to_all(share, "px", 0, 0))


def solution(mesh):
    return jax.shard_map(
        on_device,
        mesh=mesh,
        in_specs=(
            P("px", "py"),
            P(),
            P(),
            P(),
            P(),
            P(),
            P(None, None, None, "px"),
            P(None, None, None, "py"),
            P(),
        ),
        out_specs=P("py", "px", None),
        check_vma=False,
    )
```

```python
import jax
import jax.numpy as jnp
from jax import lax
from jax.experimental import pallas as pl
from jax.experimental.pallas import tpu as pltpu
from jax.sharding import PartitionSpec as P

HIGH = lax.Precision.HIGHEST
F32 = jnp.float32
BF16 = jnp.bfloat16
NT = (((1,), (1,)), ((), ()))
TN = (((0,), (0,)), ((), ()))

ROWS = 16
COLS = 1024
HID = 64
LEVELS = 16
CH = 8
KS = 5
Z = 8
U = 64
V = 64
HALO = 4
SHIFT = 5
PILLAR_ROWS = ROWS + KS - 1
SLOT = 3 * LEVELS
WINDOW = 4 * SLOT
BLOCK = 4
REL_ORDER = (0, 2, 4, 6, 1, 3, 5, 7)
PART = ROWS * CH // 2
HALF = BLOCK * CH // 2
VMEM = pl.BlockSpec(memory_space=pltpu.VMEM)
HBM = pl.BlockSpec(memory_space=pltpu.HBM)


def params(mib):
    return pltpu.CompilerParams(vmem_limit_bytes=mib << 20)

GELU_A = 0.7978845608028654
GELU_B = GELU_A * 0.044715


def iota(shape, dim):
    return lax.broadcasted_iota(jnp.int32, shape, dim)


def twice_gelu(x):
    return x + x * jnp.tanh(x * (GELU_A + GELU_B * (x * x)))


def split2(x):
    hi = x.astype(BF16)
    return hi, (x - hi.astype(F32)).astype(BF16)


def hbm(x):
    return pltpu.with_memory_space_constraint(x, pltpu.HBM)


def pack_kernel(lev_hbm, rows_hbm, to_x_ref, to_y_ref, out_ref, lev_ref, rows_ref, sems):
    z = lax.axis_index("py")
    copies = [
        pltpu.make_async_copy(lev_hbm, lev_ref, sems.at[0]),
        pltpu.make_async_copy(rows_hbm.at[z], rows_ref, sems.at[1]),
    ]
    for copy in copies:
        copy.start()
    for copy in copies:
        copy.wait()
    lev = lev_ref[...].astype(F32)
    out_ref[...] = lev
    to_x_ref[:, :COLS] = lev[8:, :]
    to_x_ref[:, COLS:] = jnp.concatenate([rows_ref[0, 8:, :], rows_ref[1, 8:, :]], axis=1)
    to_y_ref[...] = lev[:, COLS - 128 :]


def pack(levels, rows_t):
    return pl.pallas_call(
        pack_kernel,
        in_specs=[HBM] * 2,
        out_specs=[VMEM] * 3,
        out_shape=[
            jax.ShapeDtypeStruct((8, COLS + 128), F32),
            jax.ShapeDtypeStruct((ROWS, 128), F32),
            jax.ShapeDtypeStruct((ROWS, COLS), F32),
        ],
        scratch_shapes=[
            pltpu.VMEM((ROWS, COLS), jnp.int32),
            pltpu.VMEM((2, ROWS, U), F32),
            pltpu.SemaphoreType.DMA((2,)),
        ],
        compiler_params=params(4),
        name="pack",
    )(hbm(levels), hbm(rows_t))


def relay_kernel(from_x_ref, green_ref, out_ref):
    out_ref[:8, :] = from_x_ref[:, COLS - 128 : COLS]
    out_ref[8:, :] = green_ref[...]


def relay(from_x, green):
    return pl.pallas_call(
        relay_kernel,
        in_specs=[VMEM] * 2,
        out_specs=VMEM,
        out_shape=jax.ShapeDtypeStruct((8 + Z * HALO, 128), F32),
        compiler_params=params(4),
        name="relay",
    )(from_x, green)


def one_hot(row, level_ids):
    row = jnp.broadcast_to(row, level_ids.shape)
    return jnp.where(row == level_ids, 1.0, 0.0).astype(BF16)


def features(window, conv, conv_bias, mix, mix_bias):
    pre = jnp.dot(conv, window, preferred_element_type=F32) + conv_bias
    return activate(pre, mix, mix_bias)


def activate(pre, mix, mix_bias):
    hidden = twice_gelu(pre).astype(BF16)
    mixed = jnp.dot(mix, hidden, preferred_element_type=F32) + mix_bias
    return twice_gelu(mixed).astype(BF16)


def lanes_from(x, count, offset):
    shape = (x.shape[1], count)
    move = (iota(shape, 1) == iota(shape, 0) + offset).astype(BF16)
    return jnp.dot(x, move, preferred_element_type=F32)


def bias_column(row):
    shape = (2 * HID, HID)
    own = iota(shape, 1) == iota(shape, 0) % HID
    return jnp.sum(jnp.where(own, row, 0.0), axis=1, keepdims=True)


def lay_out_decoder(dec_ref, out_ref):
    n = KS * CH * BLOCK
    row = iota((n, n), 0)
    source = row // 4 % BLOCK * (KS * CH) + row // (4 * BLOCK) * 4 + row % 4
    move = (iota((n, n), 1) == source).astype(BF16)
    dec = dec_ref[...].astype(F32)
    none = jnp.zeros((KS * CH, HID), F32)

    def column(pillar):
        taps = [r - pillar + KS - 1 for r in range(BLOCK)]
        return jnp.concatenate([dec[t] if 0 <= t < KS else none for t in taps], axis=0)

    for i in range(BLOCK):
        pair = jnp.concatenate([column(2 * i), column(2 * i + 1)], axis=1).astype(BF16)
        wide = jnp.dot(move, pair, preferred_element_type=F32)
        out_ref[2, :, 2 * i * HID : (2 * i + 2) * HID] = (0.5 * wide).astype(BF16)


def inner_kernel(
    lev_ref, table_hbm, cb_hbm, mix_hbm, mb_hbm, dec_hbm, cols_hbm,
    feat_ref, hi_ref, lo_ref, green_ref, conv_ref, cb_ref, mixer_ref, mb_ref, dec_ref,
    ext_ref, hot_ref, cols_ref, table_ref, cbr_ref, mix_ref, mbr_ref, raw_ref, sems,
):
    z = lax.axis_index("py")
    small = [
        pltpu.make_async_copy(table_hbm, table_ref, sems.at[Z]),
        pltpu.make_async_copy(cb_hbm, cbr_ref, sems.at[Z + 1]),
        pltpu.make_async_copy(mix_hbm, mix_ref, sems.at[Z + 2]),
        pltpu.make_async_copy(mb_hbm, mbr_ref, sems.at[Z + 3]),
        pltpu.make_async_copy(dec_hbm, raw_ref, sems.at[Z + 4]),
    ]
    copies = [
        pltpu.make_async_copy(cols_hbm.at[z ^ REL_ORDER[g]], cols_ref.at[g], sems.at[g])
        for g in range(Z)
    ]
    for copy in small + copies:
        copy.start()
    wide = COLS - 128
    lev = lev_ref[...]
    for b in range(3):
        ext_ref[b] = pltpu.roll(lev, 3 - b, 1)[:, 128:]
    level_ids = iota((LEVELS, wide), 0).astype(F32)

    def make_hot(q, _):
        for b in range(3):
            hot_ref[pl.ds(q * SLOT + b * LEVELS, LEVELS), :] = one_hot(
                ext_ref[b, pl.ds(q, 1), :], level_ids
            )
        return 0

    lax.fori_loop(0, ROWS - 2, make_hot, 0, unroll=2)
    for copy in small:
        copy.wait()
    first_x = lax.axis_index("px") == 0
    conv_ref[0, :HID, :] = lanes_from(table_ref[...], WINDOW, 0).astype(BF16)
    conv_ref[0, HID:, :] = lanes_from(table_ref[...], WINDOW, SLOT).astype(BF16)
    conv_ref[1] = cut_conv(conv_ref[0], first_x)
    mixer_ref[:HID, :] = (0.5 * lanes_from(mix_ref[...], 2 * HID, 0)).astype(BF16)
    mixer_ref[HID:, :] = (0.5 * lanes_from(mix_ref[...], 2 * HID, HID)).astype(BF16)
    cb_ref[...] = bias_column(cbr_ref[...])
    mb_ref[...] = bias_column(mbr_ref[...])
    lay_out_decoder(raw_ref, dec_ref)
    shape = dec_ref.shape[1:]
    sample = iota(shape, 0) // 4 % BLOCK - SHIFT
    pillar = iota(shape, 1) // HID - SHIFT - 2
    for i in range(2):
        at = i * BLOCK
        apart = (sample + at >= 0) != (pillar + at >= 0)
        dec_ref[i] = dec_ref[2] * jnp.where(first_x & apart, 0.0, 1.0).astype(BF16)
    conv_bias = jnp.broadcast_to(cb_ref[...], (2 * HID, wide))
    mix_bias = jnp.broadcast_to(mb_ref[...], (2 * HID, wide))
    for i in range(ROWS // 2 - 2):
        at = (8 + 2 * i) * HID
        feat_ref[at : at + 2 * HID, 128:] = features(
            hot_ref[i * 2 * SLOT : i * 2 * SLOT + WINDOW, :],
            conv_ref[0], conv_bias, mixer_ref[...], mix_bias,
        )
    for copy in copies:
        copy.wait()

    def split(g, _):
        hi_ref[g], lo_ref[g] = split2(cols_ref[g].reshape(2 * V, COLS))
        return 0

    lax.fori_loop(0, Z, split, 0)
    for g in range(Z):
        edge = cols_ref[g, :, :, COLS - 128 :].reshape(2 * V, 128).T
        green_ref[HALO * g : HALO * (g + 1), :] = edge[128 - HALO :, :]


def inner(levels, table, conv_bias, mix, mix_bias, decoder, green_cols):
    wide = COLS - 128
    return pl.pallas_call(
        inner_kernel,
        in_specs=[VMEM] + [HBM] * 6,
        out_specs=[VMEM] * 9,
        out_shape=[
            jax.ShapeDtypeStruct((PILLAR_ROWS * HID, COLS), BF16),
            jax.ShapeDtypeStruct((Z, 2 * V, COLS), BF16),
            jax.ShapeDtypeStruct((Z, 2 * V, COLS), BF16),
            jax.ShapeDtypeStruct((Z * HALO, 128), F32),
            jax.ShapeDtypeStruct((2, 2 * HID, WINDOW), BF16),
            jax.ShapeDtypeStruct((2 * HID, 1), F32),
            jax.ShapeDtypeStruct((2 * HID, 2 * HID), BF16),
            jax.ShapeDtypeStruct((2 * HID, 1), F32),
            jax.ShapeDtypeStruct((3, KS * CH * BLOCK, 2 * BLOCK * HID), BF16),
        ],
        scratch_shapes=[
            pltpu.VMEM((3, ROWS, wide), F32),
            pltpu.VMEM(((ROWS - 2) * SLOT, wide), BF16),
            pltpu.VMEM((Z, 2, V, COLS), F32),
            pltpu.VMEM(table.shape, BF16),
            pltpu.VMEM((1, HID), F32),
            pltpu.VMEM((HID, HID), BF16),
            pltpu.VMEM((1, HID), F32),
            pltpu.VMEM(decoder.shape, BF16),
            pltpu.SemaphoreType.DMA((Z + 5,)),
        ],
        compiler_params=params(16),
        name="inner",
    )(levels, *map(hbm, (
        table, conv_bias.reshape(1, HID), mix, mix_bias.reshape(1, HID), decoder, green_cols,
    )))


def tile_windows(left, tile, first_y, ext_ref):
    ext = jnp.concatenate([left, tile], axis=1)
    lane = iota(tile.shape, 1)
    for b in range(3):
        window = pltpu.roll(ext, 3 - b, 1)[:, 128:]
        if b != 1:
            window = jnp.where(first_y & (lane == (2 if b == 0 else 1)), -1.0, window)
        ext_ref[b] = window


def near_field(i, dec, feat_ref, nf_ref, edge_ref, first_y):
    lane = iota((1, COLS), 1)
    near = iota((1, 128), 1)
    at = i * BLOCK * HID
    taps = jnp.dot(dec, feat_ref[at : at + 2 * BLOCK * HID, :], preferred_element_type=F32)
    acc = jnp.zeros((2 * HALF, COLS), F32)
    edge = jnp.zeros((2 * HALF, 128), F32)
    for s in range(KS):
        part = taps[2 * HALF * s : 2 * HALF * (s + 1), :]
        k = KS - 1 - s
        ok = (lane < COLS - k) & ((lane + k >= 2) | jnp.logical_not(first_y))
        moved = part if k == 0 else pltpu.roll(part, COLS - k, 1)
        acc = acc + jnp.where(ok, moved, 0.0)
        ok = (near >= s) & (near < HALO) & ((near - s < 2) | jnp.logical_not(first_y))
        part = part[:, :128]
        moved = part if s == 0 else pltpu.roll(part, s, 1)
        edge = edge + jnp.where(ok, moved, 0.0)
    for part, values in enumerate(split2(acc)):
        for k in range(2):
            at = (2 * part + k) * PART + i * HALF
            nf_ref[at : at + HALF, :] = values[k * HALF : (k + 1) * HALF]
    for k in range(2):
        at = k * PART + i * HALF
        edge_ref[at : at + HALF, :] = edge[k * HALF : (k + 1) * HALF]


def middle_kernel(
    lev_ref, from_y_ref, conv_ref, cb_ref, mix_ref, mb_ref, dec_ref, _,
    nf_ref, edge_ref, feat_ref, ext_ref, hot_ref,
):
    first_y = lax.axis_index("py") == 0
    tile_windows(from_y_ref[...], lev_ref[:, :128], first_y, ext_ref)
    level_ids = iota((LEVELS, 128), 0).astype(F32)
    for q in range(ROWS - 2):
        for b in range(3):
            row = one_hot(ext_ref[b, q : q + 1, :], level_ids)
            for t in range(6):
                if 0 <= q - 2 * t < 4:
                    at = (q - 2 * t) * SLOT + b * LEVELS
                    hot_ref[at : at + LEVELS, t * 128 : (t + 1) * 128] = row
    tiles = features(hot_ref[...], conv_ref[0], cb_ref[...], mix_ref[...], mb_ref[...])
    for t in range(6):
        at = (8 + 2 * t) * HID
        feat_ref[at : at + 2 * HID, :128] = tiles[:, t * 128 : (t + 1) * 128]
    for i in (2, 3):
        near_field(i, dec_ref[2], feat_ref, nf_ref, edge_ref, first_y)


def middle(levels, from_y, conv_w, conv_b, mix_w, mix_b, dec_w, feat):
    return pl.pallas_call(
        middle_kernel,
        in_specs=[VMEM] * 8,
        out_specs=[VMEM] * 3,
        out_shape=[
            jax.ShapeDtypeStruct((4 * PART, COLS), BF16),
            jax.ShapeDtypeStruct((2 * PART, 128), F32),
            jax.ShapeDtypeStruct(feat.shape, BF16),
        ],
        input_output_aliases={7: 2},
        scratch_shapes=[pltpu.VMEM((3, ROWS, 128), F32), pltpu.VMEM((WINDOW, 768), BF16)],
        compiler_params=params(8),
        name="middle",
    )(levels, from_y, conv_w, conv_b, mix_w, mix_b, dec_w, feat)


def outer_kernel(
    lev_ref, from_x_ref, conv_ref, cb_ref, mix_ref, mb_ref, _, feat_ref, ext_ref, hot_ref
):
    ext = jnp.concatenate([from_x_ref[:, :COLS], lev_ref[:8, :]], axis=0)
    for b in range(3):
        ext_ref[b] = pltpu.roll(ext, 3 - b, 1)[:, 128:]
    wide = COLS - 128
    level_ids = iota((LEVELS, wide), 0).astype(F32)
    for e in range(10):
        for b in range(3):
            at = e * SLOT + b * LEVELS
            hot_ref[at : at + LEVELS, :] = one_hot(ext_ref[b, e : e + 1, :], level_ids)
    conv_bias = jnp.broadcast_to(cb_ref[...], (2 * HID, wide))
    mix_bias = jnp.broadcast_to(mb_ref[...], (2 * HID, wide))
    for w in range(4):
        at = 2 * w * HID
        feat_ref[at : at + 2 * HID, 128:] = features(
            hot_ref[2 * w * SLOT : 2 * w * SLOT + WINDOW, :],
            conv_ref[w // 3], conv_bias, mix_ref[...], mix_bias,
        )


def cut_conv(conv, first_x):
    slot = iota((2 * HID, WINDOW), 1) // SLOT
    row = iota((2 * HID, WINDOW), 0) // HID
    keep = jnp.where(first_x & (slot + row == 2) & (slot > 0), 0.0, 1.0)
    return conv * keep.astype(BF16)


def outer(levels, from_x, conv_w, conv_b, mix_w, mix_b, feat):
    wide = COLS - 128
    return pl.pallas_call(
        outer_kernel,
        in_specs=[VMEM] * 7,
        out_specs=VMEM,
        out_shape=jax.ShapeDtypeStruct(feat.shape, BF16),
        input_output_aliases={6: 0},
        scratch_shapes=[
            pltpu.VMEM((3, 16, wide), F32),
            pltpu.VMEM((10 * SLOT, wide), BF16),
        ],
        compiler_params=params(8),
        name="outer",
    )(levels, from_x, conv_w, conv_b, mix_w, mix_b, feat)


def column_sum(hi_ref, lo_ref, nf_ref, edge_ref, from_d_ref, out_ref, first, count):
    iy = lax.axis_index("py")
    before = (iy + lax.axis_size("py") - 1) % lax.axis_size("py")
    n = 2 * PART
    sign = jnp.where(iota((1, 128), 1) < V, -1.0, 1.0)
    hi = hi_ref[first : first + count].reshape(2 * V * count, COLS)
    lo = lo_ref[first : first + count].reshape(2 * V * count, COLS)
    both = lax.dot_general(hi, nf_ref[...], NT, preferred_element_type=F32)
    both = both[:, :n] + both[:, n:]
    both = both + lax.dot_general(lo, nf_ref[:n, :], NT, preferred_element_type=F32)
    greens = []
    for g in range(count):
        rel = (iy ^ REL_ORDER[first + g]) ^ before
        at = 8 + HALO * (rel // 2 + 4 * (rel % 2))
        greens.append(from_d_ref[pl.ds(at, HALO), :])
    green = jnp.concatenate(greens, axis=1)
    green = jnp.concatenate([green, jnp.zeros((4, 2 * V * count), F32)], axis=0)
    edge = jnp.dot(edge_ref[:, :8], green, precision=HIGH, preferred_element_type=F32)
    for g in range(count):
        at = 2 * V * g
        out = both[at : at + 2 * V].T + edge[:, at : at + 2 * V]
        out_ref[g] = out[:PART] + sign * pltpu.roll(out[PART:], V, 1)


def field_kernel(
    lev_ref, from_x_ref, from_y_ref, from_d_ref, conv_ref, cb_ref, mix_ref, mb_ref, dec_ref,
    hi_ref, lo_ref, _nf, _edge, _feat, send_ref, nf_ref, edge_ref, feat_ref, ext_ref, hot_ref,
):
    first_y = lax.axis_index("py") == 0
    tile = jnp.concatenate([from_x_ref[:, :128], lev_ref[:8, :128]], axis=0)
    left = jnp.concatenate([from_d_ref[:8, :], from_y_ref[:8, :]], axis=0)
    tile_windows(left, tile, first_y, ext_ref)
    level_ids = iota((LEVELS, 128), 0).astype(F32)
    for e in range(10):
        for b in range(3):
            row = one_hot(ext_ref[b, e : e + 1, :], level_ids)
            for w in range(4):
                if 0 <= e - 2 * w < 4:
                    at = (e - 2 * w) * SLOT + b * LEVELS
                    hot_ref[at : at + LEVELS, w * 128 : (w + 1) * 128] = row
    pre = [
        jnp.dot(conv_ref[0], hot_ref[:, :384], preferred_element_type=F32),
        jnp.dot(conv_ref[1], hot_ref[:, 384:], preferred_element_type=F32),
    ]
    tiles = activate(jnp.concatenate(pre, axis=1) + cb_ref[...], mix_ref[...], mb_ref[...])
    for w in range(4):
        feat_ref[2 * w * HID : (2 * w + 2) * HID, :128] = tiles[:, w * 128 : (w + 1) * 128]

    for i in range(2):
        near_field(i, dec_ref[i], feat_ref, nf_ref, edge_ref, first_y)

    column_sum(hi_ref, lo_ref, nf_ref, edge_ref, from_d_ref, send_ref, 4, 4)


def field(
    levels, from_x, from_y, from_d, conv_w, conv_b, mix_w, mix_b, dec_w, hi, lo, nf, edge, feat
):
    return pl.pallas_call(
        field_kernel,
        in_specs=[VMEM] * 14,
        out_specs=[VMEM] * 4,
        out_shape=[
            jax.ShapeDtypeStruct((4, PART, 128), F32),
            jax.ShapeDtypeStruct((4 * PART, COLS), BF16),
            jax.ShapeDtypeStruct((2 * PART, 128), F32),
            jax.ShapeDtypeStruct(feat.shape, BF16),
        ],
        input_output_aliases={11: 1, 12: 2, 13: 3},
        scratch_shapes=[
            pltpu.VMEM((3, 16, 128), F32),
            pltpu.VMEM((WINDOW, 512), BF16),
        ],
        compiler_params=params(12),
        name="field",
    )(
        levels, from_x, from_y, from_d, conv_w, conv_b, mix_w, mix_b, dec_w, hi, lo, nf, edge, feat
    )


def keep_planes(hi, lo, nf, edge, from_d, first, count):
    def keep_kernel(hi_ref, lo_ref, nf_ref, edge_ref, from_d_ref, out_ref):
        column_sum(hi_ref, lo_ref, nf_ref, edge_ref, from_d_ref, out_ref, first, count)

    return pl.pallas_call(
        keep_kernel,
        in_specs=[VMEM] * 5,
        out_specs=VMEM,
        out_shape=jax.ShapeDtypeStruct((count, PART, 128), F32),
        compiler_params=params(8),
        name="keep_planes",
    )(hi, lo, nf, edge, from_d)


def rows_kernel(from_x_ref, rows_ref, order_ref, out_ref):
    z = lax.axis_index("py")
    green = jnp.concatenate([rows_ref[z, 0], rows_ref[z, 1]], axis=1)
    green = jnp.concatenate([from_x_ref[:, COLS:], green], axis=0)
    n = ROWS + 8
    green = jnp.concatenate(split2(green), axis=0)
    pick = (order_ref[...] == iota((U, U), 0)).astype(BF16)
    copies = (iota((U, U * 4), 1) // 4 == iota((U, U * 4), 0)).astype(BF16)
    pick = jnp.dot(pick, copies, preferred_element_type=F32).astype(BF16)
    row = iota((3 * PART, 2 * n), 0)
    source = (row % PART) // 4 + (8 - SHIFT) + jnp.where(row // PART == 1, n, 0)
    spread = (iota((3 * PART, 2 * n), 1) == source).astype(BF16)
    mask = iota((3 * PART, U * 4), 0) % 4 == iota((3 * PART, U * 4), 1) % 4
    for j in range(2):
        ordered = jnp.dot(green[:, j * U : (j + 1) * U], pick, preferred_element_type=F32)
        wide = jnp.dot(spread, ordered.astype(BF16), preferred_element_type=F32)
        out_ref[j * U * 4 : (j + 1) * U * 4, :] = jnp.where(mask, wide, 0.0).T.astype(BF16)


def row_factors(from_x, rows_t, order):
    return pl.pallas_call(
        rows_kernel,
        in_specs=[VMEM] * 3,
        out_specs=VMEM,
        out_shape=jax.ShapeDtypeStruct((2 * U * 4, 3 * PART), BF16),
        compiler_params=params(4),
        name="row_factors",
    )(from_x, rows_t, order)


def focal_kernel(factor_ref, keep_ref, got_ref, b_ref, c_ref, d_ref, out_ref):
    t = ((keep_ref[0] + got_ref[0]) + b_ref[...]) + (c_ref[...] + d_ref[...])
    hi, lo = split2(t)
    out = jnp.dot(
        factor_ref[...], jnp.concatenate([hi, hi, lo], axis=0), preferred_element_type=F32
    )
    n = U * 4
    sign = jnp.where(iota((1, 128), 1) < V, -1.0, 1.0)
    out_ref[...] = (out[:n] + sign * pltpu.roll(out[n:], V, 1)).reshape(out_ref.shape)


def focal_share(factors, keep, got, b, c, d):
    return pl.pallas_call(
        focal_kernel,
        in_specs=[VMEM] * 6,
        out_specs=VMEM,
        out_shape=jax.ShapeDtypeStruct((U // 2, 8, 128), F32),
        compiler_params=params(4),
        name="focal_share",
    )(factors, keep, got, b, c, d)


def total_kernel(x_ref, out_ref):
    s = jnp.sum(x_ref[...], axis=0)
    for u in range(2):
        for k in range(2):
            for p in range(4):
                at = (k * 4 + p) * V
                row = u * 4 + p
                out_ref[0, u : u + 1, at : at + V] = s[row : row + 1, k * V : (k + 1) * V]


def total(parts):
    return pl.pallas_call(
        total_kernel,
        in_specs=[VMEM],
        out_specs=VMEM,
        out_shape=jax.ShapeDtypeStruct((1, 2, 8 * V), F32),
        compiler_params=params(4),
        name="total",
    )(parts)


def on_device(
    levels, conv_table, conv_bias, mix_weight, mix_bias, decoder, green_rows, green_cols, focal_order
):
    count_px = lax.axis_size("px")
    count_py = lax.axis_size("py")
    rows_t = jnp.swapaxes(green_rows, 2, 3)
    next_x = [(i, (i + 1) % count_px) for i in range(count_px)]
    next_y = [(i, (i + 1) % count_py) for i in range(count_py)]
    order = focal_order.reshape(1, U)

    to_x, to_y, levels = pack(levels, rows_t)
    from_x = lax.ppermute(to_x, "px", next_x)
    from_y = lax.ppermute(to_y, "py", next_y)
    feat, hi, lo, green, conv_w, conv_b, mix_w, mix_b, dec_w = inner(
        levels, conv_table, conv_bias, mix_weight, mix_bias, decoder, green_cols
    )
    from_y, feat = lax.optimization_barrier((from_y, feat))
    nf, edge, feat = middle(levels, from_y, conv_w, conv_b, mix_w, mix_b, dec_w, feat)
    from_x, feat, nf, edge = lax.optimization_barrier((from_x, feat, nf, edge))
    from_d = lax.ppermute(relay(from_x, green), "py", next_y)
    feat = outer(levels, from_x, conv_w, conv_b, mix_w, mix_b, feat)
    send, nf, edge, _ = field(
        levels, from_x, from_y, from_d, conv_w, conv_b, mix_w, mix_b, dec_w, hi, lo, nf, edge, feat
    )

    def swap(x, mask):
        return lax.ppermute(x, "py", [(i, i ^ mask) for i in range(count_py)])

    got = swap(send, 1)
    keep = keep_planes(hi, lo, nf, edge, from_d, 1, 3)
    b, c, d = (swap(keep[i - 1] + got[i], 2 * i) for i in (1, 2, 3))
    keep = keep_planes(hi, lo, nf, edge, from_d, 0, 1)
    factors = row_factors(from_x, rows_t, order)
    share = focal_share(factors, keep, got, b, c, d)
    return total(lax.all_to_all(share, "px", 0, 0))


def solution(mesh):
    return jax.shard_map(
        on_device,
        mesh=mesh,
        in_specs=(
            P("px", "py"),
            P(),
            P(),
            P(),
            P(),
            P(),
            P(None, None, None, "px"),
            P(None, None, None, "py"),
            P(),
        ),
        out_specs=P("py", "px", None),
        check_vma=False,
    )
```

```python
import jax
import jax.numpy as jnp
from jax import lax
from jax.experimental import pallas as pl
from jax.experimental.pallas import tpu as pltpu
from jax.sharding import PartitionSpec as P

HIGH = lax.Precision.HIGHEST
F32 = jnp.float32
BF16 = jnp.bfloat16
NT = (((1,), (1,)), ((), ()))
TN = (((0,), (0,)), ((), ()))

ROWS = 16
COLS = 1024
HID = 64
LEVELS = 16
CH = 8
KS = 5
Z = 8
U = 64
V = 64
HALO = 4
SHIFT = 3
PILLAR_ROWS = ROWS + KS - 1
SLOT = 3 * LEVELS
WINDOW = 4 * SLOT
BLOCK = 4
REL_ORDER = (0, 2, 4, 6, 1, 3, 5, 7)
PART = ROWS * CH // 2
HALF = BLOCK * CH // 2
VMEM = pl.BlockSpec(memory_space=pltpu.VMEM)
HBM = pl.BlockSpec(memory_space=pltpu.HBM)


def params(mib):
    return pltpu.CompilerParams(vmem_limit_bytes=mib << 20)

GELU_A = 0.7978845608028654
GELU_B = GELU_A * 0.044715


def iota(shape, dim):
    return lax.broadcasted_iota(jnp.int32, shape, dim)


def twice_gelu(x):
    return x + x * jnp.tanh(x * (GELU_A + GELU_B * (x * x)))


def split2(x):
    hi = x.astype(BF16)
    return hi, (x - hi.astype(F32)).astype(BF16)


def hbm(x):
    return pltpu.with_memory_space_constraint(x, pltpu.HBM)


def pack_kernel(lev_hbm, rows_hbm, to_x_ref, to_y_ref, out_ref, lev_ref, rows_ref, sems):
    z = lax.axis_index("py")
    copies = [
        pltpu.make_async_copy(lev_hbm, lev_ref, sems.at[0]),
        pltpu.make_async_copy(rows_hbm.at[z], rows_ref, sems.at[1]),
    ]
    for copy in copies:
        copy.start()
    for copy in copies:
        copy.wait()
    lev = lev_ref[...].astype(F32)
    out_ref[...] = lev
    to_x_ref[:, :COLS] = lev[8:, :]
    to_x_ref[:, COLS:] = jnp.concatenate([rows_ref[0, 8:, :], rows_ref[1, 8:, :]], axis=1)
    to_y_ref[...] = lev[:, COLS - 128 :]


def pack(levels, rows_t):
    return pl.pallas_call(
        pack_kernel,
        in_specs=[HBM] * 2,
        out_specs=[VMEM] * 3,
        out_shape=[
            jax.ShapeDtypeStruct((8, COLS + 128), F32),
            jax.ShapeDtypeStruct((ROWS, 128), F32),
            jax.ShapeDtypeStruct((ROWS, COLS), F32),
        ],
        scratch_shapes=[
            pltpu.VMEM((ROWS, COLS), jnp.int32),
            pltpu.VMEM((2, ROWS, U), F32),
            pltpu.SemaphoreType.DMA((2,)),
        ],
        compiler_params=params(4),
        name="pack",
    )(hbm(levels), hbm(rows_t))


def relay_kernel(from_x_ref, green_ref, out_ref):
    out_ref[:8, :] = from_x_ref[:, COLS - 128 : COLS]
    out_ref[8:, :] = green_ref[...]


def relay(from_x, green):
    return pl.pallas_call(
        relay_kernel,
        in_specs=[VMEM] * 2,
        out_specs=VMEM,
        out_shape=jax.ShapeDtypeStruct((8 + Z * HALO, 128), F32),
        compiler_params=params(4),
        name="relay",
    )(from_x, green)


def one_hot(row, level_ids):
    row = jnp.broadcast_to(row, level_ids.shape)
    return jnp.where(row == level_ids, 1.0, 0.0).astype(BF16)


def features(window, conv, conv_bias, mix, mix_bias):
    pre = jnp.dot(conv, window, preferred_element_type=F32) + conv_bias
    return activate(pre, mix, mix_bias)


def activate(pre, mix, mix_bias):
    hidden = twice_gelu(pre).astype(BF16)
    mixed = jnp.dot(mix, hidden, preferred_element_type=F32) + mix_bias
    return twice_gelu(mixed).astype(BF16)


def lanes_from(x, count, offset):
    shape = (x.shape[1], count)
    move = (iota(shape, 1) == iota(shape, 0) + offset).astype(BF16)
    return jnp.dot(x, move, preferred_element_type=F32)


def bias_column(row):
    shape = (2 * HID, HID)
    own = iota(shape, 1) == iota(shape, 0) % HID
    return jnp.sum(jnp.where(own, row, 0.0), axis=1, keepdims=True)


def lay_out_decoder(dec_ref, out_ref):
    n = KS * CH * BLOCK
    row = iota((n, n), 0)
    source = row // 4 % BLOCK * (KS * CH) + row // (4 * BLOCK) * 4 + row % 4
    move = (iota((n, n), 1) == source).astype(BF16)
    dec = dec_ref[...].astype(F32)
    none = jnp.zeros((KS * CH, HID), F32)

    def column(pillar):
        taps = [r - pillar + KS - 1 for r in range(BLOCK)]
        return jnp.concatenate([dec[t] if 0 <= t < KS else none for t in taps], axis=0)

    for i in range(BLOCK):
        pair = jnp.concatenate([column(2 * i), column(2 * i + 1)], axis=1).astype(BF16)
        wide = jnp.dot(move, pair, preferred_element_type=F32)
        out_ref[2, :, 2 * i * HID : (2 * i + 2) * HID] = (0.5 * wide).astype(BF16)


def inner_kernel(
    lev_ref, table_hbm, cb_hbm, mix_hbm, mb_hbm, dec_hbm, cols_hbm,
    feat_ref, hi_ref, lo_ref, green_ref, conv_ref, cb_ref, mixer_ref, mb_ref, dec_ref,
    ext_ref, hot_ref, cols_ref, table_ref, cbr_ref, mix_ref, mbr_ref, raw_ref, sems,
):
    z = lax.axis_index("py")
    small = [
        pltpu.make_async_copy(table_hbm, table_ref, sems.at[Z]),
        pltpu.make_async_copy(cb_hbm, cbr_ref, sems.at[Z + 1]),
        pltpu.make_async_copy(mix_hbm, mix_ref, sems.at[Z + 2]),
        pltpu.make_async_copy(mb_hbm, mbr_ref, sems.at[Z + 3]),
        pltpu.make_async_copy(dec_hbm, raw_ref, sems.at[Z + 4]),
    ]
    copies = [
        pltpu.make_async_copy(cols_hbm.at[z ^ REL_ORDER[g]], cols_ref.at[g], sems.at[g])
        for g in range(Z)
    ]
    for copy in small + copies:
        copy.start()
    wide = COLS - 128
    lev = lev_ref[...]
    for b in range(3):
        ext_ref[b] = pltpu.roll(lev, 3 - b, 1)[:, 128:]
    level_ids = iota((LEVELS, wide), 0).astype(F32)

    def make_hot(q, _):
        for b in range(3):
            hot_ref[pl.ds(q * SLOT + b * LEVELS, LEVELS), :] = one_hot(
                ext_ref[b, pl.ds(q, 1), :], level_ids
            )
        return 0

    lax.fori_loop(0, ROWS, make_hot, 0, unroll=2)
    for copy in small:
        copy.wait()
    first_x = lax.axis_index("px") == 0
    conv_ref[0, :HID, :] = lanes_from(table_ref[...], WINDOW, 0).astype(BF16)
    conv_ref[0, HID:, :] = lanes_from(table_ref[...], WINDOW, SLOT).astype(BF16)
    conv_ref[1] = cut_conv(conv_ref[0], first_x)
    mixer_ref[:HID, :] = (0.5 * lanes_from(mix_ref[...], 2 * HID, 0)).astype(BF16)
    mixer_ref[HID:, :] = (0.5 * lanes_from(mix_ref[...], 2 * HID, HID)).astype(BF16)
    cb_ref[...] = bias_column(cbr_ref[...])
    mb_ref[...] = bias_column(mbr_ref[...])
    lay_out_decoder(raw_ref, dec_ref)
    shape = dec_ref.shape[1:]
    sample = iota(shape, 0) // 4 % BLOCK - SHIFT
    pillar = iota(shape, 1) // HID - SHIFT - 2
    for i in range(2):
        at = i * BLOCK
        apart = (sample + at >= 0) != (pillar + at >= 0)
        dec_ref[i] = dec_ref[2] * jnp.where(first_x & apart, 0.0, 1.0).astype(BF16)
    conv_bias = jnp.broadcast_to(cb_ref[...], (2 * HID, wide))
    mix_bias = jnp.broadcast_to(mb_ref[...], (2 * HID, wide))
    for i in range(ROWS // 2 - 1):
        at = (6 + 2 * i) * HID
        feat_ref[at : at + 2 * HID, 128:] = features(
            hot_ref[i * 2 * SLOT : i * 2 * SLOT + WINDOW, :],
            conv_ref[0], conv_bias, mixer_ref[...], mix_bias,
        )
    for copy in copies:
        copy.wait()

    def split(g, _):
        hi_ref[g], lo_ref[g] = split2(cols_ref[g].reshape(2 * V, COLS))
        return 0

    lax.fori_loop(0, Z, split, 0)
    for g in range(Z):
        edge = cols_ref[g, :, :, COLS - 128 :].reshape(2 * V, 128).T
        green_ref[HALO * g : HALO * (g + 1), :] = edge[128 - HALO :, :]


def inner(levels, table, conv_bias, mix, mix_bias, decoder, green_cols):
    wide = COLS - 128
    return pl.pallas_call(
        inner_kernel,
        in_specs=[VMEM] + [HBM] * 6,
        out_specs=[VMEM] * 9,
        out_shape=[
            jax.ShapeDtypeStruct((PILLAR_ROWS * HID, COLS), BF16),
            jax.ShapeDtypeStruct((Z, 2 * V, COLS), BF16),
            jax.ShapeDtypeStruct((Z, 2 * V, COLS), BF16),
            jax.ShapeDtypeStruct((Z * HALO, 128), F32),
            jax.ShapeDtypeStruct((2, 2 * HID, WINDOW), BF16),
            jax.ShapeDtypeStruct((2 * HID, 1), F32),
            jax.ShapeDtypeStruct((2 * HID, 2 * HID), BF16),
            jax.ShapeDtypeStruct((2 * HID, 1), F32),
            jax.ShapeDtypeStruct((3, KS * CH * BLOCK, 2 * BLOCK * HID), BF16),
        ],
        scratch_shapes=[
            pltpu.VMEM((3, ROWS, wide), F32),
            pltpu.VMEM((ROWS * SLOT, wide), BF16),
            pltpu.VMEM((Z, 2, V, COLS), F32),
            pltpu.VMEM(table.shape, BF16),
            pltpu.VMEM((1, HID), F32),
            pltpu.VMEM((HID, HID), BF16),
            pltpu.VMEM((1, HID), F32),
            pltpu.VMEM(decoder.shape, BF16),
            pltpu.SemaphoreType.DMA((Z + 5,)),
        ],
        compiler_params=params(16),
        name="inner",
    )(levels, *map(hbm, (
        table, conv_bias.reshape(1, HID), mix, mix_bias.reshape(1, HID), decoder, green_cols,
    )))


def tile_windows(left, tile, first_y, ext_ref):
    ext = jnp.concatenate([left, tile], axis=1)
    lane = iota(tile.shape, 1)
    for b in range(3):
        window = pltpu.roll(ext, 3 - b, 1)[:, 128:]
        if b != 1:
            window = jnp.where(first_y & (lane == (2 if b == 0 else 1)), -1.0, window)
        ext_ref[b] = window


def near_field(i, dec, feat_ref, nf_ref, edge_ref, first_y):
    lane = iota((1, COLS), 1)
    near = iota((1, 128), 1)
    at = i * BLOCK * HID
    taps = jnp.dot(dec, feat_ref[at : at + 2 * BLOCK * HID, :], preferred_element_type=F32)
    acc = jnp.zeros((2 * HALF, COLS), F32)
    edge = jnp.zeros((2 * HALF, 128), F32)
    for s in range(KS):
        part = taps[2 * HALF * s : 2 * HALF * (s + 1), :]
        k = KS - 1 - s
        ok = (lane < COLS - k) & ((lane + k >= 2) | jnp.logical_not(first_y))
        moved = part if k == 0 else pltpu.roll(part, COLS - k, 1)
        acc = acc + jnp.where(ok, moved, 0.0)
        ok = (near >= s) & (near < HALO) & ((near - s < 2) | jnp.logical_not(first_y))
        part = part[:, :128]
        moved = part if s == 0 else pltpu.roll(part, s, 1)
        edge = edge + jnp.where(ok, moved, 0.0)
    for part, values in enumerate(split2(acc)):
        for k in range(2):
            at = (2 * part + k) * PART + i * HALF
            nf_ref[at : at + HALF, :] = values[k * HALF : (k + 1) * HALF]
    for k in range(2):
        at = k * PART + i * HALF
        edge_ref[at : at + HALF, :] = edge[k * HALF : (k + 1) * HALF]


def middle_kernel(
    lev_ref, from_y_ref, conv_ref, cb_ref, mix_ref, mb_ref, dec_ref, _,
    nf_ref, edge_ref, feat_ref, ext_ref, hot_ref,
):
    first_y = lax.axis_index("py") == 0
    tile_windows(from_y_ref[...], lev_ref[:, :128], first_y, ext_ref)
    level_ids = iota((LEVELS, 128), 0).astype(F32)
    for q in range(ROWS):
        for b in range(3):
            row = one_hot(ext_ref[b, q : q + 1, :], level_ids)
            for t in range(7):
                if 0 <= q - 2 * t < 4:
                    at = (q - 2 * t) * SLOT + b * LEVELS
                    hot_ref[at : at + LEVELS, t * 128 : (t + 1) * 128] = row
    tiles = features(hot_ref[...], conv_ref[0], cb_ref[...], mix_ref[...], mb_ref[...])
    for t in range(7):
        at = (6 + 2 * t) * HID
        feat_ref[at : at + 2 * HID, :128] = tiles[:, t * 128 : (t + 1) * 128]
    for i in (2, 3):
        near_field(i, dec_ref[2], feat_ref, nf_ref, edge_ref, first_y)


def middle(levels, from_y, conv_w, conv_b, mix_w, mix_b, dec_w, feat):
    return pl.pallas_call(
        middle_kernel,
        in_specs=[VMEM] * 8,
        out_specs=[VMEM] * 3,
        out_shape=[
            jax.ShapeDtypeStruct((4 * PART, COLS), BF16),
            jax.ShapeDtypeStruct((2 * PART, 128), F32),
            jax.ShapeDtypeStruct(feat.shape, BF16),
        ],
        input_output_aliases={7: 2},
        scratch_shapes=[pltpu.VMEM((3, ROWS, 128), F32), pltpu.VMEM((WINDOW, 896), BF16)],
        compiler_params=params(8),
        name="middle",
    )(levels, from_y, conv_w, conv_b, mix_w, mix_b, dec_w, feat)


def outer_kernel(
    lev_ref, from_x_ref, conv_ref, cb_ref, mix_ref, mb_ref, _, feat_ref, ext_ref, hot_ref
):
    ext = jnp.concatenate([from_x_ref[:, :COLS], lev_ref[:8, :]], axis=0)
    for b in range(3):
        ext_ref[b] = pltpu.roll(ext, 3 - b, 1)[:, 128:]
    wide = COLS - 128
    level_ids = iota((LEVELS, wide), 0).astype(F32)
    for e in range(2, 10):
        for b in range(3):
            at = (e - 2) * SLOT + b * LEVELS
            hot_ref[at : at + LEVELS, :] = one_hot(ext_ref[b, e : e + 1, :], level_ids)
    conv_bias = jnp.broadcast_to(cb_ref[...], (2 * HID, wide))
    mix_bias = jnp.broadcast_to(mb_ref[...], (2 * HID, wide))
    for w in range(3):
        at = 2 * w * HID
        feat_ref[at : at + 2 * HID, 128:] = features(
            hot_ref[2 * w * SLOT : 2 * w * SLOT + WINDOW, :],
            conv_ref[w // 2], conv_bias, mix_ref[...], mix_bias,
        )


def cut_conv(conv, first_x):
    slot = iota((2 * HID, WINDOW), 1) // SLOT
    row = iota((2 * HID, WINDOW), 0) // HID
    keep = jnp.where(first_x & (slot + row == 2) & (slot > 0), 0.0, 1.0)
    return conv * keep.astype(BF16)


def outer(levels, from_x, conv_w, conv_b, mix_w, mix_b, feat):
    wide = COLS - 128
    return pl.pallas_call(
        outer_kernel,
        in_specs=[VMEM] * 7,
        out_specs=VMEM,
        out_shape=jax.ShapeDtypeStruct(feat.shape, BF16),
        input_output_aliases={6: 0},
        scratch_shapes=[
            pltpu.VMEM((3, 16, wide), F32),
            pltpu.VMEM((8 * SLOT, wide), BF16),
        ],
        compiler_params=params(8),
        name="outer",
    )(levels, from_x, conv_w, conv_b, mix_w, mix_b, feat)


def column_sum(hi_ref, lo_ref, nf_ref, edge_ref, from_d_ref, out_ref, first, count):
    iy = lax.axis_index("py")
    before = (iy + lax.axis_size("py") - 1) % lax.axis_size("py")
    n = 2 * PART
    sign = jnp.where(iota((1, 128), 1) < V, -1.0, 1.0)
    hi = hi_ref[first : first + count].reshape(2 * V * count, COLS)
    lo = lo_ref[first : first + count].reshape(2 * V * count, COLS)
    both = lax.dot_general(hi, nf_ref[...], NT, preferred_element_type=F32)
    both = both[:, :n] + both[:, n:]
    both = both + lax.dot_general(lo, nf_ref[:n, :], NT, preferred_element_type=F32)
    greens = []
    for g in range(count):
        rel = (iy ^ REL_ORDER[first + g]) ^ before
        at = 8 + HALO * (rel // 2 + 4 * (rel % 2))
        greens.append(from_d_ref[pl.ds(at, HALO), :])
    green = jnp.concatenate(greens, axis=1)
    green = jnp.concatenate([green, jnp.zeros((4, 2 * V * count), F32)], axis=0)
    edge = jnp.dot(edge_ref[:, :8], green, precision=HIGH, preferred_element_type=F32)
    for g in range(count):
        at = 2 * V * g
        out = both[at : at + 2 * V].T + edge[:, at : at + 2 * V]
        out_ref[g] = out[:PART] + sign * pltpu.roll(out[PART:], V, 1)


def field_kernel(
    lev_ref, from_x_ref, from_y_ref, from_d_ref, conv_ref, cb_ref, mix_ref, mb_ref, dec_ref,
    hi_ref, lo_ref, _nf, _edge, _feat, send_ref, nf_ref, edge_ref, feat_ref, ext_ref, hot_ref,
):
    first_y = lax.axis_index("py") == 0
    tile = jnp.concatenate([from_x_ref[:, :128], lev_ref[:8, :128]], axis=0)
    left = jnp.concatenate([from_d_ref[:8, :], from_y_ref[:8, :]], axis=0)
    tile_windows(left, tile, first_y, ext_ref)
    level_ids = iota((LEVELS, 128), 0).astype(F32)
    for e in range(2, 10):
        for b in range(3):
            row = one_hot(ext_ref[b, e : e + 1, :], level_ids)
            for w in range(3):
                if 0 <= e - 2 - 2 * w < 4:
                    at = (e - 2 - 2 * w) * SLOT + b * LEVELS
                    hot_ref[at : at + LEVELS, w * 128 : (w + 1) * 128] = row
    pre = [
        jnp.dot(conv_ref[0], hot_ref[:, :256], preferred_element_type=F32),
        jnp.dot(conv_ref[1], hot_ref[:, 256:], preferred_element_type=F32),
    ]
    tiles = activate(jnp.concatenate(pre, axis=1) + cb_ref[...], mix_ref[...], mb_ref[...])
    for w in range(3):
        feat_ref[2 * w * HID : (2 * w + 2) * HID, :128] = tiles[:, w * 128 : (w + 1) * 128]

    for i in range(2):
        near_field(i, dec_ref[i], feat_ref, nf_ref, edge_ref, first_y)

    column_sum(hi_ref, lo_ref, nf_ref, edge_ref, from_d_ref, send_ref, 4, 4)


def field(
    levels, from_x, from_y, from_d, conv_w, conv_b, mix_w, mix_b, dec_w, hi, lo, nf, edge, feat
):
    return pl.pallas_call(
        field_kernel,
        in_specs=[VMEM] * 14,
        out_specs=[VMEM] * 4,
        out_shape=[
            jax.ShapeDtypeStruct((4, PART, 128), F32),
            jax.ShapeDtypeStruct((4 * PART, COLS), BF16),
            jax.ShapeDtypeStruct((2 * PART, 128), F32),
            jax.ShapeDtypeStruct(feat.shape, BF16),
        ],
        input_output_aliases={11: 1, 12: 2, 13: 3},
        scratch_shapes=[
            pltpu.VMEM((3, 16, 128), F32),
            pltpu.VMEM((WINDOW, 384), BF16),
        ],
        compiler_params=params(12),
        name="field",
    )(
        levels, from_x, from_y, from_d, conv_w, conv_b, mix_w, mix_b, dec_w, hi, lo, nf, edge, feat
    )


def keep_planes(hi, lo, nf, edge, from_d, first, count):
    def keep_kernel(hi_ref, lo_ref, nf_ref, edge_ref, from_d_ref, out_ref):
        column_sum(hi_ref, lo_ref, nf_ref, edge_ref, from_d_ref, out_ref, first, count)

    return pl.pallas_call(
        keep_kernel,
        in_specs=[VMEM] * 5,
        out_specs=VMEM,
        out_shape=jax.ShapeDtypeStruct((count, PART, 128), F32),
        compiler_params=params(8),
        name="keep_planes",
    )(hi, lo, nf, edge, from_d)


def rows_kernel(from_x_ref, rows_ref, order_ref, out_ref):
    z = lax.axis_index("py")
    green = jnp.concatenate([rows_ref[z, 0], rows_ref[z, 1]], axis=1)
    green = jnp.concatenate([from_x_ref[:, COLS:], green], axis=0)
    n = ROWS + 8
    green = jnp.concatenate(split2(green), axis=0)
    pick = (order_ref[...] == iota((U, U), 0)).astype(BF16)
    copies = (iota((U, U * 4), 1) // 4 == iota((U, U * 4), 0)).astype(BF16)
    pick = jnp.dot(pick, copies, preferred_element_type=F32).astype(BF16)
    row = iota((3 * PART, 2 * n), 0)
    source = (row % PART) // 4 + (8 - SHIFT) + jnp.where(row // PART == 1, n, 0)
    spread = (iota((3 * PART, 2 * n), 1) == source).astype(BF16)
    mask = iota((3 * PART, U * 4), 0) % 4 == iota((3 * PART, U * 4), 1) % 4
    for j in range(2):
        ordered = jnp.dot(green[:, j * U : (j + 1) * U], pick, preferred_element_type=F32)
        wide = jnp.dot(spread, ordered.astype(BF16), preferred_element_type=F32)
        out_ref[j * U * 4 : (j + 1) * U * 4, :] = jnp.where(mask, wide, 0.0).T.astype(BF16)


def row_factors(from_x, rows_t, order):
    return pl.pallas_call(
        rows_kernel,
        in_specs=[VMEM] * 3,
        out_specs=VMEM,
        out_shape=jax.ShapeDtypeStruct((2 * U * 4, 3 * PART), BF16),
        compiler_params=params(4),
        name="row_factors",
    )(from_x, rows_t, order)


def focal_kernel(factor_ref, keep_ref, got_ref, b_ref, c_ref, d_ref, out_ref):
    t = ((keep_ref[0] + got_ref[0]) + b_ref[...]) + (c_ref[...] + d_ref[...])
    hi, lo = split2(t)
    out = jnp.dot(
        factor_ref[...], jnp.concatenate([hi, hi, lo], axis=0), preferred_element_type=F32
    )
    n = U * 4
    sign = jnp.where(iota((1, 128), 1) < V, -1.0, 1.0)
    out_ref[...] = (out[:n] + sign * pltpu.roll(out[n:], V, 1)).reshape(out_ref.shape)


def focal_share(factors, keep, got, b, c, d):
    return pl.pallas_call(
        focal_kernel,
        in_specs=[VMEM] * 6,
        out_specs=VMEM,
        out_shape=jax.ShapeDtypeStruct((U // 2, 8, 128), F32),
        compiler_params=params(4),
        name="focal_share",
    )(factors, keep, got, b, c, d)


def total_kernel(x_ref, out_ref):
    s = jnp.sum(x_ref[...], axis=0)
    for u in range(2):
        for k in range(2):
            for p in range(4):
                at = (k * 4 + p) * V
                row = u * 4 + p
                out_ref[0, u : u + 1, at : at + V] = s[row : row + 1, k * V : (k + 1) * V]


def total(parts):
    return pl.pallas_call(
        total_kernel,
        in_specs=[VMEM],
        out_specs=VMEM,
        out_shape=jax.ShapeDtypeStruct((1, 2, 8 * V), F32),
        compiler_params=params(4),
        name="total",
    )(parts)


def on_device(
    levels, conv_table, conv_bias, mix_weight, mix_bias, decoder, green_rows, green_cols, focal_order
):
    count_px = lax.axis_size("px")
    count_py = lax.axis_size("py")
    rows_t = jnp.swapaxes(green_rows, 2, 3)
    next_x = [(i, (i + 1) % count_px) for i in range(count_px)]
    next_y = [(i, (i + 1) % count_py) for i in range(count_py)]
    order = focal_order.reshape(1, U)

    to_x, to_y, levels = pack(levels, rows_t)
    from_x = lax.ppermute(to_x, "px", next_x)
    from_y = lax.ppermute(to_y, "py", next_y)
    feat, hi, lo, green, conv_w, conv_b, mix_w, mix_b, dec_w = inner(
        levels, conv_table, conv_bias, mix_weight, mix_bias, decoder, green_cols
    )
    from_y, feat = lax.optimization_barrier((from_y, feat))
    nf, edge, feat = middle(levels, from_y, conv_w, conv_b, mix_w, mix_b, dec_w, feat)
    from_x, feat, nf, edge = lax.optimization_barrier((from_x, feat, nf, edge))
    from_d = lax.ppermute(relay(from_x, green), "py", next_y)
    feat = outer(levels, from_x, conv_w, conv_b, mix_w, mix_b, feat)
    send, nf, edge, _ = field(
        levels, from_x, from_y, from_d, conv_w, conv_b, mix_w, mix_b, dec_w, hi, lo, nf, edge, feat
    )

    def swap(x, mask):
        return lax.ppermute(x, "py", [(i, i ^ mask) for i in range(count_py)])

    got = swap(send, 1)
    keep = keep_planes(hi, lo, nf, edge, from_d, 1, 3)
    b, c, d = (swap(keep[i - 1] + got[i], 2 * i) for i in (1, 2, 3))
    keep = keep_planes(hi, lo, nf, edge, from_d, 0, 1)
    factors = row_factors(from_x, rows_t, order)
    share = focal_share(factors, keep, got, b, c, d)
    return total(lax.all_to_all(share, "px", 0, 0))


def solution(mesh):
    return jax.shard_map(
        on_device,
        mesh=mesh,
        in_specs=(
            P("px", "py"),
            P(),
            P(),
            P(),
            P(),
            P(),
            P(None, None, None, "px"),
            P(None, None, None, "py"),
            P(),
        ),
        out_specs=P("py", "px", None),
        check_vma=False,
    )
```

```python
import jax
import jax.numpy as jnp
from jax import lax
from jax.experimental import pallas as pl
from jax.experimental.pallas import tpu as pltpu
from jax.sharding import PartitionSpec as P

HIGH = lax.Precision.HIGHEST
F32 = jnp.float32
BF16 = jnp.bfloat16
NT = (((1,), (1,)), ((), ()))
TN = (((0,), (0,)), ((), ()))

ROWS = 16
COLS = 1024
HID = 64
LEVELS = 16
CH = 8
KS = 5
Z = 8
U = 64
V = 64
HALO = 4
SHIFT = 5
PILLAR_ROWS = ROWS + KS - 1
SLOT = 3 * LEVELS
WINDOW = 4 * SLOT
BLOCK = 4
REL_ORDER = (0, 2, 4, 6, 1, 3, 5, 7)
PART = ROWS * CH // 2
HALF = BLOCK * CH // 2
VMEM = pl.BlockSpec(memory_space=pltpu.VMEM)
HBM = pl.BlockSpec(memory_space=pltpu.HBM)


def params(mib):
    return pltpu.CompilerParams(vmem_limit_bytes=mib << 20)

GELU_A = 0.7978845608028654
GELU_B = GELU_A * 0.044715


def iota(shape, dim):
    return lax.broadcasted_iota(jnp.int32, shape, dim)


def twice_gelu(x):
    return x + x * jnp.tanh(x * (GELU_A + GELU_B * (x * x)))


def split2(x):
    hi = x.astype(BF16)
    return hi, (x - hi.astype(F32)).astype(BF16)


def hbm(x):
    return pltpu.with_memory_space_constraint(x, pltpu.HBM)


def pack_kernel(lev_hbm, rows_hbm, to_x_ref, to_y_ref, out_ref, lev_ref, rows_ref, sems):
    z = lax.axis_index("py")
    copies = [
        pltpu.make_async_copy(lev_hbm, lev_ref, sems.at[0]),
        pltpu.make_async_copy(rows_hbm.at[z], rows_ref, sems.at[1]),
    ]
    for copy in copies:
        copy.start()
    for copy in copies:
        copy.wait()
    lev = lev_ref[...].astype(F32)
    out_ref[...] = lev
    to_x_ref[:, :COLS] = lev[8:, :]
    to_x_ref[:, COLS:] = jnp.concatenate([rows_ref[0, 8:, :], rows_ref[1, 8:, :]], axis=1)
    to_y_ref[...] = lev[:, COLS - 128 :]


def pack(levels, rows_t):
    return pl.pallas_call(
        pack_kernel,
        in_specs=[HBM] * 2,
        out_specs=[VMEM] * 3,
        out_shape=[
            jax.ShapeDtypeStruct((8, COLS + 128), F32),
            jax.ShapeDtypeStruct((ROWS, 128), F32),
            jax.ShapeDtypeStruct((ROWS, COLS), F32),
        ],
        scratch_shapes=[
            pltpu.VMEM((ROWS, COLS), jnp.int32),
            pltpu.VMEM((2, ROWS, U), F32),
            pltpu.SemaphoreType.DMA((2,)),
        ],
        compiler_params=params(4),
        name="pack",
    )(hbm(levels), hbm(rows_t))


def relay_kernel(from_x_ref, green_ref, out_ref):
    out_ref[:8, :] = from_x_ref[:, COLS - 128 : COLS]
    out_ref[8:, :] = green_ref[...]


def relay(from_x, green):
    return pl.pallas_call(
        relay_kernel,
        in_specs=[VMEM] * 2,
        out_specs=VMEM,
        out_shape=jax.ShapeDtypeStruct((8 + Z * HALO, 128), F32),
        compiler_params=params(4),
        name="relay",
    )(from_x, green)


def one_hot(row, level_ids):
    row = jnp.broadcast_to(row, level_ids.shape)
    return jnp.where(row == level_ids, 1.0, 0.0).astype(BF16)


def features(window, conv, conv_bias, mix, mix_bias):
    pre = jnp.dot(conv, window, preferred_element_type=F32) + conv_bias
    return activate(pre, mix, mix_bias)


def activate(pre, mix, mix_bias):
    hidden = twice_gelu(pre).astype(BF16)
    mixed = jnp.dot(mix, hidden, preferred_element_type=F32) + mix_bias
    return twice_gelu(mixed).astype(BF16)


def lanes_from(x, count, offset):
    shape = (x.shape[1], count)
    move = (iota(shape, 1) == iota(shape, 0) + offset).astype(BF16)
    return jnp.dot(x, move, preferred_element_type=F32)


def bias_column(row):
    shape = (2 * HID, HID)
    own = iota(shape, 1) == iota(shape, 0) % HID
    return jnp.sum(jnp.where(own, row, 0.0), axis=1, keepdims=True)


def lay_out_decoder(dec_ref, out_ref):
    n = KS * CH * BLOCK
    row = iota((n, n), 0)
    source = row // 4 % BLOCK * (KS * CH) + row // (4 * BLOCK) * 4 + row % 4
    move = (iota((n, n), 1) == source).astype(BF16)
    dec = dec_ref[...].astype(F32)
    none = jnp.zeros((KS * CH, HID), F32)

    def column(pillar):
        taps = [r - pillar + KS - 1 for r in range(BLOCK)]
        return jnp.concatenate([dec[t] if 0 <= t < KS else none for t in taps], axis=0)

    for i in range(BLOCK):
        pair = jnp.concatenate([column(2 * i), column(2 * i + 1)], axis=1).astype(BF16)
        wide = jnp.dot(move, pair, preferred_element_type=F32)
        out_ref[2, :, 2 * i * HID : (2 * i + 2) * HID] = (0.5 * wide).astype(BF16)


def inner_kernel(
    lev_ref, table_hbm, cb_hbm, mix_hbm, mb_hbm, dec_hbm, cols_hbm,
    feat_ref, hi_ref, lo_ref, green_ref, conv_ref, cb_ref, mixer_ref, mb_ref, dec_ref,
    ext_ref, hot_ref, cols_ref, table_ref, cbr_ref, mix_ref, mbr_ref, raw_ref, sems,
):
    z = lax.axis_index("py")
    small = [
        pltpu.make_async_copy(table_hbm, table_ref, sems.at[Z]),
        pltpu.make_async_copy(cb_hbm, cbr_ref, sems.at[Z + 1]),
        pltpu.make_async_copy(mix_hbm, mix_ref, sems.at[Z + 2]),
        pltpu.make_async_copy(mb_hbm, mbr_ref, sems.at[Z + 3]),
        pltpu.make_async_copy(dec_hbm, raw_ref, sems.at[Z + 4]),
    ]
    copies = [
        pltpu.make_async_copy(cols_hbm.at[z ^ REL_ORDER[g]], cols_ref.at[g], sems.at[g])
        for g in range(Z)
    ]
    for copy in small + copies:
        copy.start()
    wide = COLS - 128
    lev = lev_ref[...]
    for b in range(3):
        ext_ref[b] = pltpu.roll(lev, 3 - b, 1)[:, 128:]
    level_ids = iota((LEVELS, wide), 0).astype(F32)

    def make_hot(q, _):
        for b in range(3):
            hot_ref[pl.ds(q * SLOT + b * LEVELS, LEVELS), :] = one_hot(
                ext_ref[b, pl.ds(q, 1), :], level_ids
            )
        return 0

    lax.fori_loop(0, ROWS - 2, make_hot, 0, unroll=2)
    for copy in small:
        copy.wait()
    first_x = lax.axis_index("px") == 0
    conv_ref[0, :HID, :] = lanes_from(table_ref[...], WINDOW, 0).astype(BF16)
    conv_ref[0, HID:, :] = lanes_from(table_ref[...], WINDOW, SLOT).astype(BF16)
    conv_ref[1] = cut_conv(conv_ref[0], first_x)
    mixer_ref[:HID, :] = (0.5 * lanes_from(mix_ref[...], 2 * HID, 0)).astype(BF16)
    mixer_ref[HID:, :] = (0.5 * lanes_from(mix_ref[...], 2 * HID, HID)).astype(BF16)
    cb_ref[...] = bias_column(cbr_ref[...])
    mb_ref[...] = bias_column(mbr_ref[...])
    lay_out_decoder(raw_ref, dec_ref)
    shape = dec_ref.shape[1:]
    sample = iota(shape, 0) // 4 % BLOCK - SHIFT
    pillar = iota(shape, 1) // HID - SHIFT - 2
    for i in range(2):
        at = i * BLOCK
        apart = (sample + at >= 0) != (pillar + at >= 0)
        dec_ref[i] = dec_ref[2] * jnp.where(first_x & apart, 0.0, 1.0).astype(BF16)
    conv_bias = jnp.broadcast_to(cb_ref[...], (2 * HID, wide))
    mix_bias = jnp.broadcast_to(mb_ref[...], (2 * HID, wide))
    for i in range(ROWS // 2 - 2):
        at = (8 + 2 * i) * HID
        feat_ref[at : at + 2 * HID, 128:] = features(
            hot_ref[i * 2 * SLOT : i * 2 * SLOT + WINDOW, :],
            conv_ref[0], conv_bias, mixer_ref[...], mix_bias,
        )
    for copy in copies:
        copy.wait()

    def split(g, _):
        hi_ref[g], lo_ref[g] = split2(cols_ref[g].reshape(2 * V, COLS))
        return 0

    lax.fori_loop(0, Z, split, 0)
    for g in range(Z):
        edge = cols_ref[g, :, :, COLS - 128 :].reshape(2 * V, 128).T
        green_ref[HALO * g : HALO * (g + 1), :] = edge[128 - HALO :, :]


def inner(levels, table, conv_bias, mix, mix_bias, decoder, green_cols):
    wide = COLS - 128
    return pl.pallas_call(
        inner_kernel,
        in_specs=[VMEM] + [HBM] * 6,
        out_specs=[VMEM] * 9,
        out_shape=[
            jax.ShapeDtypeStruct((PILLAR_ROWS * HID, COLS), BF16),
            jax.ShapeDtypeStruct((Z, 2 * V, COLS), BF16),
            jax.ShapeDtypeStruct((Z, 2 * V, COLS), BF16),
            jax.ShapeDtypeStruct((Z * HALO, 128), F32),
            jax.ShapeDtypeStruct((2, 2 * HID, WINDOW), BF16),
            jax.ShapeDtypeStruct((2 * HID, 1), F32),
            jax.ShapeDtypeStruct((2 * HID, 2 * HID), BF16),
            jax.ShapeDtypeStruct((2 * HID, 1), F32),
            jax.ShapeDtypeStruct((3, KS * CH * BLOCK, 2 * BLOCK * HID), BF16),
        ],
        scratch_shapes=[
            pltpu.VMEM((3, ROWS, wide), F32),
            pltpu.VMEM(((ROWS - 2) * SLOT, wide), BF16),
            pltpu.VMEM((Z, 2, V, COLS), F32),
            pltpu.VMEM(table.shape, BF16),
            pltpu.VMEM((1, HID), F32),
            pltpu.VMEM((HID, HID), BF16),
            pltpu.VMEM((1, HID), F32),
            pltpu.VMEM(decoder.shape, BF16),
            pltpu.SemaphoreType.DMA((Z + 5,)),
        ],
        compiler_params=params(16),
        name="inner",
    )(levels, *map(hbm, (
        table, conv_bias.reshape(1, HID), mix, mix_bias.reshape(1, HID), decoder, green_cols,
    )))


def tile_windows(left, tile, first_y, ext_ref):
    ext = jnp.concatenate([left, tile], axis=1)
    lane = iota(tile.shape, 1)
    for b in range(3):
        window = pltpu.roll(ext, 3 - b, 1)[:, 128:]
        if b != 1:
            window = jnp.where(first_y & (lane == (2 if b == 0 else 1)), -1.0, window)
        ext_ref[b] = window


def near_field(i, dec, feat_ref, nf_ref, edge_ref, first_y):
    lane = iota((1, COLS), 1)
    near = iota((1, 128), 1)
    at = i * BLOCK * HID
    taps = jnp.dot(dec, feat_ref[at : at + 2 * BLOCK * HID, :], preferred_element_type=F32)
    acc = jnp.zeros((2 * HALF, COLS), F32)
    edge = jnp.zeros((2 * HALF, 128), F32)
    for s in range(KS):
        part = taps[2 * HALF * s : 2 * HALF * (s + 1), :]
        k = KS - 1 - s
        ok = (lane < COLS - k) & ((lane + k >= 2) | jnp.logical_not(first_y))
        moved = part if k == 0 else pltpu.roll(part, COLS - k, 1)
        acc = acc + jnp.where(ok, moved, 0.0)
        ok = (near >= s) & (near < HALO) & ((near - s < 2) | jnp.logical_not(first_y))
        part = part[:, :128]
        moved = part if s == 0 else pltpu.roll(part, s, 1)
        edge = edge + jnp.where(ok, moved, 0.0)
    for part, values in enumerate(split2(acc)):
        for k in range(2):
            at = (2 * part + k) * PART + i * HALF
            nf_ref[at : at + HALF, :] = values[k * HALF : (k + 1) * HALF]
    for k in range(2):
        at = k * PART + i * HALF
        edge_ref[at : at + HALF, :] = edge[k * HALF : (k + 1) * HALF]


def middle_kernel(
    lev_ref, from_y_ref, conv_ref, cb_ref, mix_ref, mb_ref, dec_ref, _,
    nf_ref, edge_ref, feat_ref, ext_ref, hot_ref,
):
    first_y = lax.axis_index("py") == 0
    tile_windows(from_y_ref[...], lev_ref[:, :128], first_y, ext_ref)
    level_ids = iota((LEVELS, 128), 0).astype(F32)
    for q in range(ROWS - 2):
        for b in range(3):
            row = one_hot(ext_ref[b, q : q + 1, :], level_ids)
            for t in range(6):
                if 0 <= q - 2 * t < 4:
                    at = (q - 2 * t) * SLOT + b * LEVELS
                    hot_ref[at : at + LEVELS, t * 128 : (t + 1) * 128] = row
    tiles = features(hot_ref[...], conv_ref[0], cb_ref[...], mix_ref[...], mb_ref[...])
    for t in range(6):
        at = (8 + 2 * t) * HID
        feat_ref[at : at + 2 * HID, :128] = tiles[:, t * 128 : (t + 1) * 128]
    for i in (2, 3):
        near_field(i, dec_ref[2], feat_ref, nf_ref, edge_ref, first_y)


def middle(levels, from_y, conv_w, conv_b, mix_w, mix_b, dec_w, feat):
    return pl.pallas_call(
        middle_kernel,
        in_specs=[VMEM] * 8,
        out_specs=[VMEM] * 3,
        out_shape=[
            jax.ShapeDtypeStruct((4 * PART, COLS), BF16),
            jax.ShapeDtypeStruct((2 * PART, 128), F32),
            jax.ShapeDtypeStruct(feat.shape, BF16),
        ],
        input_output_aliases={7: 2},
        scratch_shapes=[pltpu.VMEM((3, ROWS, 128), F32), pltpu.VMEM((WINDOW, 768), BF16)],
        compiler_params=params(8),
        name="middle",
    )(levels, from_y, conv_w, conv_b, mix_w, mix_b, dec_w, feat)


def outer_kernel(
    lev_ref, from_x_ref, conv_ref, cb_ref, mix_ref, mb_ref, _, feat_ref, ext_ref, hot_ref
):
    ext = jnp.concatenate([from_x_ref[:, :COLS], lev_ref[:8, :]], axis=0)
    for b in range(3):
        ext_ref[b] = pltpu.roll(ext, 3 - b, 1)[:, 128:]
    wide = COLS - 128
    level_ids = iota((LEVELS, wide), 0).astype(F32)
    for e in range(10):
        for b in range(3):
            at = e * SLOT + b * LEVELS
            hot_ref[at : at + LEVELS, :] = one_hot(ext_ref[b, e : e + 1, :], level_ids)
    conv_bias = jnp.broadcast_to(cb_ref[...], (2 * HID, wide))
    mix_bias = jnp.broadcast_to(mb_ref[...], (2 * HID, wide))
    for w in range(4):
        at = 2 * w * HID
        feat_ref[at : at + 2 * HID, 128:] = features(
            hot_ref[2 * w * SLOT : 2 * w * SLOT + WINDOW, :],
            conv_ref[w // 3], conv_bias, mix_ref[...], mix_bias,
        )


def cut_conv(conv, first_x):
    slot = iota((2 * HID, WINDOW), 1) // SLOT
    row = iota((2 * HID, WINDOW), 0) // HID
    keep = jnp.where(first_x & (slot + row == 2) & (slot > 0), 0.0, 1.0)
    return conv * keep.astype(BF16)


def outer(levels, from_x, conv_w, conv_b, mix_w, mix_b, feat):
    wide = COLS - 128
    return pl.pallas_call(
        outer_kernel,
        in_specs=[VMEM] * 7,
        out_specs=VMEM,
        out_shape=jax.ShapeDtypeStruct(feat.shape, BF16),
        input_output_aliases={6: 0},
        scratch_shapes=[
            pltpu.VMEM((3, 16, wide), F32),
            pltpu.VMEM((10 * SLOT, wide), BF16),
        ],
        compiler_params=params(8),
        name="outer",
    )(levels, from_x, conv_w, conv_b, mix_w, mix_b, feat)


def column_sum(hi_ref, lo_ref, nf_ref, edge_ref, from_d_ref, out_ref, first, count):
    iy = lax.axis_index("py")
    before = (iy + lax.axis_size("py") - 1) % lax.axis_size("py")
    n = 2 * PART
    sign = jnp.where(iota((1, 128), 1) < V, -1.0, 1.0)
    hi = hi_ref[first : first + count].reshape(2 * V * count, COLS)
    lo = lo_ref[first : first + count].reshape(2 * V * count, COLS)
    both = lax.dot_general(hi, nf_ref[...], NT, preferred_element_type=F32)
    both = both[:, :n] + both[:, n:]
    both = both + lax.dot_general(lo, nf_ref[:n, :], NT, preferred_element_type=F32)
    greens = []
    for g in range(count):
        rel = (iy ^ REL_ORDER[first + g]) ^ before
        at = 8 + HALO * (rel // 2 + 4 * (rel % 2))
        greens.append(from_d_ref[pl.ds(at, HALO), :])
    green = jnp.concatenate(greens, axis=1)
    green = jnp.concatenate([green, jnp.zeros((4, 2 * V * count), F32)], axis=0)
    edge = jnp.dot(edge_ref[:, :8], green, precision=HIGH, preferred_element_type=F32)
    for g in range(count):
        at = 2 * V * g
        out = both[at : at + 2 * V].T + edge[:, at : at + 2 * V]
        out_ref[g] = out[:PART] + sign * pltpu.roll(out[PART:], V, 1)


def field_kernel(
    lev_ref, from_x_ref, from_y_ref, from_d_ref, conv_ref, cb_ref, mix_ref, mb_ref, dec_ref,
    hi_ref, lo_ref, _nf, _edge, _feat, send_ref, nf_ref, edge_ref, feat_ref, ext_ref, hot_ref,
):
    first_y = lax.axis_index("py") == 0
    tile = jnp.concatenate([from_x_ref[:, :128], lev_ref[:8, :128]], axis=0)
    left = jnp.concatenate([from_d_ref[:8, :], from_y_ref[:8, :]], axis=0)
    tile_windows(left, tile, first_y, ext_ref)
    level_ids = iota((LEVELS, 128), 0).astype(F32)
    for e in range(10):
        for b in range(3):
            row = one_hot(ext_ref[b, e : e + 1, :], level_ids)
            for w in range(4):
                if 0 <= e - 2 * w < 4:
                    at = (e - 2 * w) * SLOT + b * LEVELS
                    hot_ref[at : at + LEVELS, w * 128 : (w + 1) * 128] = row
    pre = [
        jnp.dot(conv_ref[0], hot_ref[:, :384], preferred_element_type=F32),
        jnp.dot(conv_ref[1], hot_ref[:, 384:], preferred_element_type=F32),
    ]
    tiles = activate(jnp.concatenate(pre, axis=1) + cb_ref[...], mix_ref[...], mb_ref[...])
    for w in range(4):
        feat_ref[2 * w * HID : (2 * w + 2) * HID, :128] = tiles[:, w * 128 : (w + 1) * 128]

    for i in range(2):
        near_field(i, dec_ref[i], feat_ref, nf_ref, edge_ref, first_y)

    column_sum(hi_ref, lo_ref, nf_ref, edge_ref, from_d_ref, send_ref, 4, 4)


def field(
    levels, from_x, from_y, from_d, conv_w, conv_b, mix_w, mix_b, dec_w, hi, lo, nf, edge, feat
):
    return pl.pallas_call(
        field_kernel,
        in_specs=[VMEM] * 14,
        out_specs=[VMEM] * 4,
        out_shape=[
            jax.ShapeDtypeStruct((4, PART, 128), F32),
            jax.ShapeDtypeStruct((4 * PART, COLS), BF16),
            jax.ShapeDtypeStruct((2 * PART, 128), F32),
            jax.ShapeDtypeStruct(feat.shape, BF16),
        ],
        input_output_aliases={11: 1, 12: 2, 13: 3},
        scratch_shapes=[
            pltpu.VMEM((3, 16, 128), F32),
            pltpu.VMEM((WINDOW, 512), BF16),
        ],
        compiler_params=params(12),
        name="field",
    )(
        levels, from_x, from_y, from_d, conv_w, conv_b, mix_w, mix_b, dec_w, hi, lo, nf, edge, feat
    )


def keep_planes(hi, lo, nf, edge, from_d, first, count):
    def keep_kernel(hi_ref, lo_ref, nf_ref, edge_ref, from_d_ref, out_ref):
        column_sum(hi_ref, lo_ref, nf_ref, edge_ref, from_d_ref, out_ref, first, count)

    return pl.pallas_call(
        keep_kernel,
        in_specs=[VMEM] * 5,
        out_specs=VMEM,
        out_shape=jax.ShapeDtypeStruct((count, PART, 128), F32),
        compiler_params=params(8),
        name="keep_planes",
    )(hi, lo, nf, edge, from_d)


def rows_kernel(from_x_ref, rows_ref, order_ref, out_ref):
    z = lax.axis_index("py")
    green = jnp.concatenate([rows_ref[z, 0], rows_ref[z, 1]], axis=1)
    green = jnp.concatenate([from_x_ref[:, COLS:], green], axis=0)
    n = ROWS + 8
    green = jnp.concatenate(split2(green), axis=0)
    pick = (order_ref[...] == iota((U, U), 0)).astype(BF16)
    copies = (iota((U, U * 4), 1) // 4 == iota((U, U * 4), 0)).astype(BF16)
    pick = jnp.dot(pick, copies, preferred_element_type=F32).astype(BF16)
    row = iota((3 * PART, 2 * n), 0)
    source = (row % PART) // 4 + (8 - SHIFT) + jnp.where(row // PART == 1, n, 0)
    spread = (iota((3 * PART, 2 * n), 1) == source).astype(BF16)
    mask = iota((3 * PART, U * 4), 0) % 4 == iota((3 * PART, U * 4), 1) % 4
    for j in range(2):
        ordered = jnp.dot(green[:, j * U : (j + 1) * U], pick, preferred_element_type=F32)
        wide = jnp.dot(spread, ordered.astype(BF16), preferred_element_type=F32)
        out_ref[j * U * 4 : (j + 1) * U * 4, :] = jnp.where(mask, wide, 0.0).T.astype(BF16)


def row_factors(from_x, rows_t, order):
    return pl.pallas_call(
        rows_kernel,
        in_specs=[VMEM] * 3,
        out_specs=VMEM,
        out_shape=jax.ShapeDtypeStruct((2 * U * 4, 3 * PART), BF16),
        compiler_params=params(4),
        name="row_factors",
    )(from_x, rows_t, order)


def focal_kernel(factor_ref, keep_ref, got_ref, b_ref, c_ref, d_ref, out_ref):
    t = ((keep_ref[0] + got_ref[0]) + b_ref[...]) + (c_ref[...] + d_ref[...])
    hi, lo = split2(t)
    out = jnp.dot(
        factor_ref[...], jnp.concatenate([hi, hi, lo], axis=0), preferred_element_type=F32
    )
    n = U * 4
    sign = jnp.where(iota((1, 128), 1) < V, -1.0, 1.0)
    out_ref[...] = (out[:n] + sign * pltpu.roll(out[n:], V, 1)).reshape(out_ref.shape)


def focal_share(factors, keep, got, b, c, d):
    return pl.pallas_call(
        focal_kernel,
        in_specs=[VMEM] * 6,
        out_specs=VMEM,
        out_shape=jax.ShapeDtypeStruct((U // 2, 8, 128), F32),
        compiler_params=params(4),
        name="focal_share",
    )(factors, keep, got, b, c, d)


def total_kernel(x_ref, out_ref):
    s = jnp.sum(x_ref[...], axis=0)
    for u in range(2):
        for k in range(2):
            for p in range(4):
                at = (k * 4 + p) * V
                row = u * 4 + p
                out_ref[0, u : u + 1, at : at + V] = s[row : row + 1, k * V : (k + 1) * V]


def total(parts):
    return pl.pallas_call(
        total_kernel,
        in_specs=[VMEM],
        out_specs=VMEM,
        out_shape=jax.ShapeDtypeStruct((1, 2, 8 * V), F32),
        compiler_params=params(4),
        name="total",
    )(parts)


def on_device(
    levels, conv_table, conv_bias, mix_weight, mix_bias, decoder, green_rows, green_cols, focal_order
):
    count_px = lax.axis_size("px")
    count_py = lax.axis_size("py")
    rows_t = jnp.swapaxes(green_rows, 2, 3)
    next_x = [(i, (i + 1) % count_px) for i in range(count_px)]
    next_y = [(i, (i + 1) % count_py) for i in range(count_py)]
    order = focal_order.reshape(1, U)

    to_x, to_y, levels = pack(levels, rows_t)
    from_x = lax.ppermute(to_x, "px", next_x)
    from_y = lax.ppermute(to_y, "py", next_y)
    feat, hi, lo, green, conv_w, conv_b, mix_w, mix_b, dec_w = inner(
        levels, conv_table, conv_bias, mix_weight, mix_bias, decoder, green_cols
    )
    from_y, feat = lax.optimization_barrier((from_y, feat))
    nf, edge, feat = middle(levels, from_y, conv_w, conv_b, mix_w, mix_b, dec_w, feat)
    from_x, feat, nf, edge = lax.optimization_barrier((from_x, feat, nf, edge))
    from_d = lax.ppermute(relay(from_x, green), "py", next_y)
    feat = outer(levels, from_x, conv_w, conv_b, mix_w, mix_b, feat)
    send, nf, edge, _ = field(
        levels, from_x, from_y, from_d, conv_w, conv_b, mix_w, mix_b, dec_w, hi, lo, nf, edge, feat
    )

    def swap(x, mask):
        return lax.ppermute(x, "py", [(i, i ^ mask) for i in range(count_py)])

    got = swap(send, 1)
    keep = keep_planes(hi, lo, nf, edge, from_d, 1, 3)
    b, c, d = (swap(keep[i - 1] + got[i], 2 * i) for i in (1, 3, 2))
    keep = keep_planes(hi, lo, nf, edge, from_d, 0, 1)
    factors = row_factors(from_x, rows_t, order)
    share = focal_share(factors, keep, got, b, c, d)
    return total(lax.all_to_all(share, "px", 0, 0))


def solution(mesh):
    return jax.shard_map(
        on_device,
        mesh=mesh,
        in_specs=(
            P("px", "py"),
            P(),
            P(),
            P(),
            P(),
            P(),
            P(None, None, None, "px"),
            P(None, None, None, "py"),
            P(),
        ),
        out_specs=P("py", "px", None),
        check_vma=False,
    )
```

```python
import jax
import jax.numpy as jnp
from jax import lax
from jax.experimental import pallas as pl
from jax.experimental.pallas import tpu as pltpu
from jax.sharding import PartitionSpec as P

HIGH = lax.Precision.HIGHEST
F32 = jnp.float32
BF16 = jnp.bfloat16
NT = (((1,), (1,)), ((), ()))
TN = (((0,), (0,)), ((), ()))

ROWS = 16
COLS = 1024
HID = 64
LEVELS = 16
CH = 8
KS = 5
Z = 8
U = 64
V = 64
HALO = 4
SHIFT = 3
UP = 6
PILLAR_ROWS = ROWS + KS - 1
SLOT = 3 * LEVELS
WINDOW = 4 * SLOT
BLOCK = 4
REL_ORDER = (0, 2, 4, 6, 1, 3, 5, 7)
PART = ROWS * CH // 2
HALF = BLOCK * CH // 2
VMEM = pl.BlockSpec(memory_space=pltpu.VMEM)
HBM = pl.BlockSpec(memory_space=pltpu.HBM)


def params(mib):
    return pltpu.CompilerParams(vmem_limit_bytes=mib << 20)

GELU_A = 0.7978845608028654
GELU_B = GELU_A * 0.044715


def iota(shape, dim):
    return lax.broadcasted_iota(jnp.int32, shape, dim)


def twice_gelu(x):
    return x + x * jnp.tanh(x * (GELU_A + GELU_B * (x * x)))


def split2(x):
    hi = x.astype(BF16)
    return hi, (x - hi.astype(F32)).astype(BF16)


def hbm(x):
    return pltpu.with_memory_space_constraint(x, pltpu.HBM)


def pack_kernel(lev_hbm, rows_hbm, to_x_ref, to_y_ref, out_ref, lev_ref, rows_ref, sems):
    z = lax.axis_index("py")
    copies = [
        pltpu.make_async_copy(lev_hbm, lev_ref, sems.at[0]),
        pltpu.make_async_copy(rows_hbm.at[z], rows_ref, sems.at[1]),
    ]
    for copy in copies:
        copy.start()
    for copy in copies:
        copy.wait()
    lev = lev_ref[...].astype(F32)
    out_ref[...] = lev
    for t in range(COLS // 128):
        to_x_ref[UP * t : UP * (t + 1), :] = lev[ROWS - UP :, 128 * t : 128 * (t + 1)]
    to_x_ref[UP * COLS // 128 :, :] = jnp.concatenate([rows_ref[0, 8:, :], rows_ref[1, 8:, :]], axis=1)
    to_y_ref[...] = lev[:, COLS - 128 :]


def pack(levels, rows_t):
    return pl.pallas_call(
        pack_kernel,
        in_specs=[HBM] * 2,
        out_specs=[VMEM] * 3,
        out_shape=[
            jax.ShapeDtypeStruct((UP * COLS // 128 + 8, 128), F32),
            jax.ShapeDtypeStruct((ROWS, 128), F32),
            jax.ShapeDtypeStruct((ROWS, COLS), F32),
        ],
        scratch_shapes=[
            pltpu.VMEM((ROWS, COLS), jnp.int32),
            pltpu.VMEM((2, ROWS, U), F32),
            pltpu.SemaphoreType.DMA((2,)),
        ],
        compiler_params=params(4),
        name="pack",
    )(hbm(levels), hbm(rows_t))


def relay_kernel(from_x_ref, green_ref, out_ref):
    at = UP * (COLS // 128 - 1)
    out_ref[:8, :] = from_x_ref[at : at + 8, :]
    out_ref[8:, :] = green_ref[...]


def relay(from_x, green):
    return pl.pallas_call(
        relay_kernel,
        in_specs=[VMEM] * 2,
        out_specs=VMEM,
        out_shape=jax.ShapeDtypeStruct((8 + Z * HALO, 128), F32),
        compiler_params=params(4),
        name="relay",
    )(from_x, green)


def one_hot(row, level_ids):
    row = jnp.broadcast_to(row, level_ids.shape)
    return jnp.where(row == level_ids, 1.0, 0.0).astype(BF16)


def features(window, conv, conv_bias, mix, mix_bias):
    pre = jnp.dot(conv, window, preferred_element_type=F32) + conv_bias
    return activate(pre, mix, mix_bias)


def activate(pre, mix, mix_bias):
    hidden = twice_gelu(pre).astype(BF16)
    mixed = jnp.dot(mix, hidden, preferred_element_type=F32) + mix_bias
    return twice_gelu(mixed).astype(BF16)


def lanes_from(x, count, offset):
    shape = (x.shape[1], count)
    move = (iota(shape, 1) == iota(shape, 0) + offset).astype(BF16)
    return jnp.dot(x, move, preferred_element_type=F32)


def bias_column(row):
    shape = (2 * HID, HID)
    own = iota(shape, 1) == iota(shape, 0) % HID
    return jnp.sum(jnp.where(own, row, 0.0), axis=1, keepdims=True)


def lay_out_decoder(dec_ref, out_ref):
    n = KS * CH * BLOCK
    row = iota((n, n), 0)
    source = row // 4 % BLOCK * (KS * CH) + row // (4 * BLOCK) * 4 + row % 4
    move = (iota((n, n), 1) == source).astype(BF16)
    dec = dec_ref[...].astype(F32)
    none = jnp.zeros((KS * CH, HID), F32)

    def column(pillar):
        taps = [r - pillar + KS - 1 for r in range(BLOCK)]
        return jnp.concatenate([dec[t] if 0 <= t < KS else none for t in taps], axis=0)

    for i in range(BLOCK):
        pair = jnp.concatenate([column(2 * i), column(2 * i + 1)], axis=1).astype(BF16)
        wide = jnp.dot(move, pair, preferred_element_type=F32)
        out_ref[2, :, 2 * i * HID : (2 * i + 2) * HID] = (0.5 * wide).astype(BF16)


def inner_kernel(
    lev_ref, table_hbm, cb_hbm, mix_hbm, mb_hbm, dec_hbm, cols_hbm,
    feat_ref, hi_ref, lo_ref, green_ref, conv_ref, cb_ref, mixer_ref, mb_ref, dec_ref,
    ext_ref, hot_ref, cols_ref, table_ref, cbr_ref, mix_ref, mbr_ref, raw_ref, sems,
):
    z = lax.axis_index("py")
    small = [
        pltpu.make_async_copy(table_hbm, table_ref, sems.at[Z]),
        pltpu.make_async_copy(cb_hbm, cbr_ref, sems.at[Z + 1]),
        pltpu.make_async_copy(mix_hbm, mix_ref, sems.at[Z + 2]),
        pltpu.make_async_copy(mb_hbm, mbr_ref, sems.at[Z + 3]),
        pltpu.make_async_copy(dec_hbm, raw_ref, sems.at[Z + 4]),
    ]
    copies = [
        pltpu.make_async_copy(cols_hbm.at[z ^ REL_ORDER[g]], cols_ref.at[g], sems.at[g])
        for g in range(Z)
    ]
    for copy in small + copies:
        copy.start()
    wide = COLS - 128
    lev = lev_ref[...]
    for b in range(3):
        ext_ref[b] = pltpu.roll(lev, 3 - b, 1)[:, 128:]
    level_ids = iota((LEVELS, wide), 0).astype(F32)

    def make_hot(q, _):
        for b in range(3):
            hot_ref[pl.ds(q * SLOT + b * LEVELS, LEVELS), :] = one_hot(
                ext_ref[b, pl.ds(q, 1), :], level_ids
            )
        return 0

    lax.fori_loop(0, ROWS, make_hot, 0, unroll=2)
    for copy in small:
        copy.wait()
    first_x = lax.axis_index("px") == 0
    conv_ref[0, :HID, :] = lanes_from(table_ref[...], WINDOW, 0).astype(BF16)
    conv_ref[0, HID:, :] = lanes_from(table_ref[...], WINDOW, SLOT).astype(BF16)
    conv_ref[1] = cut_conv(conv_ref[0], first_x)
    mixer_ref[:HID, :] = (0.5 * lanes_from(mix_ref[...], 2 * HID, 0)).astype(BF16)
    mixer_ref[HID:, :] = (0.5 * lanes_from(mix_ref[...], 2 * HID, HID)).astype(BF16)
    cb_ref[...] = bias_column(cbr_ref[...])
    mb_ref[...] = bias_column(mbr_ref[...])
    lay_out_decoder(raw_ref, dec_ref)
    shape = dec_ref.shape[1:]
    sample = iota(shape, 0) // 4 % BLOCK - SHIFT
    pillar = iota(shape, 1) // HID - SHIFT - 2
    for i in range(2):
        at = i * BLOCK
        apart = (sample + at >= 0) != (pillar + at >= 0)
        dec_ref[i] = dec_ref[2] * jnp.where(first_x & apart, 0.0, 1.0).astype(BF16)
    conv_bias = jnp.broadcast_to(cb_ref[...], (2 * HID, wide))
    mix_bias = jnp.broadcast_to(mb_ref[...], (2 * HID, wide))
    for i in range(ROWS // 2 - 1):
        at = (6 + 2 * i) * HID
        feat_ref[at : at + 2 * HID, 128:] = features(
            hot_ref[i * 2 * SLOT : i * 2 * SLOT + WINDOW, :],
            conv_ref[0], conv_bias, mixer_ref[...], mix_bias,
        )
    for copy in copies:
        copy.wait()

    def split(g, _):
        hi_ref[g], lo_ref[g] = split2(cols_ref[g].reshape(2 * V, COLS))
        return 0

    lax.fori_loop(0, Z, split, 0)
    for g in range(Z):
        edge = cols_ref[g, :, :, COLS - 128 :].reshape(2 * V, 128).T
        green_ref[HALO * g : HALO * (g + 1), :] = edge[128 - HALO :, :]


def inner(levels, table, conv_bias, mix, mix_bias, decoder, green_cols):
    wide = COLS - 128
    return pl.pallas_call(
        inner_kernel,
        in_specs=[VMEM] + [HBM] * 6,
        out_specs=[VMEM] * 9,
        out_shape=[
            jax.ShapeDtypeStruct((PILLAR_ROWS * HID, COLS), BF16),
            jax.ShapeDtypeStruct((Z, 2 * V, COLS), BF16),
            jax.ShapeDtypeStruct((Z, 2 * V, COLS), BF16),
            jax.ShapeDtypeStruct((Z * HALO, 128), F32),
            jax.ShapeDtypeStruct((2, 2 * HID, WINDOW), BF16),
            jax.ShapeDtypeStruct((2 * HID, 1), F32),
            jax.ShapeDtypeStruct((2 * HID, 2 * HID), BF16),
            jax.ShapeDtypeStruct((2 * HID, 1), F32),
            jax.ShapeDtypeStruct((3, KS * CH * BLOCK, 2 * BLOCK * HID), BF16),
        ],
        scratch_shapes=[
            pltpu.VMEM((3, ROWS, wide), F32),
            pltpu.VMEM((ROWS * SLOT, wide), BF16),
            pltpu.VMEM((Z, 2, V, COLS), F32),
            pltpu.VMEM(table.shape, BF16),
            pltpu.VMEM((1, HID), F32),
            pltpu.VMEM((HID, HID), BF16),
            pltpu.VMEM((1, HID), F32),
            pltpu.VMEM(decoder.shape, BF16),
            pltpu.SemaphoreType.DMA((Z + 5,)),
        ],
        compiler_params=params(16),
        name="inner",
    )(levels, *map(hbm, (
        table, conv_bias.reshape(1, HID), mix, mix_bias.reshape(1, HID), decoder, green_cols,
    )))


def tile_windows(left, tile, first_y, ext_ref):
    ext = jnp.concatenate([left, tile], axis=1)
    lane = iota(tile.shape, 1)
    for b in range(3):
        window = pltpu.roll(ext, 3 - b, 1)[:, 128:]
        if b != 1:
            window = jnp.where(first_y & (lane == (2 if b == 0 else 1)), -1.0, window)
        ext_ref[b] = window


def near_field(i, dec, feat_ref, nf_ref, edge_ref, first_y):
    lane = iota((1, COLS), 1)
    near = iota((1, 128), 1)
    at = i * BLOCK * HID
    taps = jnp.dot(dec, feat_ref[at : at + 2 * BLOCK * HID, :], preferred_element_type=F32)
    acc = jnp.zeros((2 * HALF, COLS), F32)
    edge = jnp.zeros((2 * HALF, 128), F32)
    for s in range(KS):
        part = taps[2 * HALF * s : 2 * HALF * (s + 1), :]
        k = KS - 1 - s
        ok = (lane < COLS - k) & ((lane + k >= 2) | jnp.logical_not(first_y))
        moved = part if k == 0 else pltpu.roll(part, COLS - k, 1)
        acc = acc + jnp.where(ok, moved, 0.0)
        ok = (near >= s) & (near < HALO) & ((near - s < 2) | jnp.logical_not(first_y))
        part = part[:, :128]
        moved = part if s == 0 else pltpu.roll(part, s, 1)
        edge = edge + jnp.where(ok, moved, 0.0)
    for part, values in enumerate(split2(acc)):
        for k in range(2):
            at = (2 * part + k) * PART + i * HALF
            nf_ref[at : at + HALF, :] = values[k * HALF : (k + 1) * HALF]
    for k in range(2):
        at = k * PART + i * HALF
        edge_ref[at : at + HALF, :] = edge[k * HALF : (k + 1) * HALF]


def middle_kernel(
    lev_ref, from_y_ref, conv_ref, cb_ref, mix_ref, mb_ref, dec_ref, _,
    nf_ref, edge_ref, feat_ref, ext_ref, hot_ref,
):
    first_y = lax.axis_index("py") == 0
    tile_windows(from_y_ref[...], lev_ref[:, :128], first_y, ext_ref)
    level_ids = iota((LEVELS, 128), 0).astype(F32)
    for q in range(ROWS):
        for b in range(3):
            row = one_hot(ext_ref[b, q : q + 1, :], level_ids)
            for t in range(7):
                if 0 <= q - 2 * t < 4:
                    at = (q - 2 * t) * SLOT + b * LEVELS
                    hot_ref[at : at + LEVELS, t * 128 : (t + 1) * 128] = row
    tiles = features(hot_ref[...], conv_ref[0], cb_ref[...], mix_ref[...], mb_ref[...])
    for t in range(7):
        at = (6 + 2 * t) * HID
        feat_ref[at : at + 2 * HID, :128] = tiles[:, t * 128 : (t + 1) * 128]
    for i in (2, 3):
        near_field(i, dec_ref[2], feat_ref, nf_ref, edge_ref, first_y)


def middle(levels, from_y, conv_w, conv_b, mix_w, mix_b, dec_w, feat):
    return pl.pallas_call(
        middle_kernel,
        in_specs=[VMEM] * 8,
        out_specs=[VMEM] * 3,
        out_shape=[
            jax.ShapeDtypeStruct((4 * PART, COLS), BF16),
            jax.ShapeDtypeStruct((2 * PART, 128), F32),
            jax.ShapeDtypeStruct(feat.shape, BF16),
        ],
        input_output_aliases={7: 2},
        scratch_shapes=[pltpu.VMEM((3, ROWS, 128), F32), pltpu.VMEM((WINDOW, 896), BF16)],
        compiler_params=params(8),
        name="middle",
    )(levels, from_y, conv_w, conv_b, mix_w, mix_b, dec_w, feat)


def outer_kernel(
    lev_ref, from_x_ref, conv_ref, cb_ref, mix_ref, mb_ref, _, feat_ref, ext_ref, hot_ref
):
    tiles = [from_x_ref[UP * t : UP * (t + 1), :] for t in range(COLS // 128)]
    ext = jnp.concatenate([jnp.concatenate(tiles, axis=1), lev_ref[:2, :]], axis=0)
    for b in range(3):
        ext_ref[b] = pltpu.roll(ext, 3 - b, 1)[:, 128:]
    wide = COLS - 128
    level_ids = iota((LEVELS, wide), 0).astype(F32)
    for e in range(8):
        for b in range(3):
            at = e * SLOT + b * LEVELS
            hot_ref[at : at + LEVELS, :] = one_hot(ext_ref[b, e : e + 1, :], level_ids)
    conv_bias = jnp.broadcast_to(cb_ref[...], (2 * HID, wide))
    mix_bias = jnp.broadcast_to(mb_ref[...], (2 * HID, wide))
    for w in range(3):
        at = 2 * w * HID
        feat_ref[at : at + 2 * HID, 128:] = features(
            hot_ref[2 * w * SLOT : 2 * w * SLOT + WINDOW, :],
            conv_ref[w // 2], conv_bias, mix_ref[...], mix_bias,
        )


def cut_conv(conv, first_x):
    slot = iota((2 * HID, WINDOW), 1) // SLOT
    row = iota((2 * HID, WINDOW), 0) // HID
    keep = jnp.where(first_x & (slot + row == 2) & (slot > 0), 0.0, 1.0)
    return conv * keep.astype(BF16)


def outer(levels, from_x, conv_w, conv_b, mix_w, mix_b, feat):
    wide = COLS - 128
    return pl.pallas_call(
        outer_kernel,
        in_specs=[VMEM] * 7,
        out_specs=VMEM,
        out_shape=jax.ShapeDtypeStruct(feat.shape, BF16),
        input_output_aliases={6: 0},
        scratch_shapes=[
            pltpu.VMEM((3, 8, wide), F32),
            pltpu.VMEM((8 * SLOT, wide), BF16),
        ],
        compiler_params=params(8),
        name="outer",
    )(levels, from_x, conv_w, conv_b, mix_w, mix_b, feat)


def column_sum(hi_ref, lo_ref, nf_ref, edge_ref, from_d_ref, out_ref, first, count):
    iy = lax.axis_index("py")
    before = (iy + lax.axis_size("py") - 1) % lax.axis_size("py")
    n = 2 * PART
    sign = jnp.where(iota((1, 128), 1) < V, -1.0, 1.0)
    hi = hi_ref[first : first + count].reshape(2 * V * count, COLS)
    lo = lo_ref[first : first + count].reshape(2 * V * count, COLS)
    both = lax.dot_general(hi, nf_ref[...], NT, preferred_element_type=F32)
    both = both[:, :n] + both[:, n:]
    both = both + lax.dot_general(lo, nf_ref[:n, :], NT, preferred_element_type=F32)
    greens = []
    for g in range(count):
        rel = (iy ^ REL_ORDER[first + g]) ^ before
        at = 8 + HALO * (rel // 2 + 4 * (rel % 2))
        greens.append(from_d_ref[pl.ds(at, HALO), :])
    green = jnp.concatenate(greens, axis=1)
    green = jnp.concatenate([green, jnp.zeros((4, 2 * V * count), F32)], axis=0)
    edge = jnp.dot(edge_ref[:, :8], green, precision=HIGH, preferred_element_type=F32)
    for g in range(count):
        at = 2 * V * g
        out = both[at : at + 2 * V].T + edge[:, at : at + 2 * V]
        out_ref[g] = out[:PART] + sign * pltpu.roll(out[PART:], V, 1)


def field_kernel(
    lev_ref, from_x_ref, from_y_ref, from_d_ref, conv_ref, cb_ref, mix_ref, mb_ref, dec_ref,
    hi_ref, lo_ref, _nf, _edge, _feat, send_ref, nf_ref, edge_ref, feat_ref, ext_ref, hot_ref,
):
    first_y = lax.axis_index("py") == 0
    tile = jnp.concatenate([from_x_ref[:UP, :], lev_ref[:2, :128]], axis=0)
    left = jnp.concatenate([from_d_ref[:UP, :], from_y_ref[:2, :]], axis=0)
    tile_windows(left, tile, first_y, ext_ref)
    level_ids = iota((LEVELS, 128), 0).astype(F32)
    for e in range(8):
        for b in range(3):
            row = one_hot(ext_ref[b, e : e + 1, :], level_ids)
            for w in range(3):
                if 0 <= e - 2 * w < 4:
                    at = (e - 2 * w) * SLOT + b * LEVELS
                    hot_ref[at : at + LEVELS, w * 128 : (w + 1) * 128] = row
    pre = [
        jnp.dot(conv_ref[0], hot_ref[:, :256], preferred_element_type=F32),
        jnp.dot(conv_ref[1], hot_ref[:, 256:], preferred_element_type=F32),
    ]
    tiles = activate(jnp.concatenate(pre, axis=1) + cb_ref[...], mix_ref[...], mb_ref[...])
    for w in range(3):
        feat_ref[2 * w * HID : (2 * w + 2) * HID, :128] = tiles[:, w * 128 : (w + 1) * 128]

    for i in range(2):
        near_field(i, dec_ref[i], feat_ref, nf_ref, edge_ref, first_y)

    column_sum(hi_ref, lo_ref, nf_ref, edge_ref, from_d_ref, send_ref, 4, 4)


def field(
    levels, from_x, from_y, from_d, conv_w, conv_b, mix_w, mix_b, dec_w, hi, lo, nf, edge, feat
):
    return pl.pallas_call(
        field_kernel,
        in_specs=[VMEM] * 14,
        out_specs=[VMEM] * 4,
        out_shape=[
            jax.ShapeDtypeStruct((4, PART, 128), F32),
            jax.ShapeDtypeStruct((4 * PART, COLS), BF16),
            jax.ShapeDtypeStruct((2 * PART, 128), F32),
            jax.ShapeDtypeStruct(feat.shape, BF16),
        ],
        input_output_aliases={11: 1, 12: 2, 13: 3},
        scratch_shapes=[
            pltpu.VMEM((3, 8, 128), F32),
            pltpu.VMEM((WINDOW, 384), BF16),
        ],
        compiler_params=params(12),
        name="field",
    )(
        levels, from_x, from_y, from_d, conv_w, conv_b, mix_w, mix_b, dec_w, hi, lo, nf, edge, feat
    )


def keep_planes(hi, lo, nf, edge, from_d, first, count):
    def keep_kernel(hi_ref, lo_ref, nf_ref, edge_ref, from_d_ref, out_ref):
        column_sum(hi_ref, lo_ref, nf_ref, edge_ref, from_d_ref, out_ref, first, count)

    return pl.pallas_call(
        keep_kernel,
        in_specs=[VMEM] * 5,
        out_specs=VMEM,
        out_shape=jax.ShapeDtypeStruct((count, PART, 128), F32),
        compiler_params=params(8),
        name="keep_planes",
    )(hi, lo, nf, edge, from_d)


def rows_kernel(from_x_ref, rows_ref, order_ref, out_ref):
    z = lax.axis_index("py")
    green = jnp.concatenate([rows_ref[z, 0], rows_ref[z, 1]], axis=1)
    green = jnp.concatenate([from_x_ref[UP * COLS // 128 :, :], green], axis=0)
    n = ROWS + 8
    green = jnp.concatenate(split2(green), axis=0)
    pick = (order_ref[...] == iota((U, U), 0)).astype(BF16)
    copies = (iota((U, U * 4), 1) // 4 == iota((U, U * 4), 0)).astype(BF16)
    pick = jnp.dot(pick, copies, preferred_element_type=F32).astype(BF16)
    row = iota((3 * PART, 2 * n), 0)
    source = (row % PART) // 4 + (8 - SHIFT) + jnp.where(row // PART == 1, n, 0)
    spread = (iota((3 * PART, 2 * n), 1) == source).astype(BF16)
    mask = iota((3 * PART, U * 4), 0) % 4 == iota((3 * PART, U * 4), 1) % 4
    for j in range(2):
        ordered = jnp.dot(green[:, j * U : (j + 1) * U], pick, preferred_element_type=F32)
        wide = jnp.dot(spread, ordered.astype(BF16), preferred_element_type=F32)
        out_ref[j * U * 4 : (j + 1) * U * 4, :] = jnp.where(mask, wide, 0.0).T.astype(BF16)


def row_factors(from_x, rows_t, order):
    return pl.pallas_call(
        rows_kernel,
        in_specs=[VMEM] * 3,
        out_specs=VMEM,
        out_shape=jax.ShapeDtypeStruct((2 * U * 4, 3 * PART), BF16),
        compiler_params=params(4),
        name="row_factors",
    )(from_x, rows_t, order)


def focal_kernel(factor_ref, keep_ref, got_ref, b_ref, c_ref, d_ref, out_ref):
    t = ((keep_ref[0] + got_ref[0]) + b_ref[...]) + (c_ref[...] + d_ref[...])
    hi, lo = split2(t)
    out = jnp.dot(
        factor_ref[...], jnp.concatenate([hi, hi, lo], axis=0), preferred_element_type=F32
    )
    n = U * 4
    sign = jnp.where(iota((1, 128), 1) < V, -1.0, 1.0)
    out_ref[...] = (out[:n] + sign * pltpu.roll(out[n:], V, 1)).reshape(out_ref.shape)


def focal_share(factors, keep, got, b, c, d):
    return pl.pallas_call(
        focal_kernel,
        in_specs=[VMEM] * 6,
        out_specs=VMEM,
        out_shape=jax.ShapeDtypeStruct((U // 2, 8, 128), F32),
        compiler_params=params(4),
        name="focal_share",
    )(factors, keep, got, b, c, d)


def total_kernel(x_ref, out_ref):
    s = jnp.sum(x_ref[...], axis=0)
    for u in range(2):
        for k in range(2):
            for p in range(4):
                at = (k * 4 + p) * V
                row = u * 4 + p
                out_ref[0, u : u + 1, at : at + V] = s[row : row + 1, k * V : (k + 1) * V]


def total(parts):
    return pl.pallas_call(
        total_kernel,
        in_specs=[VMEM],
        out_specs=VMEM,
        out_shape=jax.ShapeDtypeStruct((1, 2, 8 * V), F32),
        compiler_params=params(4),
        name="total",
    )(parts)


def on_device(
    levels, conv_table, conv_bias, mix_weight, mix_bias, decoder, green_rows, green_cols, focal_order
):
    count_px = lax.axis_size("px")
    count_py = lax.axis_size("py")
    rows_t = jnp.swapaxes(green_rows, 2, 3)
    next_x = [(i, (i + 1) % count_px) for i in range(count_px)]
    next_y = [(i, (i + 1) % count_py) for i in range(count_py)]
    order = focal_order.reshape(1, U)

    to_x, to_y, levels = pack(levels, rows_t)
    from_x = lax.ppermute(to_x, "px", next_x)
    from_y = lax.ppermute(to_y, "py", next_y)
    feat, hi, lo, green, conv_w, conv_b, mix_w, mix_b, dec_w = inner(
        levels, conv_table, conv_bias, mix_weight, mix_bias, decoder, green_cols
    )
    from_y, feat = lax.optimization_barrier((from_y, feat))
    nf, edge, feat = middle(levels, from_y, conv_w, conv_b, mix_w, mix_b, dec_w, feat)
    from_x, feat, nf, edge = lax.optimization_barrier((from_x, feat, nf, edge))
    from_d = lax.ppermute(relay(from_x, green), "py", next_y)
    feat = outer(levels, from_x, conv_w, conv_b, mix_w, mix_b, feat)
    send, nf, edge, _ = field(
        levels, from_x, from_y, from_d, conv_w, conv_b, mix_w, mix_b, dec_w, hi, lo, nf, edge, feat
    )

    def swap(x, mask):
        return lax.ppermute(x, "py", [(i, i ^ mask) for i in range(count_py)])

    got = swap(send, 1)
    keep = keep_planes(hi, lo, nf, edge, from_d, 1, 3)
    b, c, d = (swap(keep[i - 1] + got[i], 2 * i) for i in (1, 2, 3))
    keep = keep_planes(hi, lo, nf, edge, from_d, 0, 1)
    factors = row_factors(from_x, rows_t, order)
    share = focal_share(factors, keep, got, b, c, d)
    return total(lax.all_to_all(share, "px", 0, 0))


def solution(mesh):
    return jax.shard_map(
        on_device,
        mesh=mesh,
        in_specs=(
            P("px", "py"),
            P(),
            P(),
            P(),
            P(),
            P(),
            P(None, None, None, "px"),
            P(None, None, None, "py"),
            P(),
        ),
        out_specs=P("py", "px", None),
        check_vma=False,
    )
```
